32 devices in a mesh: lat: 4 (over y, x), lon: 8 (over z, core).
Axes of the slice: x: 2, y: 2, z: 4, core: 2. Of those that a mesh axis runs over, the one named last changes fastest.
Arguments:
- fine_map: bfloat16 [4, 48, 256, 400], P(None, 'lat', 'lon'), may hold values from -26 to 26
- ocean_mask: int32 [4, 48, 256], P(None, 'lat', 'lon'), may hold values from 0 to 1
- out_grad: bfloat16 [4, 48, 256, 400], P(None, 'lat', 'lon'), may hold values from -6 to 6
- encode_depth: bfloat16 [7, 7, 400], replicated, may hold values from -0.875 to 0.875
- encode_gain: bfloat16 [400], replicated, may hold values from 0.099609375 to 1.8984375
- encode_shift: bfloat16 [400], replicated, may hold values from -3 to 3
- encode_up: bfloat16 [400, 1600], P('lat'), may hold values from -0.3125 to 0.3125
- encode_up_bias: bfloat16 [1600], replicated, may hold values from -3 to 3
- encode_down: bfloat16 [1600, 400], P('lat'), may hold values from -0.15625 to 0.15625
- encode_down_bias: bfloat16 [400], replicated, may hold values from -3 to 3
- widen_weight: bfloat16 [400, 800], P('lat'), may hold values from -0.3125 to 0.3125
- widen_bias: bfloat16 [800], replicated, may hold values from -3 to 3
- bottle_depth: bfloat16 [7, 7, 800], replicated, may hold values from -0.875 to 0.875
- bottle_gain: bfloat16 [800], replicated, may hold values from 0.099609375 to 1.8984375
- bottle_shift: bfloat16 [800], replicated, may hold values from -3 to 3
- bottle_up: bfloat16 [800, 3200], P('lat'), may hold values from -0.21875 to 0.21875
- bottle_up_bias: bfloat16 [3200], replicated, may hold values from -3 to 3
- bottle_down: bfloat16 [3200, 800], P('lat'), may hold values from -0.109375 to 0.109375
- bottle_down_bias: bfloat16 [800], replicated, may hold values from -3 to 3
- merge_weight: bfloat16 [1200, 400], P('lat'), may hold values from -0.1875 to 0.1875
- merge_bias: bfloat16 [400], replicated, may hold values from -3 to 3
- decode_depth: bfloat16 [7, 7, 400], replicated, may hold values from -0.875 to 0.875
- decode_gain: bfloat16 [400], replicated, may hold values from 0.099609375 to 1.8984375
- decode_shift: bfloat16 [400], replicated, may hold values from -3 to 3
- decode_up: bfloat16 [400, 1600], P('lat'), may hold values from -0.3125 to 0.3125
- decode_up_bias: bfloat16 [1600], replicated, may hold values from -3 to 3
- decode_down: bfloat16 [1600, 400], P('lat'), may hold values from -0.15625 to 0.15625
- decode_down_bias: bfloat16 [400], replicated, may hold values from -3 to 3
Outputs:
- result: bfloat16 [4, 48, 256, 400], P(None, 'lat', 'lon')
- fine_grad: bfloat16 [4, 48, 256, 400], P(None, 'lat', 'lon')
- encode_depth_grad: float32 [7, 7, 400], replicated
- encode_gain_grad: float32 [400], replicated
- encode_shift_grad: float32 [400], replicated
- encode_up_grad: float32 [400, 1600], replicated
- encode_up_bias_grad: float32 [1600], replicated
- encode_down_grad: float32 [1600, 400], replicated
- encode_down_bias_grad: float32 [400], replicated
- widen_weight_grad: float32 [400, 800], replicated
- widen_bias_grad: float32 [800], replicated
- bottle_depth_grad: float32 [7, 7, 800], replicated
- bottle_gain_grad: float32 [800], replicated
- bottle_shift_grad: float32 [800], replicated
- bottle_up_grad: float32 [800, 3200], replicated
- bottle_up_bias_grad: float32 [3200], replicated
- bottle_down_grad: float32 [3200, 800], replicated
- bottle_down_bias_grad: float32 [800], replicated
- merge_weight_grad: float32 [1200, 400], replicated
- merge_bias_grad: float32 [400], replicated
- decode_depth_grad: float32 [7, 7, 400], replicated
- decode_gain_grad: float32 [400], replicated
- decode_shift_grad: float32 [400], replicated
- decode_up_grad: float32 [400, 1600], replicated
- decode_up_bias_grad: float32 [1600], replicated
- decode_down_grad: float32 [1600, 400], replicated
- decode_down_bias_grad: float32 [400], replicated
The draws below stay inside these ranges and needn't reach their ends.
All inputs are finite; a program needn't handle non-finite values.
Results may differ from the reference program's by a relative error of at most 0.018.
Values may be sent and summed in bfloat16 or wider, within the bound.
No kernel may reach another device: no remote copies, remote signals or barrier semaphores. Data moves between devices by JAX's collectives and lax.ppermute only.
A program may use at most 320 MiB of HBM per device.

```python
import jax
import jax.numpy as jnp
from jax import lax

C = 400
CB = 800
FF = 1600
FB = 3200
B = 4
H = 48
W = 256


def draw_fine_map(key, part):
    noise_key = jax.random.fold_in(key, 11)
    pixel_key = jax.random.fold_in(key, 12)
    channel_key = jax.random.fold_in(key, 13)
    pixel_scale = jnp.exp(jax.random.uniform(pixel_key, (B, H, W, 1), jnp.float32, -1.15, 1.15))
    channel_scale = jnp.exp(jax.random.uniform(channel_key, (1, 1, 1, C), jnp.float32, -0.69, 0.69))
    noise = jnp.clip(jax.random.normal(noise_key, (B, H, W, C), jnp.float32), -4.0, 4.0)
    values = noise * pixel_scale * channel_scale
    return values.astype(jnp.bfloat16)


def draw_ocean_mask(key, part):
    latitude = jnp.arange(H, dtype=jnp.int32)[None, :, None]
    threshold = 250 + 700 * latitude // max(H - 1, 1)
    ticket = jax.random.randint(jax.random.fold_in(key, 21), (B, H, W), 0, 1000, dtype=jnp.int32)
    return (ticket < threshold).astype(jnp.int32)


def levels(key, shape, split, low, largest):
    def one(axis_at, shards_of):
        steps = jax.random.uniform(jax.random.fold_in(jax.random.fold_in(key, 6), axis_at), (shards_of,), jnp.float32, low / len(split), largest / len(split))
        return jnp.repeat(jnp.exp(steps), shape[axis_at] // shards_of).reshape((-1,) + (1,) * (len(shape) - axis_at - 1))

    factor_of = one(*split[0])
    for cut in split[1:]:
        factor_of = factor_of * one(*cut)
    return factor_of


def bell_draw(key, dims, spread, most, split=(), kind=jnp.bfloat16):
    entries = spread * jax.random.normal(key, dims, jnp.float32)
    if split:
        entries = entries * levels(key, dims, split, -0.22, 0.18)
    return jnp.clip(entries, -most, most).astype(kind)


def setup_inputs(seed: int = 0) -> dict:
    key_list = jax.random.split(jax.random.key(seed), 29)
    fine_map = draw_fine_map(jax.random.fold_in(key_list[28], 71), 0)
    ocean_mask = draw_ocean_mask(jax.random.fold_in(key_list[28], 71), 0)
    out_grad = bell_draw(key_list[2], (B, H, W, C), 1.0, 6.0, ((1, 4), (2, 8)))
    encode_depth = bell_draw(key_list[3], (7, 7, C), 49 ** -0.5, 0.875)
    encode_gain = jnp.clip(1.0 + 0.18 * jax.random.normal(key_list[4], (C,), jnp.float32), 0.099609375, 1.8984375).astype(jnp.bfloat16)
    encode_shift = bell_draw(key_list[5], (C,), 0.5, 3.0)
    encode_up = bell_draw(key_list[6], (C, FF), C ** -0.5, 0.3125, ((0, 4),))
    encode_up_bias = bell_draw(key_list[7], (FF,), 0.5, 3.0)
    encode_down = bell_draw(key_list[8], (FF, C), FF ** -0.5, 0.15625, ((0, 4),))
    encode_down_bias = bell_draw(key_list[9], (C,), 0.5, 3.0)
    widen_weight = bell_draw(key_list[10], (C, CB), C ** -0.5, 0.3125, ((0, 4),))
    widen_bias = bell_draw(key_list[11], (CB,), 0.5, 3.0)
    bottle_depth = bell_draw(key_list[12], (7, 7, CB), 49 ** -0.5, 0.875)
    bottle_gain = jnp.clip(1.0 + 0.18 * jax.random.normal(key_list[13], (CB,), jnp.float32), 0.099609375, 1.8984375).astype(jnp.bfloat16)
    bottle_shift = bell_draw(key_list[14], (CB,), 0.5, 3.0)
    bottle_up = bell_draw(key_list[15], (CB, FB), CB ** -0.5, 0.21875, ((0, 4),))
    bottle_up_bias = bell_draw(key_list[16], (FB,), 0.5, 3.0)
    bottle_down = bell_draw(key_list[17], (FB, CB), FB ** -0.5, 0.109375, ((0, 4),))
    bottle_down_bias = bell_draw(key_list[18], (CB,), 0.5, 3.0)
    merge_weight = bell_draw(key_list[19], (CB + C, C), (CB + C) ** -0.5, 0.1875, ((0, 4),))
    merge_bias = bell_draw(key_list[20], (C,), 0.5, 3.0)
    decode_depth = bell_draw(key_list[21], (7, 7, C), 49 ** -0.5, 0.875)
    decode_gain = jnp.clip(1.0 + 0.18 * jax.random.normal(key_list[22], (C,), jnp.float32), 0.099609375, 1.8984375).astype(jnp.bfloat16)
    decode_shift = bell_draw(key_list[23], (C,), 0.5, 3.0)
    decode_up = bell_draw(key_list[24], (C, FF), C ** -0.5, 0.3125, ((0, 4),))
    decode_up_bias = bell_draw(key_list[25], (FF,), 0.5, 3.0)
    decode_down = bell_draw(key_list[26], (FF, C), FF ** -0.5, 0.15625, ((0, 4),))
    decode_down_bias = bell_draw(key_list[27], (C,), 0.5, 3.0)
    return dict(fine_map=fine_map, ocean_mask=ocean_mask, out_grad=out_grad, encode_depth=encode_depth, encode_gain=encode_gain, encode_shift=encode_shift, encode_up=encode_up, encode_up_bias=encode_up_bias, encode_down=encode_down, encode_down_bias=encode_down_bias, widen_weight=widen_weight, widen_bias=widen_bias, bottle_depth=bottle_depth, bottle_gain=bottle_gain, bottle_shift=bottle_shift, bottle_up=bottle_up, bottle_up_bias=bottle_up_bias, bottle_down=bottle_down, bottle_down_bias=bottle_down_bias, merge_weight=merge_weight, merge_bias=merge_bias, decode_depth=decode_depth, decode_gain=decode_gain, decode_shift=decode_shift, decode_up=decode_up, decode_up_bias=decode_up_bias, decode_down=decode_down, decode_down_bias=decode_down_bias)


epsilon = 1e-05
highest = lax.Precision.HIGHEST

@jax.custom_vjp
def low(v):
    return lax.optimization_barrier(v.astype(jnp.bfloat16)).astype(jnp.float32)

@jax.custom_vjp
def low_back(v):
    return v

def low_keep(v):
    return (low(v), None)

def low_pass(kept, grad):
    return (grad,)

def back_keep(v):
    return (v, None)

def back_low(kept, grad):
    return (low(grad),)
low.defvjp(low_keep, low_pass)
low_back.defvjp(back_keep, back_low)

def widened(source):
    wrapped = jnp.concatenate([source[:, :, -3:], source, source[:, :, :3]], axis=2)
    return jnp.pad(wrapped, ((0, 0), (3, 3), (0, 0), (0, 0)))

def depthwise_plain(source, kernel):
    height, breadth = (source.shape[1], source.shape[2])
    extended = widened(source)
    summed = jnp.zeros(source.shape, jnp.float32)
    for across in range(7):
        for column in range(7):
            summed = summed + kernel[across, column] * extended[:, across:across + height, column:column + breadth, :]
    return summed

def block(source, params, sea_mask):
    kernel, scale_gain, norm_shift, up_weight, up_bias, down_weight, down_bias = params
    mixed = low_back(jax.checkpoint(depthwise_plain)(source, kernel))
    ocean_count = jnp.sum(sea_mask)
    mean_value = lax.optimization_barrier(jnp.sum(sea_mask * mixed, axis=(0, 1, 2))) / ocean_count
    variance = lax.optimization_barrier(jnp.sum(sea_mask * mixed * mixed, axis=(0, 1, 2))) / ocean_count - mean_value * mean_value
    normed = (mixed - mean_value) * lax.rsqrt(variance + epsilon) * scale_gain + norm_shift
    hidden = low_back(jnp.einsum('bhwc,cf->bhwf', low(normed), up_weight, precision=highest) + up_bias)
    active = low(jax.nn.gelu(hidden, approximate=False))
    branch = low_back(jnp.einsum('bhwf,fc->bhwc', active, down_weight, precision=highest) + down_bias)
    return sea_mask * (source + branch)

def forward(fine_float, params, sea_fine, sea_coarse):
    encode = params[0:7]
    widen_weight, widen_bias = (params[7], params[8])
    bottle = params[9:16]
    merge_weight, merge_bias = (params[16], params[17])
    decode = params[18:25]
    skip_float = low(block(fine_float, encode, sea_fine))
    date_count, height, breadth, channels = skip_float.shape
    pooled = lax.optimization_barrier(jnp.mean(skip_float.reshape(date_count, height // 2, 2, breadth // 2, 2, channels), axis=(2, 4)))
    coarse_in = low_back(jnp.einsum('bhwc,cd->bhwd', low(pooled), widen_weight, precision=highest) + widen_bias)
    coarse = block(low(coarse_in), bottle, sea_coarse)
    upsampled = jnp.repeat(jnp.repeat(low(coarse), 2, axis=1), 2, axis=2)
    joined = jnp.concatenate([upsampled, skip_float], axis=3)
    merged = low_back(jnp.einsum('bhwc,cd->bhwd', joined, merge_weight, precision=highest) + merge_bias)
    return block(low(merged), decode, sea_fine)

def reference(fine_map, ocean_mask, out_grad, encode_depth, encode_gain, encode_shift, encode_up, encode_up_bias, encode_down, encode_down_bias, widen_weight, widen_bias, bottle_depth, bottle_gain, bottle_shift, bottle_up, bottle_up_bias, bottle_down, bottle_down_bias, merge_weight, merge_bias, decode_depth, decode_gain, decode_shift, decode_up, decode_up_bias, decode_down, decode_down_bias):
    params = tuple((weight.astype(jnp.float32) for weight in (encode_depth, encode_gain, encode_shift, encode_up, encode_up_bias, encode_down, encode_down_bias, widen_weight, widen_bias, bottle_depth, bottle_gain, bottle_shift, bottle_up, bottle_up_bias, bottle_down, bottle_down_bias, merge_weight, merge_bias, decode_depth, decode_gain, decode_shift, decode_up, decode_up_bias, decode_down, decode_down_bias)))
    fine_float = fine_map.astype(jnp.float32)
    sea_fine = ocean_mask.astype(jnp.float32)[..., None]
    date_count, height, breadth = ocean_mask.shape
    sea_coarse = lax.optimization_barrier(jnp.max(sea_fine.reshape(date_count, height // 2, 2, breadth // 2, 2, 1), axis=(2, 4)))
    result, pullback = jax.vjp(lambda source, weights: forward(source, weights, sea_fine, sea_coarse), fine_float, params)
    fine_grad, weight_grads = pullback(out_grad.astype(jnp.float32))
    return (result.astype(jnp.bfloat16), fine_grad.astype(jnp.bfloat16), weight_grads[0], weight_grads[1], weight_grads[2], weight_grads[3], weight_grads[4], weight_grads[5], weight_grads[6], weight_grads[7], weight_grads[8], weight_grads[9], weight_grads[10], weight_grads[11], weight_grads[12], weight_grads[13], weight_grads[14], weight_grads[15], weight_grads[16], weight_grads[17], weight_grads[18], weight_grads[19], weight_grads[20], weight_grads[21], weight_grads[22], weight_grads[23], weight_grads[24])
```

```python
import math

import jax
import jax.numpy as jnp
from jax import lax
from jax.sharding import PartitionSpec as P

epsilon = 1e-05
both = ("lat", "lon")
bf16 = jnp.bfloat16
f32 = jnp.float32


def exchange_pairs(count, group, step):
    return [(i, (i // group) * group + ((i % group) ^ step)) for i in range(count)]


def to_dates(tiles):
    dates, count = tiles.shape[0], lax.axis_size("lat")
    own = lax.axis_index("lat") % dates
    pieces = [lax.dynamic_index_in_dim(tiles, own, 0, keepdims=False)]
    for step in range(1, dates):
        pieces.append(
            lax.ppermute(
                lax.dynamic_index_in_dim(tiles, own ^ step, 0, keepdims=False),
                "lat",
                exchange_pairs(count, dates, step),
            )
        )
    stacked = jnp.stack(pieces)
    ordered = [lax.dynamic_index_in_dim(stacked, own ^ tile, 0, keepdims=False) for tile in range(dates)]
    return jnp.concatenate(ordered, axis=0)


def from_dates(band, dates):
    count = lax.axis_size("lat")
    own = lax.axis_index("lat") % dates
    tiles = band.reshape((dates, band.shape[0] // dates) + band.shape[1:])
    pieces = [lax.dynamic_index_in_dim(tiles, own, 0, keepdims=False)]
    for step in range(1, dates):
        pieces.append(
            lax.ppermute(
                lax.dynamic_index_in_dim(tiles, own ^ step, 0, keepdims=False),
                "lat",
                exchange_pairs(count, dates, step),
            )
        )
    stacked = jnp.stack(pieces)
    return jnp.stack([lax.dynamic_index_in_dim(stacked, own ^ date, 0, keepdims=False) for date in range(dates)])


def widen_map(source, dates):
    count = lax.axis_size("lon")
    forward = [(i, (i + 1) % count) for i in range(count)]
    backward = [(target, origin) for origin, target in forward]
    left = lax.ppermute(source[:, -3:], "lon", forward)
    right = lax.ppermute(source[:, :3], "lon", backward)
    wrapped = jnp.concatenate([left, source, right], axis=1)
    tiles = lax.axis_size("lat")
    if tiles == dates:
        return jnp.pad(wrapped, ((3, 3), (0, 0), (0, 0)))
    down = [(i, i + dates) for i in range(tiles - dates)]
    up = [(target, origin) for origin, target in down]
    above = lax.ppermute(wrapped[-3:], "lat", down)
    below = lax.ppermute(wrapped[:3], "lat", up)
    return jnp.concatenate([above, wrapped, below], axis=0)


def sum_all(local):
    count = lax.axis_size(both)
    copies = jnp.broadcast_to(local[None], (count,) + local.shape)
    return jnp.sum(lax.all_to_all(copies, both, 0, 0, tiled=False), axis=0)


def stencil(extended, kernel, height, breadth):
    taps = kernel.astype(f32)
    summed = jnp.zeros((height, breadth, extended.shape[2]), f32)
    for across in range(7):
        for column in range(7):
            summed = summed + taps[across, column] * extended[
                across : across + height, column : column + breadth, :
            ].astype(f32)
    return summed


def kernel_terms(extended, grad_mixed, height, breadth):
    upstream = grad_mixed.astype(f32)
    terms = []
    for across in range(7):
        for column in range(7):
            window = extended[across : across + height, column : column + breadth, :].astype(f32)
            terms.append(jnp.sum(window * upstream, axis=(0, 1)))
    return jnp.stack(terms)


def cross_rows(former, latter):
    return lax.dot_general(former, latter, (((0,), (0,)), ((), ())), preferred_element_type=f32)


def by_transpose(former, latter):
    return lax.dot_general(former, latter, (((1,), (1,)), ((), ())), preferred_element_type=f32)


def gelu_pair(hidden):
    phi = 0.5 * lax.erfc(hidden * (-math.sqrt(0.5)))
    density = jnp.exp(-0.5 * hidden * hidden) * (1.0 / math.sqrt(2.0 * math.pi))
    return hidden * phi, phi + hidden * density


def block_forward(source, params, sea, dates):
    kernel, gain, shift, up, up_bias, down, down_bias = params
    height, breadth, channels = source.shape
    extended = widen_map(source, dates)
    mixed = stencil(extended, kernel, height, breadth)
    masked = sea * mixed
    local = jnp.stack(
        [jnp.sum(masked, axis=(0, 1)), jnp.sum(masked * mixed, axis=(0, 1)), jnp.full((channels,), jnp.sum(sea))]
    )
    first, square, ocean = sum_all(local)
    ocean = ocean[0]
    mean = first / ocean
    factor = lax.rsqrt(square / ocean - mean * mean + epsilon)
    unit = (mixed - mean) * factor
    normed = (unit * gain.astype(f32) + shift.astype(f32)).astype(bf16).reshape(-1, channels)
    hidden = jnp.dot(normed, up, preferred_element_type=f32) + up_bias.astype(f32)
    active, slope = gelu_pair(hidden)
    active = active.astype(bf16)
    slope = slope.astype(bf16)
    branch = jnp.dot(active, down, preferred_element_type=f32) + down_bias.astype(f32)
    output = sea * (source.astype(f32) + branch.reshape(source.shape))
    return output, (extended, mixed, mean, factor, ocean, normed, slope, active)


def block_backward(grad_output, params, sea, stored, dates):
    kernel, gain, shift, up, up_bias, down, down_bias = params
    extended, mixed, mean, factor, ocean, normed, slope, active = stored
    height, breadth, channels = mixed.shape
    grad_branch = (sea * grad_output).astype(bf16).reshape(-1, channels)
    grad_hidden = (by_transpose(grad_branch, down) * slope.astype(f32)).astype(bf16)
    grad_normed = by_transpose(grad_hidden, up).reshape(mixed.shape)
    unit = (mixed - mean) * factor
    local = jnp.stack([jnp.sum(grad_normed, axis=(0, 1)), jnp.sum(grad_normed * unit, axis=(0, 1))])
    grad_shift, grad_gain = sum_all(local)
    gain = gain.astype(f32)
    grad_mixed = factor * (gain * grad_normed - sea / ocean * (gain * grad_shift + unit * (gain * grad_gain)))
    grad_mixed = grad_mixed.astype(bf16)
    grad_extended = widen_map(grad_mixed, dates)
    grad_source = sea * grad_output + stencil(grad_extended, kernel[::-1, ::-1], height, breadth)
    grad_down = cross_rows(active, grad_branch)
    grad_down_bias = jnp.sum(grad_branch.astype(f32), axis=0)
    grad_up = cross_rows(normed, grad_hidden)
    grad_up_bias = jnp.sum(grad_hidden.astype(f32), axis=0)
    grad_kernel = kernel_terms(extended, grad_mixed, height, breadth)
    return grad_source, (grad_kernel, grad_gain, grad_shift, grad_up, grad_up_bias, grad_down, grad_down_bias)


def shards(
    fine_map,
    ocean_mask,
    out_grad,
    encode_depth,
    encode_gain,
    encode_shift,
    encode_up,
    encode_up_bias,
    encode_down,
    encode_down_bias,
    widen_weight,
    widen_bias,
    bottle_depth,
    bottle_gain,
    bottle_shift,
    bottle_up,
    bottle_up_bias,
    bottle_down,
    bottle_down_bias,
    merge_weight,
    merge_bias,
    decode_depth,
    decode_gain,
    decode_shift,
    decode_up,
    decode_up_bias,
    decode_down,
    decode_down_bias,
):
    (encode_up, encode_down, widen_weight, bottle_up, bottle_down, merge_weight, decode_up, decode_down) = (
        lax.all_gather(weight, "lat", axis=0, tiled=True)
        for weight in (
            encode_up,
            encode_down,
            widen_weight,
            bottle_up,
            bottle_down,
            merge_weight,
            decode_up,
            decode_down,
        )
    )
    dates = fine_map.shape[0]
    fine = to_dates(fine_map)
    sea_fine = to_dates(ocean_mask).astype(f32)[..., None]
    upstream = to_dates(out_grad)
    height, breadth, channels = fine.shape
    half_height, half_breadth = height // 2, breadth // 2
    wide = widen_weight.shape[1]
    sea_coarse = jnp.max(sea_fine.reshape(half_height, 2, half_breadth, 2, 1), axis=(1, 3))
    encode = (encode_depth, encode_gain, encode_shift, encode_up, encode_up_bias, encode_down, encode_down_bias)
    bottle = (bottle_depth, bottle_gain, bottle_shift, bottle_up, bottle_up_bias, bottle_down, bottle_down_bias)
    decode = (decode_depth, decode_gain, decode_shift, decode_up, decode_up_bias, decode_down, decode_down_bias)
    merge_upper = merge_weight[:wide]
    merge_lower = merge_weight[wide:]

    encode_out, encode_stored = block_forward(fine, encode, sea_fine, dates)
    skip_map = encode_out.astype(bf16)
    skip_rows = skip_map.reshape(-1, channels)
    blocks = skip_map.reshape(half_height, 2, half_breadth, 2, channels).astype(f32)
    pooled = (jnp.sum(blocks, axis=(1, 3)) * 0.25).astype(bf16).reshape(-1, channels)
    coarse_in = jnp.dot(pooled, widen_weight, preferred_element_type=f32) + widen_bias.astype(f32)
    coarse_in = coarse_in.astype(bf16).reshape(half_height, half_breadth, wide)
    coarse_out, coarse_stored = block_forward(coarse_in, bottle, sea_coarse, dates)
    coarse_low = coarse_out.astype(bf16).reshape(-1, wide)
    upper = jnp.dot(coarse_low, merge_upper, preferred_element_type=f32)
    upper = upper.reshape(half_height, 1, half_breadth, 1, channels)
    lower = jnp.dot(skip_rows, merge_lower, preferred_element_type=f32)
    lower = lower.reshape(half_height, 2, half_breadth, 2, channels)
    merged = (lower + upper).reshape(height, breadth, channels) + merge_bias.astype(f32)
    decode_out, decode_stored = block_forward(merged.astype(bf16), decode, sea_fine, dates)
    result = from_dates(decode_out.astype(bf16), dates)

    grad_decode_in, decode_grads = block_backward(upstream.astype(f32), decode, sea_fine, decode_stored, dates)
    grad_merged = grad_decode_in.astype(bf16)
    grad_merged_rows = grad_merged.reshape(-1, channels)
    grad_block_sum = jnp.sum(
        grad_merged.astype(f32).reshape(half_height, 2, half_breadth, 2, channels), axis=(1, 3)
    ).reshape(-1, channels)
    grad_merge_bias = jnp.sum(grad_block_sum, axis=0)
    grad_block_low = grad_block_sum.astype(bf16)
    grad_block_rest = (grad_block_sum - grad_block_low.astype(f32)).astype(bf16)
    grad_merge_weight = jnp.concatenate(
        [
            cross_rows(coarse_low, grad_block_low) + cross_rows(coarse_low, grad_block_rest),
            cross_rows(skip_rows, grad_merged_rows),
        ],
        axis=0,
    )
    grad_coarse = (by_transpose(grad_block_low, merge_upper) + by_transpose(grad_block_rest, merge_upper)).reshape(
        half_height, half_breadth, wide
    )
    grad_skip_direct = by_transpose(grad_merged_rows, merge_lower)
    grad_coarse_in, bottle_grads = block_backward(grad_coarse, bottle, sea_coarse, coarse_stored, dates)
    grad_wide = grad_coarse_in.astype(bf16).reshape(-1, wide)
    grad_widen_weight = cross_rows(pooled, grad_wide)
    grad_widen_bias = jnp.sum(grad_wide.astype(f32), axis=0)
    grad_pooled = by_transpose(grad_wide, widen_weight).reshape(half_height, 1, half_breadth, 1, channels) * 0.25
    grad_skip = grad_skip_direct.reshape(half_height, 2, half_breadth, 2, channels) + grad_pooled
    grad_fine, encode_grads = block_backward(
        grad_skip.reshape(height, breadth, channels), encode, sea_fine, encode_stored, dates
    )
    fine_grad = from_dates(grad_fine.astype(bf16), dates)

    def summed(parts):
        return [total.astype(f32) for total in lax.psum([part.astype(bf16) for part in parts], both)]

    decode_up_sum, decode_down_sum, merge_sum = summed([decode_grads[3], decode_grads[5], grad_merge_weight])
    bottle_up_sum, bottle_down_sum, widen_sum = summed([bottle_grads[3], bottle_grads[5], grad_widen_weight])
    encode_up_sum, encode_down_sum = summed([encode_grads[3], encode_grads[5]])
    small_parts = [
        encode_grads[0],
        encode_grads[4],
        encode_grads[6],
        grad_widen_bias,
        bottle_grads[0],
        bottle_grads[4],
        bottle_grads[6],
        grad_merge_bias,
        decode_grads[0],
        decode_grads[4],
        decode_grads[6],
    ]
    small = lax.psum(small_parts, both)
    return (
        result,
        fine_grad,
        small[0].reshape(encode_depth.shape),
        encode_grads[1],
        encode_grads[2],
        encode_up_sum,
        small[1],
        encode_down_sum,
        small[2],
        widen_sum,
        small[3],
        small[4].reshape(bottle_depth.shape),
        bottle_grads[1],
        bottle_grads[2],
        bottle_up_sum,
        small[5],
        bottle_down_sum,
        small[6],
        merge_sum,
        small[7],
        small[8].reshape(decode_depth.shape),
        decode_grads[1],
        decode_grads[2],
        decode_up_sum,
        small[9],
        decode_down_sum,
        small[10],
    )


def solution(mesh):
    whole = P()
    rows = P("lat", None)
    tile = P(None, "lat", "lon", None)
    block = (whole, whole, whole, rows, whole, rows, whole)
    placed = (tile, P(None, "lat", "lon"), tile) + block + (rows, whole) + block + (rows, whole) + block
    return jax.shard_map(
        shards,
        mesh=mesh,
        in_specs=placed,
        out_specs=(tile, tile) + (whole,) * 25,
        check_vma=False,
    )
```

```python
import functools
import math

import jax
import jax.numpy as jnp
from jax import lax
from jax.experimental import pallas as pl
from jax.experimental.pallas import tpu as pltpu
from jax.sharding import PartitionSpec as P

epsilon = 1e-05
both = ("lat", "lon")
bf16 = jnp.bfloat16
f32 = jnp.float32
lanes = 128
strip = 12
room = pltpu.CompilerParams(vmem_limit_bytes=56 << 20)


def exchange_pairs(count, group, step):
    return [(i, (i // group) * group + ((i % group) ^ step)) for i in range(count)]


def to_dates(tiles):
    dates, count = tiles.shape[0], lax.axis_size("lat")
    own = lax.axis_index("lat") % dates
    pieces = [lax.dynamic_index_in_dim(tiles, own, 0, keepdims=False)]
    for step in range(1, dates):
        pieces.append(
            lax.ppermute(
                lax.dynamic_index_in_dim(tiles, own ^ step, 0, keepdims=False),
                "lat",
                exchange_pairs(count, dates, step),
            )
        )
    stacked = jnp.stack(pieces)
    ordered = [lax.dynamic_index_in_dim(stacked, own ^ tile, 0, keepdims=False) for tile in range(dates)]
    return jnp.concatenate(ordered, axis=0)


def from_dates(band, dates):
    count = lax.axis_size("lat")
    own = lax.axis_index("lat") % dates
    tiles = band.reshape((dates, band.shape[0] // dates) + band.shape[1:])
    pieces = [lax.dynamic_index_in_dim(tiles, own, 0, keepdims=False)]
    for step in range(1, dates):
        pieces.append(
            lax.ppermute(
                lax.dynamic_index_in_dim(tiles, own ^ step, 0, keepdims=False),
                "lat",
                exchange_pairs(count, dates, step),
            )
        )
    stacked = jnp.stack(pieces)
    return jnp.stack([lax.dynamic_index_in_dim(stacked, own ^ date, 0, keepdims=False) for date in range(dates)])


def borders(source, dates):
    count = lax.axis_size("lon")
    forward = [(i, (i + 1) % count) for i in range(count)]
    backward = [(target, origin) for origin, target in forward]
    left = lax.ppermute(source[:, -3:], "lon", forward)
    right = lax.ppermute(source[:, :3], "lon", backward)
    tiles = lax.axis_size("lat")
    if tiles == dates:
        return left, right
    down = [(i, i + dates) for i in range(tiles - dates)]
    up = [(target, origin) for origin, target in down]
    last = jnp.concatenate([left[-3:], source[-3:], right[-3:]], axis=1)
    first = jnp.concatenate([left[:3], source[:3], right[:3]], axis=1)
    return left, right, lax.ppermute(last, "lat", down), lax.ppermute(first, "lat", up)


def sum_all(local):
    count = lax.axis_size(both)
    copies = jnp.broadcast_to(local[None], (count,) + local.shape)
    return jnp.sum(lax.all_to_all(copies, both, 0, 0, tiled=False), axis=0)


def fill_extended(wide_ref, centre, edges):
    rows, columns = centre.shape[0], centre.shape[1]
    blank = jnp.zeros((3, columns + 16, lanes), f32)
    wide_ref[0:3] = blank
    wide_ref[rows + 3 :] = blank
    wide_ref[3 : rows + 3, 8 : columns + 8] = centre[...].astype(f32)
    wide_ref[3 : rows + 3, 5:8] = edges[0][...].astype(f32)
    wide_ref[3 : rows + 3, columns + 8 : columns + 11] = edges[1][...].astype(f32)
    if len(edges) > 2:
        wide_ref[0:3, 5 : columns + 11] = edges[2][...].astype(f32)
        wide_ref[rows + 3 :, 5 : columns + 11] = edges[3][...].astype(f32)


def strip_sum(wide_ref, taps, top, start, flipped):
    total = None
    for column in range(7):
        window = wide_ref[pl.ds(top, strip + 6), start + 5 + column : start + 13 + column, :]
        for across in range(7):
            place = 7 * across + column
            tap = taps[pl.ds(48 - place if flipped else place, 8, stride=0), :]
            term = window[across : across + strip] * tap[None]
            total = term if total is None else total + term
    return total


def stencil_forward_kernel(edge_count, source, *refs):
    edges = refs[:edge_count]
    taps, sea, mixed, sums, wide_ref = refs[edge_count:]
    rows, columns = source.shape[0], source.shape[1]
    fill_extended(wide_ref, source, edges)

    def step(index, carry):
        first, square = carry
        top = index * strip
        for start in range(0, columns, 8):
            here = (pl.ds(top, strip), slice(start, start + 8))
            total = strip_sum(wide_ref, taps, top, start, False)
            mixed[here] = total
            masked = total * sea[here]
            first = first + jnp.sum(masked, axis=0)
            square = square + jnp.sum(masked * total, axis=0)
        return first, square

    zero = jnp.zeros((8, lanes), f32)
    first, square = lax.fori_loop(0, rows // strip, step, (zero, zero))
    sums[0:1] = jnp.sum(first, axis=0, keepdims=True)
    sums[1:2] = jnp.sum(square, axis=0, keepdims=True)


def stencil_backward_kernel(edge_count, grad, *refs):
    edges = refs[:edge_count]
    taps, sea, upstream, out, sums, wide_ref = refs[edge_count:]
    rows, columns = grad.shape[0], grad.shape[1]
    fill_extended(wide_ref, grad, edges)

    def step(index, first):
        top = index * strip
        for start in range(0, columns, 8):
            here = (pl.ds(top, strip), slice(start, start + 8))
            total = strip_sum(wide_ref, taps, top, start, True)
            low = (total + upstream[here].astype(f32) * sea[here]).astype(bf16)
            out[here] = low
            first = first + jnp.sum(low.astype(f32), axis=0)
        return first

    first = lax.fori_loop(0, rows // strip, step, jnp.zeros((8, lanes), f32))
    sums[...] = jnp.sum(first, axis=0, keepdims=True)


def kernel_grad_kernel(edge_count, source, *refs):
    edges = refs[:edge_count]
    grad, out, wide_ref, sums_ref = refs[edge_count:]
    rows, columns = source.shape[0], source.shape[1]
    fill_extended(wide_ref, source, edges)
    sums_ref[...] = jnp.zeros_like(sums_ref)

    def step(index, carry):
        top = index * strip
        for start in range(0, columns, 8):
            upstream = grad[pl.ds(top, strip), start : start + 8, :].astype(f32)
            for column in range(7):
                window = wide_ref[pl.ds(top, strip + 6), start + 5 + column : start + 13 + column, :]
                for across in range(7):
                    sums_ref[7 * across + column] += jnp.sum(window[across : across + strip] * upstream, axis=0)
        return carry

    lax.fori_loop(0, rows // strip, step, 0)
    out[...] = jnp.sum(sums_ref[...], axis=1)


def by_channel(array):
    rest = array.shape[:-1]
    return pl.BlockSpec(rest + (lanes,), lambda tile: (0,) * len(rest) + (tile,))


def same_block(array):
    return pl.BlockSpec(array.shape, lambda tile: (0,) * array.ndim)


def wide_scratch(rows, columns):
    return pltpu.VMEM((rows + 6, columns + 16, lanes), f32)


def stencil_forward(source, edges, taps, sea):
    rows, columns, channels = source.shape
    sums = jax.ShapeDtypeStruct((2, channels), f32)
    mixed = jax.ShapeDtypeStruct(source.shape, f32)
    return pl.pallas_call(
        functools.partial(stencil_forward_kernel, len(edges)),
        grid=(pl.cdiv(channels, lanes),),
        in_specs=[by_channel(array) for array in (source, *edges, taps)] + [same_block(sea)],
        out_specs=[by_channel(mixed), by_channel(sums)],
        out_shape=[mixed, sums],
        scratch_shapes=[wide_scratch(rows, columns)],
        compiler_params=room,
        name="stencil_forward",
    )(source, *edges, taps, sea)


def stencil_backward(grad, edges, taps, sea, upstream):
    rows, columns, channels = grad.shape
    out = jax.ShapeDtypeStruct(grad.shape, bf16)
    sums = jax.ShapeDtypeStruct((1, channels), f32)
    return pl.pallas_call(
        functools.partial(stencil_backward_kernel, len(edges)),
        grid=(pl.cdiv(channels, lanes),),
        in_specs=[by_channel(array) for array in (grad, *edges, taps)] + [same_block(sea), by_channel(upstream)],
        out_specs=[by_channel(out), by_channel(sums)],
        out_shape=[out, sums],
        scratch_shapes=[wide_scratch(rows, columns)],
        compiler_params=room,
        name="stencil_backward",
    )(grad, *edges, taps, sea, upstream)


def kernel_grad(source, edges, grad):
    rows, columns, channels = source.shape
    out = jax.ShapeDtypeStruct((49, channels), f32)
    return pl.pallas_call(
        functools.partial(kernel_grad_kernel, len(edges)),
        grid=(pl.cdiv(channels, lanes),),
        in_specs=[by_channel(array) for array in (source, *edges, grad)],
        out_specs=by_channel(out),
        out_shape=out,
        scratch_shapes=[wide_scratch(rows, columns), pltpu.VMEM((49, 8, lanes), f32)],
        compiler_params=room,
        name="kernel_grad",
    )(source, *edges, grad)


def chunks_of(width, size):
    edges = list(range(0, width, size))
    if len(edges) > 1 and width - edges[-1] < size // 2:
        edges.pop()
    return list(zip(edges, edges[1:] + [width]))


def spread(sea, channels):
    return jnp.concatenate([sea] * pl.cdiv(channels, lanes), axis=1)[:, :channels]


def gelu_pair(hidden):
    below = 0.5 + 0.5 * lax.erf(hidden * math.sqrt(0.5))
    density = jnp.exp(-0.5 * hidden * hidden) * (1.0 / math.sqrt(2.0 * math.pi))
    return hidden * below, below + hidden * density


def mlp_forward_kernel(
    size, mixed, source, sea, scales, up, up_bias, down, down_bias, out, active, slope, normed
):
    unit = (mixed[...] - scales[0:1]) * scales[1:2]
    low = (unit * scales[2:3] + scales[3:4]).astype(bf16)
    normed[...] = low
    branch = down_bias[...]
    for a, b in chunks_of(up.shape[1], size):
        hidden = jnp.dot(low, up[:, a:b], preferred_element_type=f32) + up_bias[:, a:b]
        value, rise = gelu_pair(hidden)
        value = value.astype(bf16)
        active[:, a:b] = value
        slope[:, a:b] = rise.astype(bf16)
        branch = branch + jnp.dot(value, down[a:b, :], preferred_element_type=f32)
    mask = spread(sea[...], out.shape[1])
    out[...] = (mask * (source[...].astype(f32) + branch)).astype(bf16)


def mlp_backward_kernel(
    size,
    upstream,
    mixed,
    slope,
    sea,
    scales,
    up,
    down,
    grad_branch,
    grad_hidden,
    grad_normed,
    sums,
    down_sums,
    up_sums,
):
    @pl.when(pl.program_id(0) == 0)
    def _():
        sums[...] = jnp.zeros_like(sums)
        down_sums[...] = jnp.zeros_like(down_sums)
        up_sums[...] = jnp.zeros_like(up_sums)

    mask = spread(sea[...], upstream.shape[1])
    low = (mask * upstream[...].astype(f32)).astype(bf16)
    grad_branch[...] = low
    down_sums[...] += jnp.sum(low.astype(f32), axis=0, keepdims=True)
    normed = None
    for a, b in chunks_of(up.shape[1], size):
        grad_active = lax.dot_general(low, down[a:b, :], (((1,), (1,)), ((), ())), preferred_element_type=f32)
        hidden = (grad_active * slope[:, a:b].astype(f32)).astype(bf16)
        grad_hidden[:, a:b] = hidden
        up_sums[:, a:b] += jnp.sum(hidden.astype(f32), axis=0, keepdims=True)
        part = lax.dot_general(hidden, up[:, a:b], (((1,), (1,)), ((), ())), preferred_element_type=f32)
        normed = part if normed is None else normed + part
    grad_normed[...] = normed
    unit = (mixed[...] - scales[0:1]) * scales[1:2]
    sums[0:1] += jnp.sum(normed, axis=0, keepdims=True)
    sums[1:2] += jnp.sum(normed * unit, axis=0, keepdims=True)


def tall(rows, width):
    return pl.BlockSpec((rows, width), lambda i: (i, 0))


def fixed(array):
    return pl.BlockSpec(array.shape, lambda i: (0, 0), pipeline_mode=pl.Buffered(1))


def mlp_forward(mixed, source, sea, scales, up, up_bias, down, down_bias):
    pixels, channels = mixed.shape
    wide = up.shape[1]
    rows = math.gcd(pixels, 384)
    return pl.pallas_call(
        functools.partial(mlp_forward_kernel, 512),
        grid=(pixels // rows,),
        in_specs=[tall(rows, channels), tall(rows, channels), tall(rows, lanes)]
        + [fixed(array) for array in (scales, up, up_bias, down, down_bias)],
        out_specs=[tall(rows, channels), tall(rows, wide), tall(rows, wide), tall(rows, channels)],
        out_shape=[jax.ShapeDtypeStruct((pixels, width), bf16) for width in (channels, wide, wide, channels)],
        compiler_params=room,
        name="mlp_forward",
    )(mixed, source, sea, scales, up, up_bias, down, down_bias)


def mlp_backward(upstream, mixed, slope, sea, scales, up, down):
    pixels, channels = mixed.shape
    wide = up.shape[1]
    rows = math.gcd(pixels, 384)
    sums = [jax.ShapeDtypeStruct(shape, f32) for shape in ((2, channels), (1, channels), (1, wide))]
    return pl.pallas_call(
        functools.partial(mlp_backward_kernel, 512),
        grid=(pixels // rows,),
        in_specs=[tall(rows, channels), tall(rows, channels), tall(rows, wide), tall(rows, lanes)]
        + [fixed(array) for array in (scales, up, down)],
        out_specs=[tall(rows, channels), tall(rows, wide), tall(rows, channels)]
        + [pl.BlockSpec(array.shape, lambda i: (0, 0)) for array in sums],
        out_shape=[
            jax.ShapeDtypeStruct((pixels, channels), bf16),
            jax.ShapeDtypeStruct((pixels, wide), bf16),
            jax.ShapeDtypeStruct((pixels, channels), f32),
        ]
        + sums,
        compiler_params=room,
        name="mlp_backward",
    )(upstream, mixed, slope, sea, scales, up, down)


def cross_rows(former, latter):
    return lax.dot_general(former, latter, (((0,), (0,)), ((), ())), preferred_element_type=f32)


def by_transpose(former, latter):
    return lax.dot_general(former, latter, (((1,), (1,)), ((), ())), preferred_element_type=f32)


def block_forward(source, params, sea, ocean, dates):
    kernel, gain, shift, up, up_bias, down, down_bias = params
    height, breadth, channels = source.shape
    taps = kernel.astype(f32).reshape(49, channels)
    edges = borders(source, dates)
    mixed, local = stencil_forward(source, edges, taps, sea)
    first, square, ocean = sum_all(jnp.concatenate([local, jnp.broadcast_to(ocean, (1, channels))]))
    mean = first / ocean
    factor = lax.rsqrt(square / ocean - mean * mean + epsilon)
    scales = jnp.stack([mean, factor, gain.astype(f32), shift.astype(f32)])
    mixed = mixed.reshape(-1, channels)
    output, active, slope, normed = mlp_forward(
        mixed,
        source.reshape(-1, channels),
        sea.reshape(-1, lanes),
        scales,
        up,
        up_bias.astype(f32)[None],
        down,
        down_bias.astype(f32)[None],
    )
    return output, (source, edges, taps, mixed, scales, ocean, normed, slope, active)


def block_backward(upstream, params, sea, stored, dates):
    kernel, gain, shift, up, up_bias, down, down_bias = params
    source, edges, taps, mixed, scales, ocean, normed, slope, active = stored
    channels = source.shape[2]
    grad_branch, grad_hidden, grad_normed, local, down_sums, up_sums = mlp_backward(
        upstream, mixed, slope, sea.reshape(-1, lanes), scales, up, down
    )
    grad_shift, grad_gain = sum_all(local)
    mean, factor, gain = scales[0], scales[1], scales[2]
    unit = (mixed - mean) * factor
    weight = spread(sea.reshape(-1, lanes), channels) / ocean
    grad_mixed = factor * (gain * grad_normed - weight * (gain * grad_shift + unit * (gain * grad_gain)))
    grad_mixed = grad_mixed.astype(bf16).reshape(source.shape)
    grad_edges = borders(grad_mixed, dates)
    grad_kernel = kernel_grad(source, edges, grad_mixed)
    grad_source, source_sums = stencil_backward(grad_mixed, grad_edges, taps, sea, upstream.reshape(source.shape))
    grad_down = cross_rows(active, grad_branch)
    grad_up = cross_rows(normed, grad_hidden)
    return (
        grad_source.reshape(-1, channels),
        source_sums[0],
        (grad_kernel, grad_gain, grad_shift, grad_up, up_sums[0], grad_down, down_sums[0]),
    )


def shards(
    fine_map,
    ocean_mask,
    out_grad,
    encode_depth,
    encode_gain,
    encode_shift,
    encode_up,
    encode_up_bias,
    encode_down,
    encode_down_bias,
    widen_weight,
    widen_bias,
    bottle_depth,
    bottle_gain,
    bottle_shift,
    bottle_up,
    bottle_up_bias,
    bottle_down,
    bottle_down_bias,
    merge_weight,
    merge_bias,
    decode_depth,
    decode_gain,
    decode_shift,
    decode_up,
    decode_up_bias,
    decode_down,
    decode_down_bias,
):
    (encode_up, encode_down, widen_weight, bottle_up, bottle_down, merge_weight, decode_up, decode_down) = (
        lax.all_gather(weight, "lat", axis=0, tiled=True)
        for weight in (
            encode_up,
            encode_down,
            widen_weight,
            bottle_up,
            bottle_down,
            merge_weight,
            decode_up,
            decode_down,
        )
    )
    dates = fine_map.shape[0]
    fine = to_dates(fine_map)
    ocean_band = to_dates(ocean_mask).astype(f32)
    upstream = to_dates(out_grad)
    height, breadth, channels = fine.shape
    half_height, half_breadth = height // 2, breadth // 2
    wide = widen_weight.shape[1]
    coarse_band = jnp.max(ocean_band.reshape(half_height, 2, half_breadth, 2), axis=(1, 3))
    sea_fine = jnp.broadcast_to(ocean_band[..., None], (height, breadth, lanes))
    sea_coarse = jnp.broadcast_to(coarse_band[..., None], (half_height, half_breadth, lanes))
    encode = (encode_depth, encode_gain, encode_shift, encode_up, encode_up_bias, encode_down, encode_down_bias)
    bottle = (bottle_depth, bottle_gain, bottle_shift, bottle_up, bottle_up_bias, bottle_down, bottle_down_bias)
    decode = (decode_depth, decode_gain, decode_shift, decode_up, decode_up_bias, decode_down, decode_down_bias)
    merge_upper = merge_weight[:wide]
    merge_lower = merge_weight[wide:]
    ocean_fine = jnp.sum(ocean_band)
    ocean_coarse = jnp.sum(coarse_band)

    skip_rows, encode_stored = block_forward(fine, encode, sea_fine, ocean_fine, dates)
    blocks = skip_rows.reshape(half_height, 2, half_breadth, 2, channels).astype(f32)
    pooled = (jnp.sum(blocks, axis=(1, 3)) * 0.25).astype(bf16).reshape(-1, channels)
    coarse_in = jnp.dot(pooled, widen_weight, preferred_element_type=f32) + widen_bias.astype(f32)
    coarse_in = coarse_in.astype(bf16).reshape(half_height, half_breadth, wide)
    coarse_low, coarse_stored = block_forward(coarse_in, bottle, sea_coarse, ocean_coarse, dates)
    upper = jnp.dot(coarse_low, merge_upper, preferred_element_type=f32)
    upper = upper.reshape(half_height, 1, half_breadth, 1, channels)
    lower = jnp.dot(skip_rows, merge_lower, preferred_element_type=f32)
    lower = lower.reshape(half_height, 2, half_breadth, 2, channels)
    merged = (lower + upper).reshape(height, breadth, channels) + merge_bias.astype(f32)
    decode_rows, decode_stored = block_forward(merged.astype(bf16), decode, sea_fine, ocean_fine, dates)
    result = from_dates(decode_rows.reshape(fine.shape), dates)

    grad_merged, grad_merge_bias, decode_grads = block_backward(
        upstream.reshape(-1, channels), decode, sea_fine, decode_stored, dates
    )
    grad_block_sum = jnp.sum(
        grad_merged.astype(f32).reshape(half_height, 2, half_breadth, 2, channels), axis=(1, 3)
    ).reshape(-1, channels)
    grad_block_low = grad_block_sum.astype(bf16)
    grad_block_rest = (grad_block_sum - grad_block_low.astype(f32)).astype(bf16)
    grad_merge_weight = jnp.concatenate(
        [
            cross_rows(coarse_low, grad_block_low) + cross_rows(coarse_low, grad_block_rest),
            cross_rows(skip_rows, grad_merged),
        ],
        axis=0,
    )
    grad_coarse = by_transpose(grad_block_low, merge_upper) + by_transpose(grad_block_rest, merge_upper)
    grad_skip_direct = by_transpose(grad_merged, merge_lower)
    grad_wide, grad_widen_bias, bottle_grads = block_backward(grad_coarse, bottle, sea_coarse, coarse_stored, dates)
    grad_widen_weight = cross_rows(pooled, grad_wide)
    grad_pooled = by_transpose(grad_wide, widen_weight).reshape(half_height, 1, half_breadth, 1, channels) * 0.25
    grad_skip = grad_skip_direct.reshape(half_height, 2, half_breadth, 2, channels) + grad_pooled
    grad_fine, _, encode_grads = block_backward(
        grad_skip.reshape(-1, channels), encode, sea_fine, encode_stored, dates
    )
    fine_grad = from_dates(grad_fine.reshape(fine.shape), dates)

    def summed(parts):
        return [total.astype(f32) for total in lax.psum([part.astype(bf16) for part in parts], both)]

    decode_up_sum, decode_down_sum, merge_sum = summed([decode_grads[3], decode_grads[5], grad_merge_weight])
    bottle_up_sum, bottle_down_sum, widen_sum = summed([bottle_grads[3], bottle_grads[5], grad_widen_weight])
    encode_up_sum, encode_down_sum = summed([encode_grads[3], encode_grads[5]])
    small_parts = [
        encode_grads[0],
        encode_grads[4],
        encode_grads[6],
        grad_widen_bias,
        bottle_grads[0],
        bottle_grads[4],
        bottle_grads[6],
        grad_merge_bias,
        decode_grads[0],
        decode_grads[4],
        decode_grads[6],
    ]
    small = lax.psum(small_parts, both)
    return (
        result,
        fine_grad,
        small[0].reshape(encode_depth.shape),
        encode_grads[1],
        encode_grads[2],
        encode_up_sum,
        small[1],
        encode_down_sum,
        small[2],
        widen_sum,
        small[3],
        small[4].reshape(bottle_depth.shape),
        bottle_grads[1],
        bottle_grads[2],
        bottle_up_sum,
        small[5],
        bottle_down_sum,
        small[6],
        merge_sum,
        small[7],
        small[8].reshape(decode_depth.shape),
        decode_grads[1],
        decode_grads[2],
        decode_up_sum,
        small[9],
        decode_down_sum,
        small[10],
    )


def solution(mesh):
    whole = P()
    rows = P("lat", None)
    tile = P(None, "lat", "lon", None)
    block = (whole, whole, whole, rows, whole, rows, whole)
    placed = (tile, P(None, "lat", "lon"), tile) + block + (rows, whole) + block + (rows, whole) + block
    return jax.shard_map(
        shards,
        mesh=mesh,
        in_specs=placed,
        out_specs=(tile, tile) + (whole,) * 25,
        check_vma=False,
    )
```

```python
import functools
import math

import jax
import jax.numpy as jnp
from jax import lax
from jax.experimental import pallas as pl
from jax.experimental.pallas import tpu as pltpu
from jax.sharding import PartitionSpec as P

epsilon = 1e-05
both = ("lat", "lon")
bf16 = jnp.bfloat16
f32 = jnp.float32
lanes = 128
strip = 12
room = pltpu.CompilerParams(vmem_limit_bytes=56 << 20)


def exchange_pairs(count, group, step):
    return [(i, (i // group) * group + ((i % group) ^ step)) for i in range(count)]


def to_dates(tiles):
    dates, count = tiles.shape[0], lax.axis_size("lat")
    own = lax.axis_index("lat") % dates
    pieces = [lax.dynamic_index_in_dim(tiles, own, 0, keepdims=False)]
    for step in range(1, dates):
        pieces.append(
            lax.ppermute(
                lax.dynamic_index_in_dim(tiles, own ^ step, 0, keepdims=False),
                "lat",
                exchange_pairs(count, dates, step),
            )
        )
    stacked = jnp.stack(pieces)
    ordered = [lax.dynamic_index_in_dim(stacked, own ^ tile, 0, keepdims=False) for tile in range(dates)]
    return jnp.concatenate(ordered, axis=0)


def from_dates(band, dates):
    count = lax.axis_size("lat")
    own = lax.axis_index("lat") % dates
    tiles = band.reshape((dates, band.shape[0] // dates) + band.shape[1:])
    pieces = [lax.dynamic_index_in_dim(tiles, own, 0, keepdims=False)]
    for step in range(1, dates):
        pieces.append(
            lax.ppermute(
                lax.dynamic_index_in_dim(tiles, own ^ step, 0, keepdims=False),
                "lat",
                exchange_pairs(count, dates, step),
            )
        )
    stacked = jnp.stack(pieces)
    return jnp.stack([lax.dynamic_index_in_dim(stacked, own ^ date, 0, keepdims=False) for date in range(dates)])


def borders(source, dates):
    count = lax.axis_size("lon")
    forward = [(i, (i + 1) % count) for i in range(count)]
    backward = [(target, origin) for origin, target in forward]
    left = lax.ppermute(source[:, -3:], "lon", forward)
    right = lax.ppermute(source[:, :3], "lon", backward)
    tiles = lax.axis_size("lat")
    if tiles == dates:
        return left, right
    down = [(i, i + dates) for i in range(tiles - dates)]
    up = [(target, origin) for origin, target in down]
    last = jnp.concatenate([left[-3:], source[-3:], right[-3:]], axis=1)
    first = jnp.concatenate([left[:3], source[:3], right[:3]], axis=1)
    return left, right, lax.ppermute(last, "lat", down), lax.ppermute(first, "lat", up)


def sum_all(local):
    count = lax.axis_size(both)
    copies = jnp.broadcast_to(local[None], (count,) + local.shape)
    return jnp.sum(lax.all_to_all(copies, both, 0, 0, tiled=False), axis=0)


def fill_extended(wide_ref, centre, edges):
    rows, columns = centre.shape[0], centre.shape[1]
    blank = jnp.zeros((3, columns + 16, lanes), f32)
    wide_ref[0:3] = blank
    wide_ref[rows + 3 :] = blank
    wide_ref[3 : rows + 3, 8 : columns + 8] = centre[...].astype(f32)
    wide_ref[3 : rows + 3, 5:8] = edges[0][...].astype(f32)
    wide_ref[3 : rows + 3, columns + 8 : columns + 11] = edges[1][...].astype(f32)
    if len(edges) > 2:
        wide_ref[0:3, 5 : columns + 11] = edges[2][...].astype(f32)
        wide_ref[rows + 3 :, 5 : columns + 11] = edges[3][...].astype(f32)


def strip_sum(wide_ref, taps, top, start, flipped):
    total = None
    for column in range(7):
        window = wide_ref[pl.ds(top, strip + 6), start + 5 + column : start + 13 + column, :]
        for across in range(7):
            place = 7 * across + column
            tap = taps[pl.ds(48 - place if flipped else place, 8, stride=0), :]
            term = window[across : across + strip] * tap[None]
            total = term if total is None else total + term
    return total


def stencil_forward_kernel(edge_count, source, *refs):
    edges = refs[:edge_count]
    taps, sea, mixed, sums, wide_ref = refs[edge_count:]
    rows, columns = source.shape[0], source.shape[1]
    fill_extended(wide_ref, source, edges)

    def step(index, carry):
        first, square = carry
        top = index * strip
        for start in range(0, columns, 8):
            here = (pl.ds(top, strip), slice(start, start + 8))
            total = strip_sum(wide_ref, taps, top, start, False)
            mixed[here] = total
            masked = total * sea[here]
            first = first + jnp.sum(masked, axis=0)
            square = square + jnp.sum(masked * total, axis=0)
        return first, square

    zero = jnp.zeros((8, lanes), f32)
    first, square = lax.fori_loop(0, rows // strip, step, (zero, zero))
    sums[0:1] = jnp.sum(first, axis=0, keepdims=True)
    sums[1:2] = jnp.sum(square, axis=0, keepdims=True)


def stencil_backward_kernel(edge_count, grad, *refs):
    edges = refs[:edge_count]
    taps, sea, upstream, out, sums, wide_ref = refs[edge_count:]
    rows, columns = grad.shape[0], grad.shape[1]
    fill_extended(wide_ref, grad, edges)

    def step(index, first):
        top = index * strip
        for start in range(0, columns, 8):
            here = (pl.ds(top, strip), slice(start, start + 8))
            total = strip_sum(wide_ref, taps, top, start, True)
            low = (total + upstream[here].astype(f32) * sea[here]).astype(bf16)
            out[here] = low
            first = first + jnp.sum(low.astype(f32), axis=0)
        return first

    first = lax.fori_loop(0, rows // strip, step, jnp.zeros((8, lanes), f32))
    sums[...] = jnp.sum(first, axis=0, keepdims=True)


def kernel_grad_kernel(edge_count, source, *refs):
    edges = refs[:edge_count]
    grad, out, wide_ref, sums_ref = refs[edge_count:]
    rows, columns = source.shape[0], source.shape[1]
    fill_extended(wide_ref, source, edges)
    sums_ref[...] = jnp.zeros_like(sums_ref)

    def step(index, carry):
        top = index * strip
        for start in range(0, columns, 8):
            upstream = grad[pl.ds(top, strip), start : start + 8, :].astype(f32)
            for column in range(7):
                window = wide_ref[pl.ds(top, strip + 6), start + 5 + column : start + 13 + column, :]
                for across in range(7):
                    sums_ref[7 * across + column] += jnp.sum(window[across : across + strip] * upstream, axis=0)
        return carry

    lax.fori_loop(0, rows // strip, step, 0)
    out[0, 0:49] = jnp.sum(sums_ref[...], axis=1)
    out[0, 49:56] = jnp.zeros((7, lanes), f32)


def by_channel(array):
    rest = array.shape[:-1]
    return pl.BlockSpec(rest + (lanes,), lambda tile: (0,) * len(rest) + (tile,))


def same_block(array):
    return pl.BlockSpec(array.shape, lambda tile: (0,) * array.ndim)


def wide_scratch(rows, columns):
    return pltpu.VMEM((rows + 6, columns + 16, lanes), f32)


def stencil_forward(source, edges, taps, sea):
    rows, columns, channels = source.shape
    sums = jax.ShapeDtypeStruct((2, channels), f32)
    mixed = jax.ShapeDtypeStruct(source.shape, f32)
    return pl.pallas_call(
        functools.partial(stencil_forward_kernel, len(edges)),
        grid=(pl.cdiv(channels, lanes),),
        in_specs=[by_channel(array) for array in (source, *edges, taps)] + [same_block(sea)],
        out_specs=[by_channel(mixed), by_channel(sums)],
        out_shape=[mixed, sums],
        scratch_shapes=[wide_scratch(rows, columns)],
        compiler_params=room,
        name="stencil_forward",
    )(source, *edges, taps, sea)


def stencil_backward(grad, edges, taps, sea, upstream):
    rows, columns, channels = grad.shape
    out = jax.ShapeDtypeStruct(grad.shape, bf16)
    sums = jax.ShapeDtypeStruct((1, channels), f32)
    return pl.pallas_call(
        functools.partial(stencil_backward_kernel, len(edges)),
        grid=(pl.cdiv(channels, lanes),),
        in_specs=[by_channel(array) for array in (grad, *edges, taps)] + [same_block(sea), by_channel(upstream)],
        out_specs=[by_channel(out), by_channel(sums)],
        out_shape=[out, sums],
        scratch_shapes=[wide_scratch(rows, columns)],
        compiler_params=room,
        name="stencil_backward",
    )(grad, *edges, taps, sea, upstream)


def kernel_grad(source, edges, grad):
    rows, columns, channels = source.shape
    tiles = pl.cdiv(channels, lanes)
    out = jax.ShapeDtypeStruct((tiles, 56, lanes), f32)
    return pl.pallas_call(
        functools.partial(kernel_grad_kernel, len(edges)),
        grid=(tiles,),
        in_specs=[by_channel(array) for array in (source, *edges, grad)],
        out_specs=pl.BlockSpec((1, 56, lanes), lambda tile: (tile, 0, 0)),
        out_shape=out,
        scratch_shapes=[wide_scratch(rows, columns), pltpu.VMEM((49, 8, lanes), f32)],
        compiler_params=room,
        name="kernel_grad",
    )(source, *edges, grad)


def chunks_of(width, size):
    edges = list(range(0, width, size))
    if len(edges) > 1 and width - edges[-1] < size // 2:
        edges.pop()
    return list(zip(edges, edges[1:] + [width]))


def spread(sea, channels):
    return jnp.concatenate([sea] * pl.cdiv(channels, lanes), axis=1)[:, :channels]


def gelu_pair(hidden):
    below = 0.5 + 0.5 * lax.erf(hidden * math.sqrt(0.5))
    density = jnp.exp(-0.5 * hidden * hidden) * (1.0 / math.sqrt(2.0 * math.pi))
    return hidden * below, below + hidden * density


def mlp_forward_kernel(
    size, mixed, source, sea, scales, up, up_bias, down, down_bias, out, active, slope, normed
):
    unit = (mixed[...] - scales[0:1]) * scales[1:2]
    low = (unit * scales[2:3] + scales[3:4]).astype(bf16)
    normed[...] = low
    branch = down_bias[...]
    for a, b in chunks_of(up.shape[1], size):
        hidden = jnp.dot(low, up[:, a:b], preferred_element_type=f32) + up_bias[:, a:b]
        value, rise = gelu_pair(hidden)
        value = value.astype(bf16)
        active[:, a:b] = value
        slope[:, a:b] = rise.astype(bf16)
        branch = branch + jnp.dot(value, down[a:b, :], preferred_element_type=f32)
    mask = spread(sea[...], out.shape[1])
    out[...] = (mask * (source[...].astype(f32) + branch)).astype(bf16)


def mlp_backward_kernel(
    size,
    upstream,
    mixed,
    slope,
    sea,
    scales,
    up,
    down,
    grad_branch,
    grad_hidden,
    grad_normed,
    sums,
    down_sums,
    up_sums,
):
    @pl.when(pl.program_id(0) == 0)
    def _():
        sums[...] = jnp.zeros_like(sums)
        down_sums[...] = jnp.zeros_like(down_sums)
        up_sums[...] = jnp.zeros_like(up_sums)

    mask = spread(sea[...], upstream.shape[1])
    low = (mask * upstream[...].astype(f32)).astype(bf16)
    grad_branch[...] = low
    down_sums[...] += jnp.sum(low.astype(f32), axis=0, keepdims=True)
    normed = None
    for a, b in chunks_of(up.shape[1], size):
        grad_active = lax.dot_general(low, down[a:b, :], (((1,), (1,)), ((), ())), preferred_element_type=f32)
        hidden = (grad_active * slope[:, a:b].astype(f32)).astype(bf16)
        grad_hidden[:, a:b] = hidden
        up_sums[:, a:b] += jnp.sum(hidden.astype(f32), axis=0, keepdims=True)
        part = lax.dot_general(hidden, up[:, a:b], (((1,), (1,)), ((), ())), preferred_element_type=f32)
        normed = part if normed is None else normed + part
    grad_normed[...] = normed
    unit = (mixed[...] - scales[0:1]) * scales[1:2]
    sums[0:1] += jnp.sum(normed, axis=0, keepdims=True)
    sums[1:2] += jnp.sum(normed * unit, axis=0, keepdims=True)


def tall(rows, width):
    return pl.BlockSpec((rows, width), lambda i: (i, 0))


def fixed(array):
    return pl.BlockSpec(array.shape, lambda i: (0, 0), pipeline_mode=pl.Buffered(1))


def mlp_forward(mixed, source, sea, scales, up, up_bias, down, down_bias):
    pixels, channels = mixed.shape
    wide = up.shape[1]
    rows = math.gcd(pixels, 384)
    return pl.pallas_call(
        functools.partial(mlp_forward_kernel, 512),
        grid=(pixels // rows,),
        in_specs=[tall(rows, channels), tall(rows, channels), tall(rows, lanes)]
        + [fixed(array) for array in (scales, up, up_bias, down, down_bias)],
        out_specs=[tall(rows, channels), tall(rows, wide), tall(rows, wide), tall(rows, channels)],
        out_shape=[jax.ShapeDtypeStruct((pixels, width), bf16) for width in (channels, wide, wide, channels)],
        compiler_params=room,
        name="mlp_forward",
    )(mixed, source, sea, scales, up, up_bias, down, down_bias)


def mlp_backward(upstream, mixed, slope, sea, scales, up, down):
    pixels, channels = mixed.shape
    wide = up.shape[1]
    rows = math.gcd(pixels, 384)
    sums = [jax.ShapeDtypeStruct(shape, f32) for shape in ((2, channels), (1, channels), (1, wide))]
    return pl.pallas_call(
        functools.partial(mlp_backward_kernel, 512),
        grid=(pixels // rows,),
        in_specs=[tall(rows, channels), tall(rows, channels), tall(rows, wide), tall(rows, lanes)]
        + [fixed(array) for array in (scales, up, down)],
        out_specs=[tall(rows, channels), tall(rows, wide), tall(rows, channels)]
        + [pl.BlockSpec(array.shape, lambda i: (0, 0)) for array in sums],
        out_shape=[
            jax.ShapeDtypeStruct((pixels, channels), bf16),
            jax.ShapeDtypeStruct((pixels, wide), bf16),
            jax.ShapeDtypeStruct((pixels, channels), f32),
        ]
        + sums,
        compiler_params=room,
        name="mlp_backward",
    )(upstream, mixed, slope, sea, scales, up, down)


def weight_grads_kernel(grad_branch, normed, active, grad_hidden, out, branch_ref, normed_ref):
    @pl.when(pl.program_id(0) == 0)
    def _():
        branch_ref[...] = grad_branch[...].T
        normed_ref[...] = normed[...].T

    up = jnp.dot(normed_ref[...], grad_hidden[...], preferred_element_type=f32).astype(bf16)
    down = jnp.dot(branch_ref[...], active[...], preferred_element_type=f32).astype(bf16)
    for part in range(out.shape[1]):
        out[0, part] = up[:, part * lanes : (part + 1) * lanes]
        out[1, part] = down[:, part * lanes : (part + 1) * lanes]


def weight_grads(grad_branch, normed, active, grad_hidden):
    pixels, channels = normed.shape
    hidden = active.shape[1]
    tiles = pl.cdiv(hidden, lanes)
    parts = next(count for count in (5, 4, 3, 2, 1) if count == 2 or tiles % count == 0)
    return pl.pallas_call(
        weight_grads_kernel,
        grid=(pl.cdiv(tiles, parts),),
        in_specs=[fixed(grad_branch), fixed(normed)]
        + [pl.BlockSpec((pixels, parts * lanes), lambda tile: (0, tile))] * 2,
        out_specs=pl.BlockSpec((2, parts, channels, lanes), lambda tile: (0, tile, 0, 0)),
        out_shape=jax.ShapeDtypeStruct((2, tiles, channels, lanes), bf16),
        scratch_shapes=[pltpu.VMEM((channels, pixels), bf16)] * 2,
        compiler_params=room,
        name="weight_grads",
    )(grad_branch, normed, active, grad_hidden)


def unpack_kernel(core, own, other, up, down):
    mine, theirs = own[...].astype(f32), other[...].astype(f32)
    first = core[0] == 0
    up[...] = jnp.where(first, mine, theirs)
    down[...] = jnp.where(first, theirs, mine).T


def unpack(core, own, other, channels, hidden):
    block = pl.BlockSpec((channels, lanes), lambda tile, core: (tile, 0))
    return pl.pallas_call(
        unpack_kernel,
        grid_spec=pltpu.PrefetchScalarGridSpec(
            num_scalar_prefetch=1,
            grid=(pl.cdiv(hidden, lanes),),
            in_specs=[block, block],
            out_specs=[
                pl.BlockSpec((channels, lanes), lambda tile, core: (0, tile)),
                pl.BlockSpec((lanes, channels), lambda tile, core: (tile, 0)),
            ],
        ),
        out_shape=[
            jax.ShapeDtypeStruct((channels, hidden), f32),
            jax.ShapeDtypeStruct((hidden, channels), f32),
        ],
        compiler_params=room,
        name="unpack",
    )(core, own, other)


def swap(array, axis, step):
    return lax.ppermute(array, axis, [(i, i ^ step) for i in range(lax.axis_size(axis))])


def take(stacked, index):
    return lax.dynamic_index_in_dim(stacked, index, 0, keepdims=False)


def exchange_add(stacked, axis, own, scale):
    count = stacked.shape[0]
    got = [swap(take(stacked, own ^ step), axis, scale * step) for step in range(1, count)]
    total = take(stacked, own).astype(f32)
    for piece in got:
        total = total + piece.astype(f32)
    return total.astype(bf16)


def exchange_all(piece, axis, own, scale, count):
    got = jnp.stack([piece] + [swap(piece, axis, scale * step) for step in range(1, count)])
    return jnp.concatenate([take(got, own ^ place) for place in range(count)], axis=0)


def sum_group(pair):
    tiles, columns = lax.axis_size("lat"), lax.axis_size("lon") // 2
    tile, place = lax.axis_index("lat"), lax.axis_index("lon")
    core, column = place % 2, place // 2
    rows = pair.shape[1]
    padded = -(-rows // (8 * tiles * columns)) * 8 * tiles * columns
    pair = jnp.pad(pair, ((0, 0), (0, padded - rows), (0, 0)))
    got = swap(take(pair, 1 - core), "lon", 1)
    half = (take(pair, core).astype(f32) + got.astype(f32)).astype(bf16)
    share = exchange_add(half.reshape(tiles, -1, lanes), "lat", tile, 1)
    share = exchange_add(share.reshape(columns, -1, lanes), "lon", column, 2)
    share = exchange_all(share, "lon", column, 2, columns)
    half = exchange_all(share, "lat", tile, 1, tiles)
    return half, swap(half, "lon", 1)


def sum_small(flat):
    count = lax.axis_size(both)
    rows = flat.shape[0]
    padded = -(-rows // (8 * count)) * 8 * count
    pieces = jnp.pad(flat, ((0, padded - rows), (0, 0))).reshape(count, -1, lanes)
    share = jnp.sum(lax.all_to_all(pieces, both, 0, 0, tiled=False), axis=0)
    copies = jnp.broadcast_to(share[None], pieces.shape)
    return lax.all_to_all(copies, both, 0, 0, tiled=False).reshape(padded, lanes)[:rows]


def cross_rows(former, latter):
    return lax.dot_general(former, latter, (((0,), (0,)), ((), ())), preferred_element_type=f32)


def by_transpose(former, latter):
    return lax.dot_general(former, latter, (((1,), (1,)), ((), ())), preferred_element_type=f32)


def block_forward(source, params, sea, ocean, dates):
    kernel, gain, shift, up, up_bias, down, down_bias = params
    height, breadth, channels = source.shape
    taps = kernel.astype(f32).reshape(49, channels)
    edges = borders(source, dates)
    mixed, local = stencil_forward(source, edges, taps, sea)
    first, square, ocean = sum_all(jnp.concatenate([local, jnp.broadcast_to(ocean, (1, channels))]))
    mean = first / ocean
    factor = lax.rsqrt(square / ocean - mean * mean + epsilon)
    scales = jnp.stack([mean, factor, gain.astype(f32), shift.astype(f32)])
    mixed = mixed.reshape(-1, channels)
    output, active, slope, normed = mlp_forward(
        mixed,
        source.reshape(-1, channels),
        sea.reshape(-1, lanes),
        scales,
        up,
        up_bias.astype(f32)[None],
        down,
        down_bias.astype(f32)[None],
    )
    return output, (source, edges, taps, mixed, scales, ocean, normed, slope, active)


def block_backward(upstream, params, sea, stored, dates):
    kernel, gain, shift, up, up_bias, down, down_bias = params
    source, edges, taps, mixed, scales, ocean, normed, slope, active = stored
    channels = source.shape[2]
    grad_branch, grad_hidden, grad_normed, local, down_sums, up_sums = mlp_backward(
        upstream, mixed, slope, sea.reshape(-1, lanes), scales, up, down
    )
    grad_shift, grad_gain = sum_all(local)
    mean, factor, gain = scales[0], scales[1], scales[2]
    unit = (mixed - mean) * factor
    weight = spread(sea.reshape(-1, lanes), channels) / ocean
    grad_mixed = factor * (gain * grad_normed - weight * (gain * grad_shift + unit * (gain * grad_gain)))
    grad_mixed = grad_mixed.astype(bf16).reshape(source.shape)
    grad_edges = borders(grad_mixed, dates)
    grad_kernel = kernel_grad(source, edges, grad_mixed)
    grad_source, source_sums = stencil_backward(grad_mixed, grad_edges, taps, sea, upstream.reshape(source.shape))
    return (
        grad_source.reshape(-1, channels),
        source_sums,
        (grad_gain, grad_shift, (grad_branch, normed, active, grad_hidden)),
        (grad_kernel, down_sums, up_sums),
    )


def shards(
    fine_map,
    ocean_mask,
    out_grad,
    encode_depth,
    encode_gain,
    encode_shift,
    encode_up,
    encode_up_bias,
    encode_down,
    encode_down_bias,
    widen_weight,
    widen_bias,
    bottle_depth,
    bottle_gain,
    bottle_shift,
    bottle_up,
    bottle_up_bias,
    bottle_down,
    bottle_down_bias,
    merge_weight,
    merge_bias,
    decode_depth,
    decode_gain,
    decode_shift,
    decode_up,
    decode_up_bias,
    decode_down,
    decode_down_bias,
):
    (encode_up, encode_down, widen_weight, bottle_up, bottle_down, merge_weight, decode_up, decode_down) = (
        lax.all_gather(weight, "lat", axis=0, tiled=True)
        for weight in (
            encode_up,
            encode_down,
            widen_weight,
            bottle_up,
            bottle_down,
            merge_weight,
            decode_up,
            decode_down,
        )
    )
    dates = fine_map.shape[0]
    fine = to_dates(fine_map)
    ocean_band = to_dates(ocean_mask).astype(f32)
    upstream = to_dates(out_grad)
    height, breadth, channels = fine.shape
    half_height, half_breadth = height // 2, breadth // 2
    wide = widen_weight.shape[1]
    coarse_band = jnp.max(ocean_band.reshape(half_height, 2, half_breadth, 2), axis=(1, 3))
    sea_fine = jnp.broadcast_to(ocean_band[..., None], (height, breadth, lanes))
    sea_coarse = jnp.broadcast_to(coarse_band[..., None], (half_height, half_breadth, lanes))
    encode = (encode_depth, encode_gain, encode_shift, encode_up, encode_up_bias, encode_down, encode_down_bias)
    bottle = (bottle_depth, bottle_gain, bottle_shift, bottle_up, bottle_up_bias, bottle_down, bottle_down_bias)
    decode = (decode_depth, decode_gain, decode_shift, decode_up, decode_up_bias, decode_down, decode_down_bias)
    merge_upper = merge_weight[:wide]
    merge_lower = merge_weight[wide:]
    ocean_fine = jnp.sum(ocean_band)
    ocean_coarse = jnp.sum(coarse_band)

    skip_rows, encode_stored = block_forward(fine, encode, sea_fine, ocean_fine, dates)
    blocks = skip_rows.reshape(half_height, 2, half_breadth, 2, channels).astype(f32)
    pooled = (jnp.sum(blocks, axis=(1, 3)) * 0.25).astype(bf16).reshape(-1, channels)
    coarse_in = jnp.dot(pooled, widen_weight, preferred_element_type=f32) + widen_bias.astype(f32)
    coarse_in = coarse_in.astype(bf16).reshape(half_height, half_breadth, wide)
    coarse_low, coarse_stored = block_forward(coarse_in, bottle, sea_coarse, ocean_coarse, dates)
    upper = jnp.dot(coarse_low, merge_upper, preferred_element_type=f32)
    upper = upper.reshape(half_height, 1, half_breadth, 1, channels)
    lower = jnp.dot(skip_rows, merge_lower, preferred_element_type=f32)
    lower = lower.reshape(half_height, 2, half_breadth, 2, channels)
    merged = (lower + upper).reshape(height, breadth, channels) + merge_bias.astype(f32)
    decode_rows, decode_stored = block_forward(merged.astype(bf16), decode, sea_fine, ocean_fine, dates)
    result = from_dates(decode_rows.reshape(fine.shape), dates)

    grad_merged, merge_sums, decode_grads, decode_small = block_backward(
        upstream.reshape(-1, channels), decode, sea_fine, decode_stored, dates
    )
    grad_block_sum = jnp.sum(
        grad_merged.astype(f32).reshape(half_height, 2, half_breadth, 2, channels), axis=(1, 3)
    ).reshape(-1, channels)
    grad_block_low = grad_block_sum.astype(bf16)
    grad_block_rest = (grad_block_sum - grad_block_low.astype(f32)).astype(bf16)
    grad_merge_weight = jnp.concatenate(
        [
            cross_rows(coarse_low, grad_block_low) + cross_rows(coarse_low, grad_block_rest),
            cross_rows(skip_rows, grad_merged),
        ],
        axis=0,
    )
    grad_branch, normed, active, grad_hidden = decode_grads[2]
    decode_parts = [cross_rows(normed, grad_hidden), cross_rows(active, grad_branch), grad_merge_weight]
    decode_sums = lax.psum([part.astype(bf16) for part in decode_parts], both)
    decode_up_sum, decode_down_sum, merge_sum = [total.astype(f32) for total in decode_sums]

    grad_coarse = by_transpose(grad_block_low, merge_upper) + by_transpose(grad_block_rest, merge_upper)
    grad_skip_direct = by_transpose(grad_merged, merge_lower)
    grad_wide, widen_sums, bottle_grads, bottle_small = block_backward(
        grad_coarse, bottle, sea_coarse, coarse_stored, dates
    )
    core = (lax.axis_index("lon") % 2).astype(jnp.int32)[None]
    bottle_pair = weight_grads(*bottle_grads[2]).reshape(2, -1, lanes)
    bottle_up_sum, bottle_down_sum = unpack(core, *sum_group(bottle_pair), wide, bottle_up.shape[1])

    grad_widen = cross_rows(pooled, grad_wide).astype(bf16)
    widen_tiles = pl.cdiv(wide, 2 * lanes)
    grad_widen = jnp.pad(grad_widen, ((0, 0), (0, 2 * widen_tiles * lanes - wide)))
    grad_widen = grad_widen.reshape(channels, 2, widen_tiles, lanes).transpose(1, 2, 0, 3).reshape(2, -1, lanes)
    grad_pooled = by_transpose(grad_wide, widen_weight).reshape(half_height, 1, half_breadth, 1, channels) * 0.25
    grad_skip = grad_skip_direct.reshape(half_height, 2, half_breadth, 2, channels) + grad_pooled
    grad_fine, _, encode_grads, encode_small = block_backward(
        grad_skip.reshape(-1, channels), encode, sea_fine, encode_stored, dates
    )
    fine_grad = from_dates(grad_fine.reshape(fine.shape), dates)
    encode_pair = weight_grads(*encode_grads[2]).reshape(2, -1, lanes)
    own, other = sum_group(jnp.concatenate([encode_pair, grad_widen], axis=1))
    encode_up_sum, encode_down_sum = unpack(core, own, other, channels, encode_up.shape[1])
    start = encode_pair.shape[1]
    lower = jnp.where(core == 0, own[start : start + grad_widen.shape[1]], other[start : start + grad_widen.shape[1]])
    upper = jnp.where(core == 0, other[start : start + grad_widen.shape[1]], own[start : start + grad_widen.shape[1]])
    widen_sum = jnp.stack([lower, upper]).reshape(2 * widen_tiles, channels, lanes).astype(f32)
    widen_sum = widen_sum.transpose(1, 0, 2).reshape(channels, -1)[:, :wide]

    kernels = [encode_small[0], bottle_small[0], decode_small[0]]
    rows = [encode_small[1:], (widen_sums,), bottle_small[1:], (merge_sums,), decode_small[1:]]
    rows = [row for group in rows for row in group]
    padded = [jnp.pad(row, ((0, 0), (0, -row.shape[1] % lanes))) for row in rows]
    line = jnp.concatenate(padded, axis=1)
    small = sum_small(jnp.concatenate([array.reshape(-1, lanes) for array in kernels] + [line.reshape(-1, lanes)]))
    kernel_sums, at = [], 0
    for array, shape in zip(kernels, (encode_depth.shape, bottle_depth.shape, decode_depth.shape)):
        count = array.shape[0] * 56
        total = small[at : at + count].reshape(array.shape)[:, :49].transpose(1, 0, 2).reshape(49, -1)
        kernel_sums.append(total[:, : shape[2]].reshape(shape))
        at += count
    line = small[at:].reshape(-1)
    row_sums, at = [], 0
    for row, wider in zip(rows, padded):
        row_sums.append(line[at : at + row.shape[1]])
        at += wider.shape[1]
    (encode_upb, encode_downb, widen_b, bottle_upb, bottle_downb, bottle_merge_b, decode_upb, decode_downb) = (
        row_sums[1],
        row_sums[0],
        row_sums[2],
        row_sums[4],
        row_sums[3],
        row_sums[5],
        row_sums[7],
        row_sums[6],
    )
    return (
        result,
        fine_grad,
        kernel_sums[0],
        encode_grads[0],
        encode_grads[1],
        encode_up_sum,
        encode_upb,
        encode_down_sum,
        encode_downb,
        widen_sum,
        widen_b,
        kernel_sums[1],
        bottle_grads[0],
        bottle_grads[1],
        bottle_up_sum,
        bottle_upb,
        bottle_down_sum,
        bottle_downb,
        merge_sum,
        bottle_merge_b,
        kernel_sums[2],
        decode_grads[0],
        decode_grads[1],
        decode_up_sum,
        decode_upb,
        decode_down_sum,
        decode_downb,
    )


def solution(mesh):
    whole = P()
    rows = P("lat", None)
    tile = P(None, "lat", "lon", None)
    block = (whole, whole, whole, rows, whole, rows, whole)
    placed = (tile, P(None, "lat", "lon"), tile) + block + (rows, whole) + block + (rows, whole) + block
    return jax.shard_map(
        shards,
        mesh=mesh,
        in_specs=placed,
        out_specs=(tile, tile) + (whole,) * 25,
        check_vma=False,
    )
```

```python
import functools
import math

import jax
import jax.numpy as jnp
from jax import lax
from jax.experimental import pallas as pl
from jax.experimental.pallas import tpu as pltpu
from jax.sharding import PartitionSpec as P

epsilon = 1e-05
both = ("lat", "lon")
bf16 = jnp.bfloat16
f32 = jnp.float32
lanes = 128
strip = 12
room = pltpu.CompilerParams(vmem_limit_bytes=56 << 20)


def exchange_pairs(count, group, step):
    return [(i, (i // group) * group + ((i % group) ^ step)) for i in range(count)]


def to_dates(tiles):
    dates, count = tiles.shape[0], lax.axis_size("lat")
    own = lax.axis_index("lat") % dates
    pieces = [lax.dynamic_index_in_dim(tiles, own, 0, keepdims=False)]
    for step in range(1, dates):
        pieces.append(
            lax.ppermute(
                lax.dynamic_index_in_dim(tiles, own ^ step, 0, keepdims=False),
                "lat",
                exchange_pairs(count, dates, step),
            )
        )
    stacked = jnp.stack(pieces)
    ordered = [lax.dynamic_index_in_dim(stacked, own ^ tile, 0, keepdims=False) for tile in range(dates)]
    return jnp.concatenate(ordered, axis=0)


def from_dates(band, dates):
    count = lax.axis_size("lat")
    own = lax.axis_index("lat") % dates
    tiles = band.reshape((dates, band.shape[0] // dates) + band.shape[1:])
    pieces = [lax.dynamic_index_in_dim(tiles, own, 0, keepdims=False)]
    for step in range(1, dates):
        pieces.append(
            lax.ppermute(
                lax.dynamic_index_in_dim(tiles, own ^ step, 0, keepdims=False),
                "lat",
                exchange_pairs(count, dates, step),
            )
        )
    stacked = jnp.stack(pieces)
    return jnp.stack([lax.dynamic_index_in_dim(stacked, own ^ date, 0, keepdims=False) for date in range(dates)])


def borders(source, dates):
    count = lax.axis_size("lon")
    forward = [(i, (i + 1) % count) for i in range(count)]
    backward = [(target, origin) for origin, target in forward]
    left = lax.ppermute(source[:, -3:], "lon", forward)
    right = lax.ppermute(source[:, :3], "lon", backward)
    tiles = lax.axis_size("lat")
    if tiles == dates:
        return left, right
    down = [(i, i + dates) for i in range(tiles - dates)]
    up = [(target, origin) for origin, target in down]
    last = jnp.concatenate([left[-3:], source[-3:], right[-3:]], axis=1)
    first = jnp.concatenate([left[:3], source[:3], right[:3]], axis=1)
    return left, right, lax.ppermute(last, "lat", down), lax.ppermute(first, "lat", up)


def sum_all(local):
    count = lax.axis_size(both)
    copies = jnp.broadcast_to(local[None], (count,) + local.shape)
    return jnp.sum(lax.all_to_all(copies, both, 0, 0, tiled=False), axis=0)


def fill_extended(wide_ref, centre, edges):
    rows, columns = centre.shape[0], centre.shape[1]
    blank = jnp.zeros((3, columns + 16, lanes), f32)
    wide_ref[0:3] = blank
    wide_ref[rows + 3 :] = blank
    wide_ref[3 : rows + 3, 8 : columns + 8] = centre[...].astype(f32)
    wide_ref[3 : rows + 3, 5:8] = edges[0][...].astype(f32)
    wide_ref[3 : rows + 3, columns + 8 : columns + 11] = edges[1][...].astype(f32)
    if len(edges) > 2:
        wide_ref[0:3, 5 : columns + 11] = edges[2][...].astype(f32)
        wide_ref[rows + 3 :, 5 : columns + 11] = edges[3][...].astype(f32)


def strip_sum(wide_ref, taps, top, start, flipped):
    total = None
    for column in range(7):
        window = wide_ref[pl.ds(top, strip + 6), start + 5 + column : start + 13 + column, :]
        for across in range(7):
            place = 7 * across + column
            tap = taps[pl.ds(48 - place if flipped else place, 8, stride=0), :]
            term = window[across : across + strip] * tap[None]
            total = term if total is None else total + term
    return total


def stencil_forward_kernel(edge_count, source, *refs):
    edges = refs[:edge_count]
    taps, sea, mixed, sums, wide_ref = refs[edge_count:]
    rows, columns = source.shape[0], source.shape[1]
    fill_extended(wide_ref, source, edges)

    def step(index, carry):
        first, square = carry
        top = index * strip
        for start in range(0, columns, 8):
            here = (pl.ds(top, strip), slice(start, start + 8))
            total = strip_sum(wide_ref, taps, top, start, False)
            mixed[here] = total
            masked = total * sea[here]
            first = first + jnp.sum(masked, axis=0)
            square = square + jnp.sum(masked * total, axis=0)
        return first, square

    zero = jnp.zeros((8, lanes), f32)
    first, square = lax.fori_loop(0, rows // strip, step, (zero, zero))
    sums[0:1] = jnp.sum(first, axis=0, keepdims=True)
    sums[1:2] = jnp.sum(square, axis=0, keepdims=True)


def stencil_backward_kernel(edge_count, grad, *refs):
    edges = refs[:edge_count]
    taps, sea, upstream, out, sums, wide_ref = refs[edge_count:]
    rows, columns = grad.shape[0], grad.shape[1]
    fill_extended(wide_ref, grad, edges)

    def step(index, first):
        top = index * strip
        for start in range(0, columns, 8):
            here = (pl.ds(top, strip), slice(start, start + 8))
            total = strip_sum(wide_ref, taps, top, start, True)
            low = (total + upstream[here].astype(f32) * sea[here]).astype(bf16)
            out[here] = low
            first = first + jnp.sum(low.astype(f32), axis=0)
        return first

    first = lax.fori_loop(0, rows // strip, step, jnp.zeros((8, lanes), f32))
    sums[...] = jnp.sum(first, axis=0, keepdims=True)


def kernel_grad_kernel(edge_count, source, *refs):
    edges = refs[:edge_count]
    grad, out, wide_ref, sums_ref = refs[edge_count:]
    rows, columns = source.shape[0], source.shape[1]
    fill_extended(wide_ref, source, edges)
    sums_ref[...] = jnp.zeros_like(sums_ref)

    def step(index, carry):
        top = index * strip
        for start in range(0, columns, 8):
            upstream = grad[pl.ds(top, strip), start : start + 8, :].astype(f32)
            for column in range(7):
                window = wide_ref[pl.ds(top, strip + 6), start + 5 + column : start + 13 + column, :]
                for across in range(7):
                    sums_ref[7 * across + column] += jnp.sum(window[across : across + strip] * upstream, axis=0)
        return carry

    lax.fori_loop(0, rows // strip, step, 0)
    out[0, 0:49] = jnp.sum(sums_ref[...], axis=1)
    out[0, 49:56] = jnp.zeros((7, lanes), f32)


def by_channel(array):
    rest = array.shape[:-1]
    return pl.BlockSpec(rest + (lanes,), lambda tile: (0,) * len(rest) + (tile,))


def same_block(array):
    return pl.BlockSpec(array.shape, lambda tile: (0,) * array.ndim)


def wide_scratch(rows, columns):
    return pltpu.VMEM((rows + 6, columns + 16, lanes), f32)


def stencil_forward(source, edges, taps, sea):
    rows, columns, channels = source.shape
    sums = jax.ShapeDtypeStruct((2, channels), f32)
    mixed = jax.ShapeDtypeStruct(source.shape, f32)
    return pl.pallas_call(
        functools.partial(stencil_forward_kernel, len(edges)),
        grid=(pl.cdiv(channels, lanes),),
        in_specs=[by_channel(array) for array in (source, *edges, taps)] + [same_block(sea)],
        out_specs=[by_channel(mixed), by_channel(sums)],
        out_shape=[mixed, sums],
        scratch_shapes=[wide_scratch(rows, columns)],
        compiler_params=room,
        name="stencil_forward",
    )(source, *edges, taps, sea)


def stencil_backward(grad, edges, taps, sea, upstream):
    rows, columns, channels = grad.shape
    out = jax.ShapeDtypeStruct(grad.shape, bf16)
    sums = jax.ShapeDtypeStruct((1, channels), f32)
    return pl.pallas_call(
        functools.partial(stencil_backward_kernel, len(edges)),
        grid=(pl.cdiv(channels, lanes),),
        in_specs=[by_channel(array) for array in (grad, *edges, taps)] + [same_block(sea), by_channel(upstream)],
        out_specs=[by_channel(out), by_channel(sums)],
        out_shape=[out, sums],
        scratch_shapes=[wide_scratch(rows, columns)],
        compiler_params=room,
        name="stencil_backward",
    )(grad, *edges, taps, sea, upstream)


def kernel_grad(source, edges, grad):
    rows, columns, channels = source.shape
    tiles = pl.cdiv(channels, lanes)
    out = jax.ShapeDtypeStruct((tiles, 56, lanes), f32)
    return pl.pallas_call(
        functools.partial(kernel_grad_kernel, len(edges)),
        grid=(tiles,),
        in_specs=[by_channel(array) for array in (source, *edges, grad)],
        out_specs=pl.BlockSpec((1, 56, lanes), lambda tile: (tile, 0, 0)),
        out_shape=out,
        scratch_shapes=[wide_scratch(rows, columns), pltpu.VMEM((49, 8, lanes), f32)],
        compiler_params=room,
        name="kernel_grad",
    )(source, *edges, grad)


def chunks_of(width, size):
    edges = list(range(0, width, size))
    if len(edges) > 1 and width - edges[-1] < size // 2:
        edges.pop()
    return list(zip(edges, edges[1:] + [width]))


def spread(sea, channels):
    return jnp.concatenate([sea] * pl.cdiv(channels, lanes), axis=1)[:, :channels]


def gelu_pair(hidden):
    below = 0.5 + 0.5 * lax.erf(hidden * math.sqrt(0.5))
    density = jnp.exp(-0.5 * hidden * hidden) * (1.0 / math.sqrt(2.0 * math.pi))
    return hidden * below, below + hidden * density


def mlp_forward_kernel(
    size, mixed, source, sea, scales, up, up_bias, down, down_bias, out, active, slope, normed
):
    unit = (mixed[...] - scales[0:1]) * scales[1:2]
    low = (unit * scales[2:3] + scales[3:4]).astype(bf16)
    normed[...] = low
    branch = down_bias[...]
    for a, b in chunks_of(up.shape[1], size):
        hidden = jnp.dot(low, up[:, a:b], preferred_element_type=f32) + up_bias[:, a:b]
        value, rise = gelu_pair(hidden)
        value = value.astype(bf16)
        active[:, a:b] = value
        slope[:, a:b] = rise.astype(bf16)
        branch = branch + jnp.dot(value, down[a:b, :], preferred_element_type=f32)
    mask = spread(sea[...], out.shape[1])
    out[...] = (mask * (source[...].astype(f32) + branch)).astype(bf16)


def mlp_backward_kernel(
    size,
    upstream,
    mixed,
    slope,
    sea,
    scales,
    up,
    down,
    grad_branch,
    grad_hidden,
    grad_normed,
    sums,
    down_sums,
    up_sums,
):
    @pl.when(pl.program_id(0) == 0)
    def _():
        sums[...] = jnp.zeros_like(sums)
        down_sums[...] = jnp.zeros_like(down_sums)
        up_sums[...] = jnp.zeros_like(up_sums)

    mask = spread(sea[...], upstream.shape[1])
    low = (mask * upstream[...].astype(f32)).astype(bf16)
    grad_branch[...] = low
    down_sums[...] += jnp.sum(low.astype(f32), axis=0, keepdims=True)
    normed = None
    for a, b in chunks_of(up.shape[1], size):
        grad_active = lax.dot_general(low, down[a:b, :], (((1,), (1,)), ((), ())), preferred_element_type=f32)
        hidden = (grad_active * slope[:, a:b].astype(f32)).astype(bf16)
        grad_hidden[:, a:b] = hidden
        up_sums[:, a:b] += jnp.sum(hidden.astype(f32), axis=0, keepdims=True)
        part = lax.dot_general(hidden, up[:, a:b], (((1,), (1,)), ((), ())), preferred_element_type=f32)
        normed = part if normed is None else normed + part
    grad_normed[...] = normed
    unit = (mixed[...] - scales[0:1]) * scales[1:2]
    sums[0:1] += jnp.sum(normed, axis=0, keepdims=True)
    sums[1:2] += jnp.sum(normed * unit, axis=0, keepdims=True)


def tall(rows, width):
    return pl.BlockSpec((rows, width), lambda i: (i, 0))


def fixed(array):
    return pl.BlockSpec(array.shape, lambda i: (0, 0), pipeline_mode=pl.Buffered(1))


def mlp_forward(mixed, source, sea, scales, up, up_bias, down, down_bias):
    pixels, channels = mixed.shape
    wide = up.shape[1]
    rows = math.gcd(pixels, 384)
    return pl.pallas_call(
        functools.partial(mlp_forward_kernel, 512),
        grid=(pixels // rows,),
        in_specs=[tall(rows, channels), tall(rows, channels), tall(rows, lanes)]
        + [fixed(array) for array in (scales, up, up_bias, down, down_bias)],
        out_specs=[tall(rows, channels), tall(rows, wide), tall(rows, wide), tall(rows, channels)],
        out_shape=[jax.ShapeDtypeStruct((pixels, width), bf16) for width in (channels, wide, wide, channels)],
        compiler_params=room,
        name="mlp_forward",
    )(mixed, source, sea, scales, up, up_bias, down, down_bias)


def mlp_backward(upstream, mixed, slope, sea, scales, up, down):
    pixels, channels = mixed.shape
    wide = up.shape[1]
    rows = math.gcd(pixels, 384)
    sums = [jax.ShapeDtypeStruct(shape, f32) for shape in ((2, channels), (1, channels), (1, wide))]
    return pl.pallas_call(
        functools.partial(mlp_backward_kernel, 512),
        grid=(pixels // rows,),
        in_specs=[tall(rows, channels), tall(rows, channels), tall(rows, wide), tall(rows, lanes)]
        + [fixed(array) for array in (scales, up, down)],
        out_specs=[tall(rows, channels), tall(rows, wide), tall(rows, channels)]
        + [pl.BlockSpec(array.shape, lambda i: (0, 0)) for array in sums],
        out_shape=[
            jax.ShapeDtypeStruct((pixels, channels), bf16),
            jax.ShapeDtypeStruct((pixels, wide), bf16),
            jax.ShapeDtypeStruct((pixels, channels), f32),
        ]
        + sums,
        compiler_params=room,
        name="mlp_backward",
    )(upstream, mixed, slope, sea, scales, up, down)


def weight_grads_kernel(grad_branch, normed, active, grad_hidden, out, branch_ref, normed_ref):
    @pl.when(pl.program_id(0) == 0)
    def _():
        branch_ref[...] = grad_branch[...].T
        normed_ref[...] = normed[...].T

    up = jnp.dot(normed_ref[...], grad_hidden[...], preferred_element_type=f32).astype(bf16)
    down = jnp.dot(branch_ref[...], active[...], preferred_element_type=f32).astype(bf16)
    for part in range(out.shape[1]):
        out[0, part] = up[:, part * lanes : (part + 1) * lanes]
        out[1, part] = down[:, part * lanes : (part + 1) * lanes]


def weight_grads(grad_branch, normed, active, grad_hidden):
    pixels, channels = normed.shape
    hidden = active.shape[1]
    tiles = pl.cdiv(hidden, lanes)
    parts = next(count for count in (5, 4, 3, 2, 1) if count == 2 or tiles % count == 0)
    return pl.pallas_call(
        weight_grads_kernel,
        grid=(pl.cdiv(tiles, parts),),
        in_specs=[fixed(grad_branch), fixed(normed)]
        + [pl.BlockSpec((pixels, parts * lanes), lambda tile: (0, tile))] * 2,
        out_specs=pl.BlockSpec((2, parts, channels, lanes), lambda tile: (0, tile, 0, 0)),
        out_shape=jax.ShapeDtypeStruct((2, tiles, channels, lanes), bf16),
        scratch_shapes=[pltpu.VMEM((channels, pixels), bf16)] * 2,
        compiler_params=room,
        name="weight_grads",
    )(grad_branch, normed, active, grad_hidden)


def unpack_kernel(core, own, other, up, down):
    mine, theirs = own[...].astype(f32), other[...].astype(f32)
    first = core[0] == 0
    up[...] = jnp.where(first, mine, theirs)
    down[...] = jnp.where(first, theirs, mine)


def unpack(core, own, other, channels, hidden):
    block = pl.BlockSpec((channels, lanes), lambda tile, core: (tile, 0))
    return pl.pallas_call(
        unpack_kernel,
        grid_spec=pltpu.PrefetchScalarGridSpec(
            num_scalar_prefetch=1,
            grid=(pl.cdiv(hidden, lanes),),
            in_specs=[block, block],
            out_specs=[pl.BlockSpec((channels, lanes), lambda tile, core: (0, tile))] * 2,
        ),
        out_shape=[jax.ShapeDtypeStruct((channels, hidden), f32)] * 2,
        compiler_params=room,
        name="unpack",
    )(core, own, other)


def swap(array, axis, step):
    return lax.ppermute(array, axis, [(i, i ^ step) for i in range(lax.axis_size(axis))])


def take(stacked, index):
    return lax.dynamic_index_in_dim(stacked, index, 0, keepdims=False)


def exchange_add(stacked, axis, own, scale):
    count = stacked.shape[0]
    got = [swap(take(stacked, own ^ step), axis, scale * step) for step in range(1, count)]
    total = take(stacked, own).astype(f32)
    for piece in got:
        total = total + piece.astype(f32)
    return total.astype(bf16)


def exchange_all(piece, axis, own, scale, count):
    got = jnp.stack([piece] + [swap(piece, axis, scale * step) for step in range(1, count)])
    return jnp.concatenate([take(got, own ^ place) for place in range(count)], axis=0)


def sum_group(pair):
    tiles, columns = lax.axis_size("lat"), lax.axis_size("lon") // 2
    tile, place = lax.axis_index("lat"), lax.axis_index("lon")
    core, column = place % 2, place // 2
    rows = pair.shape[1]
    padded = -(-rows // (8 * tiles * columns)) * 8 * tiles * columns
    pair = jnp.pad(pair, ((0, 0), (0, padded - rows), (0, 0)))
    got = swap(take(pair, 1 - core), "lon", 1)
    half = (take(pair, core).astype(f32) + got.astype(f32)).astype(bf16)
    share = exchange_add(half.reshape(tiles, -1, lanes), "lat", tile, 1)
    share = exchange_add(share.reshape(columns, -1, lanes), "lon", column, 2)
    share = exchange_all(share, "lon", column, 2, columns)
    half = exchange_all(share, "lat", tile, 1, tiles)
    return half, swap(half, "lon", 1)


def sum_small(flat):
    count = lax.axis_size(both)
    rows = flat.shape[0]
    padded = -(-rows // (8 * count)) * 8 * count
    pieces = jnp.pad(flat, ((0, padded - rows), (0, 0))).reshape(count, -1, lanes)
    share = jnp.sum(lax.all_to_all(pieces, both, 0, 0, tiled=False), axis=0)
    copies = jnp.broadcast_to(share[None], pieces.shape)
    return lax.all_to_all(copies, both, 0, 0, tiled=False).reshape(padded, lanes)[:rows]


def cross_rows(former, latter):
    return lax.dot_general(former, latter, (((0,), (0,)), ((), ())), preferred_element_type=f32)


def by_transpose(former, latter):
    return lax.dot_general(former, latter, (((1,), (1,)), ((), ())), preferred_element_type=f32)


def block_forward(source, params, sea, ocean, dates):
    kernel, gain, shift, up, up_bias, down, down_bias = params
    height, breadth, channels = source.shape
    taps = kernel.astype(f32).reshape(49, channels)
    edges = borders(source, dates)
    mixed, local = stencil_forward(source, edges, taps, sea)
    first, square, ocean = sum_all(jnp.concatenate([local, jnp.broadcast_to(ocean, (1, channels))]))
    mean = first / ocean
    factor = lax.rsqrt(square / ocean - mean * mean + epsilon)
    scales = jnp.stack([mean, factor, gain.astype(f32), shift.astype(f32)])
    mixed = mixed.reshape(-1, channels)
    output, active, slope, normed = mlp_forward(
        mixed,
        source.reshape(-1, channels),
        sea.reshape(-1, lanes),
        scales,
        up,
        up_bias.astype(f32)[None],
        down,
        down_bias.astype(f32)[None],
    )
    return output, (source, edges, taps, mixed, scales, ocean, normed, slope, active)


def block_backward(upstream, params, sea, stored, dates):
    kernel, gain, shift, up, up_bias, down, down_bias = params
    source, edges, taps, mixed, scales, ocean, normed, slope, active = stored
    channels = source.shape[2]
    grad_branch, grad_hidden, grad_normed, local, down_sums, up_sums = mlp_backward(
        upstream, mixed, slope, sea.reshape(-1, lanes), scales, up, down
    )
    grad_shift, grad_gain = sum_all(local)
    mean, factor, gain = scales[0], scales[1], scales[2]
    unit = (mixed - mean) * factor
    weight = spread(sea.reshape(-1, lanes), channels) / ocean
    grad_mixed = factor * (gain * grad_normed - weight * (gain * grad_shift + unit * (gain * grad_gain)))
    grad_mixed = grad_mixed.astype(bf16).reshape(source.shape)
    grad_edges = borders(grad_mixed, dates)
    grad_kernel = kernel_grad(source, edges, grad_mixed)
    grad_source, source_sums = stencil_backward(grad_mixed, grad_edges, taps, sea, upstream.reshape(source.shape))
    return (
        grad_source.reshape(-1, channels),
        source_sums,
        (grad_gain, grad_shift, (grad_branch, normed, active, grad_hidden)),
        (grad_kernel, down_sums, up_sums),
    )


def shards(
    fine_map,
    ocean_mask,
    out_grad,
    encode_depth,
    encode_gain,
    encode_shift,
    encode_up,
    encode_up_bias,
    encode_down,
    encode_down_bias,
    widen_weight,
    widen_bias,
    bottle_depth,
    bottle_gain,
    bottle_shift,
    bottle_up,
    bottle_up_bias,
    bottle_down,
    bottle_down_bias,
    merge_weight,
    merge_bias,
    decode_depth,
    decode_gain,
    decode_shift,
    decode_up,
    decode_up_bias,
    decode_down,
    decode_down_bias,
):
    (encode_up, encode_down, widen_weight, bottle_up, bottle_down, merge_weight, decode_up, decode_down) = (
        lax.all_gather(weight, "lat", axis=0, tiled=True)
        for weight in (
            encode_up,
            encode_down,
            widen_weight,
            bottle_up,
            bottle_down,
            merge_weight,
            decode_up,
            decode_down,
        )
    )
    dates = fine_map.shape[0]
    fine = to_dates(fine_map)
    ocean_band = to_dates(ocean_mask).astype(f32)
    upstream = to_dates(out_grad)
    height, breadth, channels = fine.shape
    half_height, half_breadth = height // 2, breadth // 2
    wide = widen_weight.shape[1]
    coarse_band = jnp.max(ocean_band.reshape(half_height, 2, half_breadth, 2), axis=(1, 3))
    sea_fine = jnp.broadcast_to(ocean_band[..., None], (height, breadth, lanes))
    sea_coarse = jnp.broadcast_to(coarse_band[..., None], (half_height, half_breadth, lanes))
    encode = (encode_depth, encode_gain, encode_shift, encode_up, encode_up_bias, encode_down, encode_down_bias)
    bottle = (bottle_depth, bottle_gain, bottle_shift, bottle_up, bottle_up_bias, bottle_down, bottle_down_bias)
    decode = (decode_depth, decode_gain, decode_shift, decode_up, decode_up_bias, decode_down, decode_down_bias)
    merge_upper = merge_weight[:wide]
    merge_lower = merge_weight[wide:]
    ocean_fine = jnp.sum(ocean_band)
    ocean_coarse = jnp.sum(coarse_band)

    skip_rows, encode_stored = block_forward(fine, encode, sea_fine, ocean_fine, dates)
    blocks = skip_rows.reshape(half_height, 2, half_breadth, 2, channels).astype(f32)
    pooled = (jnp.sum(blocks, axis=(1, 3)) * 0.25).astype(bf16).reshape(-1, channels)
    coarse_in = jnp.dot(pooled, widen_weight, preferred_element_type=f32) + widen_bias.astype(f32)
    coarse_in = coarse_in.astype(bf16).reshape(half_height, half_breadth, wide)
    coarse_low, coarse_stored = block_forward(coarse_in, bottle, sea_coarse, ocean_coarse, dates)
    upper = jnp.dot(coarse_low, merge_upper, preferred_element_type=f32)
    upper = upper.reshape(half_height, 1, half_breadth, 1, channels)
    lower = jnp.dot(skip_rows, merge_lower, preferred_element_type=f32)
    lower = lower.reshape(half_height, 2, half_breadth, 2, channels)
    merged = (lower + upper).reshape(height, breadth, channels) + merge_bias.astype(f32)
    decode_rows, decode_stored = block_forward(merged.astype(bf16), decode, sea_fine, ocean_fine, dates)
    result = from_dates(decode_rows.reshape(fine.shape), dates)

    grad_merged, merge_sums, decode_grads, decode_small = block_backward(
        upstream.reshape(-1, channels), decode, sea_fine, decode_stored, dates
    )
    grad_block_sum = jnp.sum(
        grad_merged.astype(f32).reshape(half_height, 2, half_breadth, 2, channels), axis=(1, 3)
    ).reshape(-1, channels)
    grad_block_low = grad_block_sum.astype(bf16)
    grad_merge_upper = cross_rows(grad_block_low, coarse_low)
    grad_merge_lower = cross_rows(grad_merged, skip_rows)
    grad_coarse = by_transpose(grad_block_low, merge_upper)
    grad_skip_direct = by_transpose(grad_merged, merge_lower)
    grad_wide, widen_sums, bottle_grads, bottle_small = block_backward(
        grad_coarse, bottle, sea_coarse, coarse_stored, dates
    )
    early = [grad_merge_upper, grad_merge_lower]
    for grad_branch, normed, active, grad_hidden in (decode_grads[2], bottle_grads[2]):
        early += [cross_rows(normed, grad_hidden), cross_rows(grad_branch, active)]
    early = lax.psum([part.astype(bf16) for part in early], both)
    early = [total.astype(f32) for total in early]
    merge_sum = jnp.concatenate(early[:2], axis=1).T
    decode_up_sum, decode_down_sum, bottle_up_sum, bottle_down_sum = early[2], early[3].T, early[4], early[5].T
    core = (lax.axis_index("lon") % 2).astype(jnp.int32)[None]
    grad_widen = cross_rows(pooled, grad_wide).astype(bf16)
    widen_tiles = pl.cdiv(wide, 2 * lanes)
    grad_widen = jnp.pad(grad_widen, ((0, 0), (0, 2 * widen_tiles * lanes - wide)))
    grad_widen = grad_widen.reshape(channels, 2, widen_tiles, lanes).transpose(1, 2, 0, 3).reshape(2, -1, lanes)
    grad_pooled = by_transpose(grad_wide, widen_weight).reshape(half_height, 1, half_breadth, 1, channels) * 0.25
    grad_skip = grad_skip_direct.reshape(half_height, 2, half_breadth, 2, channels) + grad_pooled
    grad_fine, _, encode_grads, encode_small = block_backward(
        grad_skip.reshape(-1, channels), encode, sea_fine, encode_stored, dates
    )
    fine_grad = from_dates(grad_fine.reshape(fine.shape), dates)
    encode_pair = weight_grads(*encode_grads[2]).reshape(2, -1, lanes)
    own, other = sum_group(jnp.concatenate([encode_pair, grad_widen], axis=1))
    encode_up_sum, encode_down_sum = unpack(core, own, other, channels, encode_up.shape[1])
    encode_down_sum = encode_down_sum.T
    start = encode_pair.shape[1]
    lower = jnp.where(core == 0, own[start : start + grad_widen.shape[1]], other[start : start + grad_widen.shape[1]])
    upper = jnp.where(core == 0, other[start : start + grad_widen.shape[1]], own[start : start + grad_widen.shape[1]])
    widen_sum = jnp.stack([lower, upper]).reshape(2 * widen_tiles, channels, lanes).astype(f32)
    widen_sum = widen_sum.transpose(1, 0, 2).reshape(channels, -1)[:, :wide]

    kernels = [encode_small[0], bottle_small[0], decode_small[0]]
    rows = [encode_small[1:], (widen_sums,), bottle_small[1:], (merge_sums,), decode_small[1:]]
    rows = [row for group in rows for row in group]
    padded = [jnp.pad(row, ((0, 0), (0, -row.shape[1] % lanes))) for row in rows]
    line = jnp.concatenate(padded, axis=1)
    small = sum_small(jnp.concatenate([array.reshape(-1, lanes) for array in kernels] + [line.reshape(-1, lanes)]))
    kernel_sums, at = [], 0
    for array, shape in zip(kernels, (encode_depth.shape, bottle_depth.shape, decode_depth.shape)):
        count = array.shape[0] * 56
        total = small[at : at + count].reshape(array.shape)[:, :49].transpose(1, 0, 2).reshape(49, -1)
        kernel_sums.append(total[:, : shape[2]].reshape(shape))
        at += count
    line = small[at:].reshape(-1)
    row_sums, at = [], 0
    for row, wider in zip(rows, padded):
        row_sums.append(line[at : at + row.shape[1]])
        at += wider.shape[1]
    (encode_upb, encode_downb, widen_b, bottle_upb, bottle_downb, bottle_merge_b, decode_upb, decode_downb) = (
        row_sums[1],
        row_sums[0],
        row_sums[2],
        row_sums[4],
        row_sums[3],
        row_sums[5],
        row_sums[7],
        row_sums[6],
    )
    return (
        result,
        fine_grad,
        kernel_sums[0],
        encode_grads[0],
        encode_grads[1],
        encode_up_sum,
        encode_upb,
        encode_down_sum,
        encode_downb,
        widen_sum,
        widen_b,
        kernel_sums[1],
        bottle_grads[0],
        bottle_grads[1],
        bottle_up_sum,
        bottle_upb,
        bottle_down_sum,
        bottle_downb,
        merge_sum,
        bottle_merge_b,
        kernel_sums[2],
        decode_grads[0],
        decode_grads[1],
        decode_up_sum,
        decode_upb,
        decode_down_sum,
        decode_downb,
    )


def solution(mesh):
    whole = P()
    rows = P("lat", None)
    tile = P(None, "lat", "lon", None)
    block = (whole, whole, whole, rows, whole, rows, whole)
    placed = (tile, P(None, "lat", "lon"), tile) + block + (rows, whole) + block + (rows, whole) + block
    return jax.shard_map(
        shards,
        mesh=mesh,
        in_specs=placed,
        out_specs=(tile, tile) + (whole,) * 25,
        check_vma=False,
    )
```

```python
import functools
import math

import jax
import jax.numpy as jnp
from jax import lax
from jax.experimental import pallas as pl
from jax.experimental.pallas import tpu as pltpu
from jax.sharding import PartitionSpec as P

epsilon = 1e-05
both = ("lat", "lon")
bf16 = jnp.bfloat16
f32 = jnp.float32
lanes = 128
strip = 12
room = pltpu.CompilerParams(vmem_limit_bytes=56 << 20)


def exchange_pairs(count, group, step):
    return [(i, (i // group) * group + ((i % group) ^ step)) for i in range(count)]


def to_dates(tiles):
    dates, count = tiles.shape[0], lax.axis_size("lat")
    own = lax.axis_index("lat") % dates
    pieces = [lax.dynamic_index_in_dim(tiles, own, 0, keepdims=False)]
    for step in range(1, dates):
        pieces.append(
            lax.ppermute(
                lax.dynamic_index_in_dim(tiles, own ^ step, 0, keepdims=False),
                "lat",
                exchange_pairs(count, dates, step),
            )
        )
    stacked = jnp.stack(pieces)
    ordered = [lax.dynamic_index_in_dim(stacked, own ^ tile, 0, keepdims=False) for tile in range(dates)]
    return jnp.concatenate(ordered, axis=0)


def from_dates(band, dates):
    count = lax.axis_size("lat")
    own = lax.axis_index("lat") % dates
    tiles = band.reshape((dates, band.shape[0] // dates) + band.shape[1:])
    pieces = [lax.dynamic_index_in_dim(tiles, own, 0, keepdims=False)]
    for step in range(1, dates):
        pieces.append(
            lax.ppermute(
                lax.dynamic_index_in_dim(tiles, own ^ step, 0, keepdims=False),
                "lat",
                exchange_pairs(count, dates, step),
            )
        )
    stacked = jnp.stack(pieces)
    return jnp.stack([lax.dynamic_index_in_dim(stacked, own ^ date, 0, keepdims=False) for date in range(dates)])


def after(array, event):
    return lax.optimization_barrier((array, event))[0]


def gathered(shard):
    return exchange_all(shard, "lat", lax.axis_index("lat"), 1, lax.axis_size("lat"))


def both_halves(half):
    other = swap(half, "lon", 1)
    first = lax.axis_index("lon") % 2 == 0
    return jnp.where(first, half, other), jnp.where(first, other, half)


def gathered_by_columns(shard):
    columns = shard.shape[1]
    start = columns // 2 // lanes * lanes
    width = columns - start
    core = lax.axis_index("lon") % 2
    half = lax.dynamic_slice_in_dim(shard, core * start, width, axis=1)
    low, high = both_halves(lax.all_gather(half, "lat", axis=0, tiled=True))
    return jnp.concatenate([low[:, :start], high], axis=1)


def gathered_by_rows(shard):
    rows, columns = shard.shape
    core = lax.axis_index("lon") % 2
    half = lax.dynamic_slice_in_dim(shard, core * (rows // 2), rows // 2, axis=0)
    low, high = both_halves(lax.all_gather(half, "lat", axis=0, tiled=True))
    pieces = [piece.reshape(-1, 1, rows // 2, columns) for piece in (low, high)]
    return jnp.concatenate(pieces, axis=1).reshape(-1, columns)


def borders(source, dates):
    count = lax.axis_size("lon")
    forward = [(i, (i + 1) % count) for i in range(count)]
    backward = [(target, origin) for origin, target in forward]
    left = lax.ppermute(source[:, -3:], "lon", forward)
    right = lax.ppermute(source[:, :3], "lon", backward)
    tiles = lax.axis_size("lat")
    if tiles == dates:
        return left, right
    down = [(i, i + dates) for i in range(tiles - dates)]
    up = [(target, origin) for origin, target in down]
    last = jnp.concatenate([left[-3:], source[-3:], right[-3:]], axis=1)
    first = jnp.concatenate([left[:3], source[:3], right[:3]], axis=1)
    return left, right, lax.ppermute(last, "lat", down), lax.ppermute(first, "lat", up)


def sum_all(local):
    count = lax.axis_size(both)
    copies = jnp.broadcast_to(local[None], (count,) + local.shape)
    return jnp.sum(lax.all_to_all(copies, both, 0, 0, tiled=False), axis=0)


def fill_extended(wide_ref, centre, edges):
    rows, columns = centre.shape[0], centre.shape[1]
    blank = jnp.zeros((3, columns + 16, lanes), f32)
    wide_ref[0:3] = blank
    wide_ref[rows + 3 :] = blank
    wide_ref[3 : rows + 3, 8 : columns + 8] = centre[...].astype(f32)
    wide_ref[3 : rows + 3, 5:8] = edges[0][...].astype(f32)
    wide_ref[3 : rows + 3, columns + 8 : columns + 11] = edges[1][...].astype(f32)
    if len(edges) > 2:
        wide_ref[0:3, 5 : columns + 11] = edges[2][...].astype(f32)
        wide_ref[rows + 3 :, 5 : columns + 11] = edges[3][...].astype(f32)


def strip_sum(wide_ref, taps, top, start, flipped):
    total = None
    for column in range(7):
        window = wide_ref[pl.ds(top, strip + 6), start + 5 + column : start + 13 + column, :]
        for across in range(7):
            place = 7 * across + column
            tap = taps[pl.ds(48 - place if flipped else place, 8, stride=0), :]
            term = window[across : across + strip] * tap[None]
            total = term if total is None else total + term
    return total


def stencil_forward_kernel(edge_count, source, *refs):
    edges = refs[:edge_count]
    taps, sea, mixed, sums, wide_ref = refs[edge_count:]
    rows, columns = source.shape[0], source.shape[1]
    fill_extended(wide_ref, source, edges)

    def step(index, carry):
        first, square = carry
        top = index * strip
        for start in range(0, columns, 8):
            here = (pl.ds(top, strip), slice(start, start + 8))
            total = strip_sum(wide_ref, taps, top, start, False)
            mixed[here] = total
            masked = total * sea[here]
            first = first + jnp.sum(masked, axis=0)
            square = square + jnp.sum(masked * total, axis=0)
        return first, square

    zero = jnp.zeros((8, lanes), f32)
    first, square = lax.fori_loop(0, rows // strip, step, (zero, zero))
    sums[0:1] = jnp.sum(first, axis=0, keepdims=True)
    sums[1:2] = jnp.sum(square, axis=0, keepdims=True)


def stencil_backward_kernel(edge_count, grad, *refs):
    edges = refs[:edge_count]
    taps, sea, upstream, out, sums, wide_ref = refs[edge_count:]
    rows, columns = grad.shape[0], grad.shape[1]
    fill_extended(wide_ref, grad, edges)

    def step(index, first):
        top = index * strip
        for start in range(0, columns, 8):
            here = (pl.ds(top, strip), slice(start, start + 8))
            total = strip_sum(wide_ref, taps, top, start, True)
            low = (total + upstream[here].astype(f32) * sea[here]).astype(bf16)
            out[here] = low
            first = first + jnp.sum(low.astype(f32), axis=0)
        return first

    first = lax.fori_loop(0, rows // strip, step, jnp.zeros((8, lanes), f32))
    sums[...] = jnp.sum(first, axis=0, keepdims=True)


def kernel_grad_kernel(edge_count, source, *refs):
    edges = refs[:edge_count]
    grad, out, wide_ref, sums_ref = refs[edge_count:]
    rows, columns = source.shape[0], source.shape[1]
    fill_extended(wide_ref, source, edges)
    sums_ref[...] = jnp.zeros_like(sums_ref)

    def step(index, carry):
        top = index * strip
        for start in range(0, columns, 8):
            upstream = grad[pl.ds(top, strip), start : start + 8, :].astype(f32)
            for column in range(7):
                window = wide_ref[pl.ds(top, strip + 6), start + 5 + column : start + 13 + column, :]
                for across in range(7):
                    sums_ref[7 * across + column] += jnp.sum(window[across : across + strip] * upstream, axis=0)
        return carry

    lax.fori_loop(0, rows // strip, step, 0)
    out[0, 0:49] = jnp.sum(sums_ref[...], axis=1)
    out[0, 49:56] = jnp.zeros((7, lanes), f32)


def by_channel(array):
    rest = array.shape[:-1]
    return pl.BlockSpec(rest + (lanes,), lambda tile: (0,) * len(rest) + (tile,))


def same_block(array):
    return pl.BlockSpec(array.shape, lambda tile: (0,) * array.ndim)


def wide_scratch(rows, columns):
    return pltpu.VMEM((rows + 6, columns + 16, lanes), f32)


def stencil_forward(source, edges, taps, sea):
    rows, columns, channels = source.shape
    sums = jax.ShapeDtypeStruct((2, channels), f32)
    mixed = jax.ShapeDtypeStruct(source.shape, f32)
    return pl.pallas_call(
        functools.partial(stencil_forward_kernel, len(edges)),
        grid=(pl.cdiv(channels, lanes),),
        in_specs=[by_channel(array) for array in (source, *edges, taps)] + [same_block(sea)],
        out_specs=[by_channel(mixed), by_channel(sums)],
        out_shape=[mixed, sums],
        scratch_shapes=[wide_scratch(rows, columns)],
        compiler_params=room,
        name="stencil_forward",
    )(source, *edges, taps, sea)


def stencil_backward(grad, edges, taps, sea, upstream):
    rows, columns, channels = grad.shape
    out = jax.ShapeDtypeStruct(grad.shape, bf16)
    sums = jax.ShapeDtypeStruct((1, channels), f32)
    return pl.pallas_call(
        functools.partial(stencil_backward_kernel, len(edges)),
        grid=(pl.cdiv(channels, lanes),),
        in_specs=[by_channel(array) for array in (grad, *edges, taps)] + [same_block(sea), by_channel(upstream)],
        out_specs=[by_channel(out), by_channel(sums)],
        out_shape=[out, sums],
        scratch_shapes=[wide_scratch(rows, columns)],
        compiler_params=room,
        name="stencil_backward",
    )(grad, *edges, taps, sea, upstream)


def kernel_grad(source, edges, grad):
    rows, columns, channels = source.shape
    tiles = pl.cdiv(channels, lanes)
    out = jax.ShapeDtypeStruct((tiles, 56, lanes), f32)
    return pl.pallas_call(
        functools.partial(kernel_grad_kernel, len(edges)),
        grid=(tiles,),
        in_specs=[by_channel(array) for array in (source, *edges, grad)],
        out_specs=pl.BlockSpec((1, 56, lanes), lambda tile: (tile, 0, 0)),
        out_shape=out,
        scratch_shapes=[wide_scratch(rows, columns), pltpu.VMEM((49, 8, lanes), f32)],
        compiler_params=room,
        name="kernel_grad",
    )(source, *edges, grad)


def chunks_of(width, size):
    edges = list(range(0, width, size))
    if len(edges) > 1 and width - edges[-1] < size // 2:
        edges.pop()
    return list(zip(edges, edges[1:] + [width]))


def spread(sea, channels):
    return jnp.concatenate([sea] * pl.cdiv(channels, lanes), axis=1)[:, :channels]


def gelu_pair(hidden):
    below = 0.5 + 0.5 * lax.erf(hidden * math.sqrt(0.5))
    density = jnp.exp(-0.5 * hidden * hidden) * (1.0 / math.sqrt(2.0 * math.pi))
    return hidden * below, below + hidden * density


def mlp_forward_kernel(
    size, mixed, source, sea, scales, up, up_bias, down, down_bias, out, active, slope, normed
):
    unit = (mixed[...] - scales[0:1]) * scales[1:2]
    low = (unit * scales[2:3] + scales[3:4]).astype(bf16)
    normed[...] = low
    branch = down_bias[...]
    for a, b in chunks_of(up.shape[1], size):
        hidden = jnp.dot(low, up[:, a:b], preferred_element_type=f32) + up_bias[:, a:b]
        value, rise = gelu_pair(hidden)
        value = value.astype(bf16)
        active[:, a:b] = value
        slope[:, a:b] = rise.astype(bf16)
        branch = branch + jnp.dot(value, down[a:b, :], preferred_element_type=f32)
    mask = spread(sea[...], out.shape[1])
    out[...] = (mask * (source[...].astype(f32) + branch)).astype(bf16)


def mlp_backward_kernel(
    size,
    upstream,
    mixed,
    slope,
    sea,
    scales,
    up,
    down,
    grad_branch,
    grad_hidden,
    grad_normed,
    sums,
    down_sums,
    up_sums,
):
    @pl.when(pl.program_id(0) == 0)
    def _():
        sums[...] = jnp.zeros_like(sums)
        down_sums[...] = jnp.zeros_like(down_sums)
        up_sums[...] = jnp.zeros_like(up_sums)

    mask = spread(sea[...], upstream.shape[1])
    low = (mask * upstream[...].astype(f32)).astype(bf16)
    grad_branch[...] = low
    down_sums[...] += jnp.sum(low.astype(f32), axis=0, keepdims=True)
    normed = None
    for a, b in chunks_of(up.shape[1], size):
        grad_active = lax.dot_general(low, down[a:b, :], (((1,), (1,)), ((), ())), preferred_element_type=f32)
        hidden = (grad_active * slope[:, a:b].astype(f32)).astype(bf16)
        grad_hidden[:, a:b] = hidden
        up_sums[:, a:b] += jnp.sum(hidden.astype(f32), axis=0, keepdims=True)
        part = lax.dot_general(hidden, up[:, a:b], (((1,), (1,)), ((), ())), preferred_element_type=f32)
        normed = part if normed is None else normed + part
    grad_normed[...] = normed
    unit = (mixed[...] - scales[0:1]) * scales[1:2]
    sums[0:1] += jnp.sum(normed, axis=0, keepdims=True)
    sums[1:2] += jnp.sum(normed * unit, axis=0, keepdims=True)


def tall(rows, width):
    return pl.BlockSpec((rows, width), lambda i: (i, 0))


def fixed(array):
    return pl.BlockSpec(array.shape, lambda i: (0, 0), pipeline_mode=pl.Buffered(1))


def mlp_forward(mixed, source, sea, scales, up, up_bias, down, down_bias):
    pixels, channels = mixed.shape
    wide = up.shape[1]
    rows = math.gcd(pixels, 384)
    return pl.pallas_call(
        functools.partial(mlp_forward_kernel, 512),
        grid=(pixels // rows,),
        in_specs=[tall(rows, channels), tall(rows, channels), tall(rows, lanes)]
        + [fixed(array) for array in (scales, up, up_bias, down, down_bias)],
        out_specs=[tall(rows, channels), tall(rows, wide), tall(rows, wide), tall(rows, channels)],
        out_shape=[jax.ShapeDtypeStruct((pixels, width), bf16) for width in (channels, wide, wide, channels)],
        compiler_params=room,
        name="mlp_forward",
    )(mixed, source, sea, scales, up, up_bias, down, down_bias)


def mlp_backward(upstream, mixed, slope, sea, scales, up, down):
    pixels, channels = mixed.shape
    wide = up.shape[1]
    rows = math.gcd(pixels, 384)
    sums = [jax.ShapeDtypeStruct(shape, f32) for shape in ((2, channels), (1, channels), (1, wide))]
    return pl.pallas_call(
        functools.partial(mlp_backward_kernel, 512),
        grid=(pixels // rows,),
        in_specs=[tall(rows, channels), tall(rows, channels), tall(rows, wide), tall(rows, lanes)]
        + [fixed(array) for array in (scales, up, down)],
        out_specs=[tall(rows, channels), tall(rows, wide), tall(rows, channels)]
        + [pl.BlockSpec(array.shape, lambda i: (0, 0)) for array in sums],
        out_shape=[
            jax.ShapeDtypeStruct((pixels, channels), bf16),
            jax.ShapeDtypeStruct((pixels, wide), bf16),
            jax.ShapeDtypeStruct((pixels, channels), f32),
        ]
        + sums,
        compiler_params=room,
        name="mlp_backward",
    )(upstream, mixed, slope, sea, scales, up, down)


def weight_grads_kernel(grad_branch, normed, active, grad_hidden, out, branch_ref, normed_ref):
    @pl.when(pl.program_id(0) == 0)
    def _():
        branch_ref[...] = grad_branch[...].T
        normed_ref[...] = normed[...].T

    up = jnp.dot(normed_ref[...], grad_hidden[...], preferred_element_type=f32).astype(bf16)
    down = jnp.dot(branch_ref[...], active[...], preferred_element_type=f32).astype(bf16)
    for part in range(out.shape[1]):
        out[0, part] = up[:, part * lanes : (part + 1) * lanes]
        out[1, part] = down[:, part * lanes : (part + 1) * lanes]


def weight_grads(grad_branch, normed, active, grad_hidden):
    pixels, channels = normed.shape
    hidden = active.shape[1]
    tiles = pl.cdiv(hidden, lanes)
    parts = next(count for count in (5, 4, 3, 2, 1) if count == 2 or tiles % count == 0)
    return pl.pallas_call(
        weight_grads_kernel,
        grid=(pl.cdiv(tiles, parts),),
        in_specs=[fixed(grad_branch), fixed(normed)]
        + [pl.BlockSpec((pixels, parts * lanes), lambda tile: (0, tile))] * 2,
        out_specs=pl.BlockSpec((2, parts, channels, lanes), lambda tile: (0, tile, 0, 0)),
        out_shape=jax.ShapeDtypeStruct((2, tiles, channels, lanes), bf16),
        scratch_shapes=[pltpu.VMEM((channels, pixels), bf16)] * 2,
        compiler_params=room,
        name="weight_grads",
    )(grad_branch, normed, active, grad_hidden)


def unpack_kernel(core, own, other, up, down):
    mine, theirs = own[...].astype(f32), other[...].astype(f32)
    first = core[0] == 0
    up[...] = jnp.where(first, mine, theirs)
    down[...] = jnp.where(first, theirs, mine)


def unpack(core, own, other, channels, hidden):
    block = pl.BlockSpec((channels, lanes), lambda tile, core: (tile, 0))
    return pl.pallas_call(
        unpack_kernel,
        grid_spec=pltpu.PrefetchScalarGridSpec(
            num_scalar_prefetch=1,
            grid=(pl.cdiv(hidden, lanes),),
            in_specs=[block, block],
            out_specs=[pl.BlockSpec((channels, lanes), lambda tile, core: (0, tile))] * 2,
        ),
        out_shape=[jax.ShapeDtypeStruct((channels, hidden), f32)] * 2,
        compiler_params=room,
        name="unpack",
    )(core, own, other)


def swap(array, axis, step):
    return lax.ppermute(array, axis, [(i, i ^ step) for i in range(lax.axis_size(axis))])


def take(stacked, index):
    return lax.dynamic_index_in_dim(stacked, index, 0, keepdims=False)


def exchange_add(stacked, axis, own, scale):
    count = stacked.shape[0]
    got = [swap(take(stacked, own ^ step), axis, scale * step) for step in range(1, count)]
    total = take(stacked, own).astype(f32)
    for piece in got:
        total = total + piece.astype(f32)
    return total.astype(bf16)


def exchange_all(piece, axis, own, scale, count):
    got = jnp.stack([piece] + [swap(piece, axis, scale * step) for step in range(1, count)])
    return jnp.concatenate([take(got, own ^ place) for place in range(count)], axis=0)


def sum_group(pair):
    tiles, columns = lax.axis_size("lat"), lax.axis_size("lon") // 2
    tile, place = lax.axis_index("lat"), lax.axis_index("lon")
    core, column = place % 2, place // 2
    rows = pair.shape[1]
    padded = -(-rows // (8 * tiles * columns)) * 8 * tiles * columns
    pair = jnp.pad(pair, ((0, 0), (0, padded - rows), (0, 0)))
    got = swap(take(pair, 1 - core), "lon", 1)
    half = (take(pair, core).astype(f32) + got.astype(f32)).astype(bf16)
    share = exchange_add(half.reshape(tiles, -1, lanes), "lat", tile, 1)
    share = exchange_add(share.reshape(columns, -1, lanes), "lon", column, 2)
    share = exchange_all(share, "lon", column, 2, columns)
    half = exchange_all(share, "lat", tile, 1, tiles)
    return half, swap(half, "lon", 1)


def sum_small(flat):
    count = lax.axis_size(both)
    rows = flat.shape[0]
    padded = -(-rows // (8 * count)) * 8 * count
    pieces = jnp.pad(flat, ((0, padded - rows), (0, 0))).reshape(count, -1, lanes)
    share = jnp.sum(lax.all_to_all(pieces, both, 0, 0, tiled=False), axis=0)
    copies = jnp.broadcast_to(share[None], pieces.shape)
    return lax.all_to_all(copies, both, 0, 0, tiled=False).reshape(padded, lanes)[:rows]


def cross_rows(former, latter):
    return lax.dot_general(former, latter, (((0,), (0,)), ((), ())), preferred_element_type=f32)


def by_transpose(former, latter):
    return lax.dot_general(former, latter, (((1,), (1,)), ((), ())), preferred_element_type=f32)


def block_forward(source, params, sea, ocean, dates):
    kernel, gain, shift, up, up_bias, down, down_bias = params
    height, breadth, channels = source.shape
    taps = kernel.astype(f32).reshape(49, channels)
    edges = borders(source, dates)
    mixed, local = stencil_forward(source, edges, taps, sea)
    first, square, ocean = sum_all(jnp.concatenate([local, jnp.broadcast_to(ocean, (1, channels))]))
    mean = first / ocean
    factor = lax.rsqrt(square / ocean - mean * mean + epsilon)
    scales = jnp.stack([mean, factor, gain.astype(f32), shift.astype(f32)])
    mixed = mixed.reshape(-1, channels)
    output, active, slope, normed = mlp_forward(
        mixed,
        source.reshape(-1, channels),
        sea.reshape(-1, lanes),
        scales,
        up,
        up_bias.astype(f32)[None],
        down,
        down_bias.astype(f32)[None],
    )
    return output, (source, edges, taps, mixed, scales, ocean, normed, slope, active)


def block_backward(upstream, params, sea, stored, dates):
    kernel, gain, shift, up, up_bias, down, down_bias = params
    source, edges, taps, mixed, scales, ocean, normed, slope, active = stored
    channels = source.shape[2]
    grad_branch, grad_hidden, grad_normed, local, down_sums, up_sums = mlp_backward(
        upstream, mixed, slope, sea.reshape(-1, lanes), scales, up, down
    )
    grad_shift, grad_gain = sum_all(local)
    mean, factor, gain = scales[0], scales[1], scales[2]
    unit = (mixed - mean) * factor
    weight = spread(sea.reshape(-1, lanes), channels) / ocean
    grad_mixed = factor * (gain * grad_normed - weight * (gain * grad_shift + unit * (gain * grad_gain)))
    grad_mixed = grad_mixed.astype(bf16).reshape(source.shape)
    grad_edges = borders(grad_mixed, dates)
    grad_kernel = kernel_grad(source, edges, grad_mixed)
    grad_source, source_sums = stencil_backward(grad_mixed, grad_edges, taps, sea, upstream.reshape(source.shape))
    return (
        grad_source.reshape(-1, channels),
        source_sums,
        (grad_gain, grad_shift, (grad_branch, normed, active, grad_hidden)),
        (grad_kernel, down_sums, up_sums),
    )


def shards(
    fine_map,
    ocean_mask,
    out_grad,
    encode_depth,
    encode_gain,
    encode_shift,
    encode_up,
    encode_up_bias,
    encode_down,
    encode_down_bias,
    widen_weight,
    widen_bias,
    bottle_depth,
    bottle_gain,
    bottle_shift,
    bottle_up,
    bottle_up_bias,
    bottle_down,
    bottle_down_bias,
    merge_weight,
    merge_bias,
    decode_depth,
    decode_gain,
    decode_shift,
    decode_up,
    decode_up_bias,
    decode_down,
    decode_down_bias,
):
    dates = fine_map.shape[0]
    fine = to_dates(fine_map)
    encode_up, encode_down = (gathered(after(weight, fine)) for weight in (encode_up, encode_down))
    bottle_up, bottle_down = gathered_by_columns(bottle_up), gathered_by_rows(bottle_down)
    decode_up = lax.all_gather(decode_up, "lat", axis=0, tiled=True)
    decode_down = lax.all_gather(decode_down, "lat", axis=0, tiled=True)
    ocean_band = to_dates(after(ocean_mask, fine)).astype(f32)
    height, breadth, channels = fine.shape
    half_height, half_breadth = height // 2, breadth // 2
    wide = bottle_depth.shape[2]
    coarse_band = jnp.max(ocean_band.reshape(half_height, 2, half_breadth, 2), axis=(1, 3))
    sea_fine = jnp.broadcast_to(ocean_band[..., None], (height, breadth, lanes))
    sea_coarse = jnp.broadcast_to(coarse_band[..., None], (half_height, half_breadth, lanes))
    encode = (encode_depth, encode_gain, encode_shift, encode_up, encode_up_bias, encode_down, encode_down_bias)
    bottle = (bottle_depth, bottle_gain, bottle_shift, bottle_up, bottle_up_bias, bottle_down, bottle_down_bias)
    decode = (decode_depth, decode_gain, decode_shift, decode_up, decode_up_bias, decode_down, decode_down_bias)
    ocean_fine = jnp.sum(ocean_band)
    ocean_coarse = jnp.sum(coarse_band)

    skip_rows, encode_stored = block_forward(fine, encode, sea_fine, ocean_fine, dates)
    widen_weight = gathered(after(widen_weight, encode_stored[3]))
    blocks = skip_rows.reshape(half_height, 2, half_breadth, 2, channels).astype(f32)
    pooled = (jnp.sum(blocks, axis=(1, 3)) * 0.25).astype(bf16).reshape(-1, channels)
    coarse_in = jnp.dot(pooled, widen_weight, preferred_element_type=f32) + widen_bias.astype(f32)
    coarse_in = coarse_in.astype(bf16).reshape(half_height, half_breadth, wide)
    coarse_low, coarse_stored = block_forward(coarse_in, bottle, sea_coarse, ocean_coarse, dates)
    merge_weight = gathered(after(merge_weight, coarse_stored[3]))
    merge_upper = merge_weight[:wide]
    merge_lower = merge_weight[wide:]
    upstream = to_dates(after(out_grad, coarse_stored[3]))
    upper = jnp.dot(coarse_low, merge_upper, preferred_element_type=f32)
    upper = upper.reshape(half_height, 1, half_breadth, 1, channels)
    lower = jnp.dot(skip_rows, merge_lower, preferred_element_type=f32)
    lower = lower.reshape(half_height, 2, half_breadth, 2, channels)
    merged = (lower + upper).reshape(height, breadth, channels) + merge_bias.astype(f32)
    decode_rows, decode_stored = block_forward(merged.astype(bf16), decode, sea_fine, ocean_fine, dates)
    result = from_dates(decode_rows.reshape(fine.shape), dates)

    grad_merged, merge_sums, decode_grads, decode_small = block_backward(
        upstream.reshape(-1, channels), decode, sea_fine, decode_stored, dates
    )
    grad_block_sum = jnp.sum(
        grad_merged.astype(f32).reshape(half_height, 2, half_breadth, 2, channels), axis=(1, 3)
    ).reshape(-1, channels)
    grad_block_low = grad_block_sum.astype(bf16)
    grad_merge_upper = cross_rows(grad_block_low, coarse_low)
    grad_merge_lower = cross_rows(grad_merged, skip_rows)
    grad_coarse = by_transpose(grad_block_low, merge_upper)
    grad_skip_direct = by_transpose(grad_merged, merge_lower)
    grad_wide, widen_sums, bottle_grads, bottle_small = block_backward(
        grad_coarse, bottle, sea_coarse, coarse_stored, dates
    )
    early = [grad_merge_upper, grad_merge_lower]
    for grad_branch, normed, active, grad_hidden in (decode_grads[2], bottle_grads[2]):
        early += [cross_rows(normed, grad_hidden), cross_rows(grad_branch, active)]
    early = lax.psum([part.astype(bf16) for part in early], both)
    early = [total.astype(f32) for total in early]
    merge_sum = jnp.concatenate(early[:2], axis=1).T
    decode_up_sum, decode_down_sum, bottle_up_sum, bottle_down_sum = early[2], early[3].T, early[4], early[5].T
    core = (lax.axis_index("lon") % 2).astype(jnp.int32)[None]
    grad_widen = cross_rows(pooled, grad_wide).astype(bf16)
    widen_tiles = pl.cdiv(wide, 2 * lanes)
    grad_widen = jnp.pad(grad_widen, ((0, 0), (0, 2 * widen_tiles * lanes - wide)))
    grad_widen = grad_widen.reshape(channels, 2, widen_tiles, lanes).transpose(1, 2, 0, 3).reshape(2, -1, lanes)
    grad_pooled = by_transpose(grad_wide, widen_weight).reshape(half_height, 1, half_breadth, 1, channels) * 0.25
    grad_skip = grad_skip_direct.reshape(half_height, 2, half_breadth, 2, channels) + grad_pooled
    grad_fine, _, encode_grads, encode_small = block_backward(
        grad_skip.reshape(-1, channels), encode, sea_fine, encode_stored, dates
    )
    fine_grad = from_dates(grad_fine.reshape(fine.shape), dates)
    encode_pair = weight_grads(*encode_grads[2]).reshape(2, -1, lanes)
    own, other = sum_group(jnp.concatenate([encode_pair, grad_widen], axis=1))
    encode_up_sum, encode_down_sum = unpack(core, own, other, channels, encode_up.shape[1])
    encode_down_sum = encode_down_sum.T
    start = encode_pair.shape[1]
    lower = jnp.where(core == 0, own[start : start + grad_widen.shape[1]], other[start : start + grad_widen.shape[1]])
    upper = jnp.where(core == 0, other[start : start + grad_widen.shape[1]], own[start : start + grad_widen.shape[1]])
    widen_sum = jnp.stack([lower, upper]).reshape(2 * widen_tiles, channels, lanes).astype(f32)
    widen_sum = widen_sum.transpose(1, 0, 2).reshape(channels, -1)[:, :wide]

    kernels = [encode_small[0], bottle_small[0], decode_small[0]]
    rows = [encode_small[1:], (widen_sums,), bottle_small[1:], (merge_sums,), decode_small[1:]]
    rows = [row for group in rows for row in group]
    padded = [jnp.pad(row, ((0, 0), (0, -row.shape[1] % lanes))) for row in rows]
    line = jnp.concatenate(padded, axis=1)
    small = sum_small(jnp.concatenate([array.reshape(-1, lanes) for array in kernels] + [line.reshape(-1, lanes)]))
    kernel_sums, at = [], 0
    for array, shape in zip(kernels, (encode_depth.shape, bottle_depth.shape, decode_depth.shape)):
        count = array.shape[0] * 56
        total = small[at : at + count].reshape(array.shape)[:, :49].transpose(1, 0, 2).reshape(49, -1)
        kernel_sums.append(total[:, : shape[2]].reshape(shape))
        at += count
    line = small[at:].reshape(-1)
    row_sums, at = [], 0
    for row, wider in zip(rows, padded):
        row_sums.append(line[at : at + row.shape[1]])
        at += wider.shape[1]
    (encode_upb, encode_downb, widen_b, bottle_upb, bottle_downb, bottle_merge_b, decode_upb, decode_downb) = (
        row_sums[1],
        row_sums[0],
        row_sums[2],
        row_sums[4],
        row_sums[3],
        row_sums[5],
        row_sums[7],
        row_sums[6],
    )
    return (
        result,
        fine_grad,
        kernel_sums[0],
        encode_grads[0],
        encode_grads[1],
        encode_up_sum,
        encode_upb,
        encode_down_sum,
        encode_downb,
        widen_sum,
        widen_b,
        kernel_sums[1],
        bottle_grads[0],
        bottle_grads[1],
        bottle_up_sum,
        bottle_upb,
        bottle_down_sum,
        bottle_downb,
        merge_sum,
        bottle_merge_b,
        kernel_sums[2],
        decode_grads[0],
        decode_grads[1],
        decode_up_sum,
        decode_upb,
        decode_down_sum,
        decode_downb,
    )


def solution(mesh):
    whole = P()
    rows = P("lat", None)
    tile = P(None, "lat", "lon", None)
    block = (whole, whole, whole, rows, whole, rows, whole)
    placed = (tile, P(None, "lat", "lon"), tile) + block + (rows, whole) + block + (rows, whole) + block
    return jax.shard_map(
        shards,
        mesh=mesh,
        in_specs=placed,
        out_specs=(tile, tile) + (whole,) * 25,
        check_vma=False,
    )
```

```python
import functools
import math

import jax
import jax.numpy as jnp
import numpy as np
from jax import lax
from jax.experimental import pallas as pl
from jax.experimental.pallas import tpu as pltpu
from jax.sharding import PartitionSpec as P

epsilon = 1e-05
both = ("lat", "lon")
bf16 = jnp.bfloat16
f32 = jnp.float32
lanes = 128
strip = 12
room = pltpu.CompilerParams(vmem_limit_bytes=56 << 20)


def exchange_pairs(count, group, step):
    return [(i, (i // group) * group + ((i % group) ^ step)) for i in range(count)]


def to_dates(tiles):
    dates, count = tiles.shape[0], lax.axis_size("lat")
    own = lax.axis_index("lat") % dates
    pieces = [lax.dynamic_index_in_dim(tiles, own, 0, keepdims=False)]
    for step in range(1, dates):
        pieces.append(
            lax.ppermute(
                lax.dynamic_index_in_dim(tiles, own ^ step, 0, keepdims=False),
                "lat",
                exchange_pairs(count, dates, step),
            )
        )
    stacked = jnp.stack(pieces)
    ordered = [lax.dynamic_index_in_dim(stacked, own ^ tile, 0, keepdims=False) for tile in range(dates)]
    return jnp.concatenate(ordered, axis=0)


def from_dates(band, dates):
    count = lax.axis_size("lat")
    own = lax.axis_index("lat") % dates
    tiles = band.reshape((dates, band.shape[0] // dates) + band.shape[1:])
    pieces = [lax.dynamic_index_in_dim(tiles, own, 0, keepdims=False)]
    for step in range(1, dates):
        pieces.append(
            lax.ppermute(
                lax.dynamic_index_in_dim(tiles, own ^ step, 0, keepdims=False),
                "lat",
                exchange_pairs(count, dates, step),
            )
        )
    stacked = jnp.stack(pieces)
    return jnp.stack([lax.dynamic_index_in_dim(stacked, own ^ date, 0, keepdims=False) for date in range(dates)])


def after(array, event):
    return lax.optimization_barrier((array, event))[0]


def gathered(shard):
    return exchange_all(shard, "lat", lax.axis_index("lat"), 1, lax.axis_size("lat"))


def borders(source, dates):
    count = lax.axis_size("lon")
    forward = [(i, (i + 1) % count) for i in range(count)]
    backward = [(target, origin) for origin, target in forward]
    left = lax.ppermute(source[:, -3:], "lon", forward)
    right = lax.ppermute(source[:, :3], "lon", backward)
    tiles = lax.axis_size("lat")
    if tiles == dates:
        return left, right
    down = [(i, i + dates) for i in range(tiles - dates)]
    up = [(target, origin) for origin, target in down]
    last = jnp.concatenate([left[-3:], source[-3:], right[-3:]], axis=1)
    first = jnp.concatenate([left[:3], source[:3], right[:3]], axis=1)
    return left, right, lax.ppermute(last, "lat", down), lax.ppermute(first, "lat", up)


def sum_all(local):
    count = lax.axis_size(both)
    copies = jnp.broadcast_to(local[None], (count,) + local.shape)
    return jnp.sum(lax.all_to_all(copies, both, 0, 0, tiled=False), axis=0)


def fill_extended(wide_ref, centre, edges):
    rows, columns = centre.shape[0], centre.shape[1]
    blank = jnp.zeros((3, columns + 16, lanes), f32)
    wide_ref[0:3] = blank
    wide_ref[rows + 3 :] = blank
    wide_ref[3 : rows + 3, 8 : columns + 8] = centre[...].astype(f32)
    wide_ref[3 : rows + 3, 5:8] = edges[0][...].astype(f32)
    wide_ref[3 : rows + 3, columns + 8 : columns + 11] = edges[1][...].astype(f32)
    if len(edges) > 2:
        wide_ref[0:3, 5 : columns + 11] = edges[2][...].astype(f32)
        wide_ref[rows + 3 :, 5 : columns + 11] = edges[3][...].astype(f32)


def strip_sum(wide_ref, taps, top, start, flipped):
    total = None
    for column in range(7):
        window = wide_ref[pl.ds(top, strip + 6), start + 5 + column : start + 13 + column, :]
        for across in range(7):
            place = 7 * across + column
            tap = taps[pl.ds(48 - place if flipped else place, 8, stride=0), :]
            term = window[across : across + strip] * tap[None]
            total = term if total is None else total + term
    return total


def stencil_forward_kernel(edge_count, source, *refs):
    edges = refs[:edge_count]
    taps, sea, mixed, sums, wide_ref = refs[edge_count:]
    rows, columns = source.shape[0], source.shape[1]
    fill_extended(wide_ref, source, edges)

    def step(index, carry):
        first, square = carry
        top = index * strip
        for start in range(0, columns, 8):
            here = (pl.ds(top, strip), slice(start, start + 8))
            total = strip_sum(wide_ref, taps, top, start, False)
            mixed[here] = total
            masked = total * sea[here]
            first = first + jnp.sum(masked, axis=0)
            square = square + jnp.sum(masked * total, axis=0)
        return first, square

    zero = jnp.zeros((8, lanes), f32)
    first, square = lax.fori_loop(0, rows // strip, step, (zero, zero))
    sums[0:1] = jnp.sum(first, axis=0, keepdims=True)
    sums[1:2] = jnp.sum(square, axis=0, keepdims=True)


def stencil_backward_kernel(edge_count, grad, *refs):
    edges = refs[:edge_count]
    taps, sea, upstream, out, sums, wide_ref = refs[edge_count:]
    rows, columns = grad.shape[0], grad.shape[1]
    fill_extended(wide_ref, grad, edges)

    def step(index, first):
        top = index * strip
        for start in range(0, columns, 8):
            here = (pl.ds(top, strip), slice(start, start + 8))
            total = strip_sum(wide_ref, taps, top, start, True)
            low = (total + upstream[here].astype(f32) * sea[here]).astype(bf16)
            out[here] = low
            first = first + jnp.sum(low.astype(f32), axis=0)
        return first

    first = lax.fori_loop(0, rows // strip, step, jnp.zeros((8, lanes), f32))
    sums[...] = jnp.sum(first, axis=0, keepdims=True)


def kernel_grad_kernel(edge_count, source, *refs):
    edges = refs[:edge_count]
    grad, out, wide_ref, sums_ref = refs[edge_count:]
    rows, columns = source.shape[0], source.shape[1]
    fill_extended(wide_ref, source, edges)
    sums_ref[...] = jnp.zeros_like(sums_ref)

    def step(index, carry):
        top = index * strip
        for start in range(0, columns, 8):
            upstream = grad[pl.ds(top, strip), start : start + 8, :].astype(f32)
            for column in range(7):
                window = wide_ref[pl.ds(top, strip + 6), start + 5 + column : start + 13 + column, :]
                for across in range(7):
                    sums_ref[7 * across + column] += jnp.sum(window[across : across + strip] * upstream, axis=0)
        return carry

    lax.fori_loop(0, rows // strip, step, 0)
    out[0, 0:49] = jnp.sum(sums_ref[...], axis=1)
    out[0, 49:56] = jnp.zeros((7, lanes), f32)


def by_channel(array):
    rest = array.shape[:-1]
    return pl.BlockSpec(rest + (lanes,), lambda tile: (0,) * len(rest) + (tile,))


def same_block(array):
    return pl.BlockSpec(array.shape, lambda tile: (0,) * array.ndim)


def wide_scratch(rows, columns):
    return pltpu.VMEM((rows + 6, columns + 16, lanes), f32)


def stencil_forward(source, edges, taps, sea):
    rows, columns, channels = source.shape
    sums = jax.ShapeDtypeStruct((2, channels), f32)
    mixed = jax.ShapeDtypeStruct(source.shape, f32)
    return pl.pallas_call(
        functools.partial(stencil_forward_kernel, len(edges)),
        grid=(pl.cdiv(channels, lanes),),
        in_specs=[by_channel(array) for array in (source, *edges, taps)] + [same_block(sea)],
        out_specs=[by_channel(mixed), by_channel(sums)],
        out_shape=[mixed, sums],
        scratch_shapes=[wide_scratch(rows, columns)],
        compiler_params=room,
        name="stencil_forward",
    )(source, *edges, taps, sea)


def stencil_backward(grad, edges, taps, sea, upstream):
    rows, columns, channels = grad.shape
    out = jax.ShapeDtypeStruct(grad.shape, bf16)
    sums = jax.ShapeDtypeStruct((1, channels), f32)
    return pl.pallas_call(
        functools.partial(stencil_backward_kernel, len(edges)),
        grid=(pl.cdiv(channels, lanes),),
        in_specs=[by_channel(array) for array in (grad, *edges, taps)] + [same_block(sea), by_channel(upstream)],
        out_specs=[by_channel(out), by_channel(sums)],
        out_shape=[out, sums],
        scratch_shapes=[wide_scratch(rows, columns)],
        compiler_params=room,
        name="stencil_backward",
    )(grad, *edges, taps, sea, upstream)


def kernel_grad(source, edges, grad):
    rows, columns, channels = source.shape
    tiles = pl.cdiv(channels, lanes)
    out = jax.ShapeDtypeStruct((tiles, 56, lanes), f32)
    return pl.pallas_call(
        functools.partial(kernel_grad_kernel, len(edges)),
        grid=(tiles,),
        in_specs=[by_channel(array) for array in (source, *edges, grad)],
        out_specs=pl.BlockSpec((1, 56, lanes), lambda tile: (tile, 0, 0)),
        out_shape=out,
        scratch_shapes=[wide_scratch(rows, columns), pltpu.VMEM((49, 8, lanes), f32)],
        compiler_params=room,
        name="kernel_grad",
    )(source, *edges, grad)


def chunks_of(width, size):
    edges = list(range(0, width, size))
    if len(edges) > 1 and width - edges[-1] < size // 2:
        edges.pop()
    return list(zip(edges, edges[1:] + [width]))


def spread(sea, channels):
    return jnp.concatenate([sea] * pl.cdiv(channels, lanes), axis=1)[:, :channels]


def gelu_pair(hidden):
    below = 0.5 + 0.5 * lax.erf(hidden * math.sqrt(0.5))
    density = jnp.exp(-0.5 * hidden * hidden) * (1.0 / math.sqrt(2.0 * math.pi))
    return hidden * below, below + hidden * density


def mlp_forward_kernel(
    size, mixed, source, sea, scales, up, up_bias, down, down_bias, *refs
):
    unit = (mixed[...] - scales[0:1]) * scales[1:2]
    low = (unit * scales[2:3] + scales[3:4]).astype(bf16)
    out, active, slope, normed = refs[-4:] if len(refs) == 4 else refs[3:7]
    normed[...] = low
    branch = down_bias[...]
    for a, b in chunks_of(up.shape[1], size):
        hidden = jnp.dot(low, up[:, a:b], preferred_element_type=f32) + up_bias[:, a:b]
        value, rise = gelu_pair(hidden)
        value = value.astype(bf16)
        active[:, a:b] = value
        slope[:, a:b] = rise.astype(bf16)
        branch = branch + jnp.dot(value, down[a:b, :], preferred_element_type=f32)
    mask = spread(sea[...], out.shape[1])
    result = (mask * (source[...].astype(f32) + branch)).astype(bf16)
    out[...] = result
    if len(refs) > 4:
        blocks, widen, widen_bias = refs[:3]
        pooled, coarse = refs[7:]
        mean = (0.25 * jnp.dot(blocks[...], result, preferred_element_type=f32)).astype(bf16)
        pooled[...] = mean
        coarse[...] = (jnp.dot(mean, widen[...], preferred_element_type=f32) + widen_bias[...]).astype(bf16)


def merge_forward_kernel(coarse, skip, merge, bias, members, merged):
    wide = coarse.shape[1]
    upper = jnp.dot(coarse[...], merge[:wide, :], preferred_element_type=f32)
    high = upper.astype(bf16)
    rest = (upper - high.astype(f32)).astype(bf16)
    total = jnp.dot(members[...], high, preferred_element_type=f32)
    total = total + jnp.dot(members[...], rest, preferred_element_type=f32)
    total = total + jnp.dot(skip[...], merge[wide:, :], preferred_element_type=f32)
    merged[...] = (total + bias[...]).astype(bf16)


def merge_backward_kernel(grad, merge, blocks, block_sums, grad_coarse):
    wide = grad_coarse.shape[1]
    low = jnp.dot(blocks[...], grad[...], preferred_element_type=f32).astype(bf16)
    block_sums[...] = low
    grad_coarse[...] = lax.dot_general(
        low, merge[:wide, :], (((1,), (1,)), ((), ())), preferred_element_type=f32
    )


def skip_backward_kernel(grad, grad_wide, merge, widen, members, grad_skip):
    wide = grad_wide.shape[1]
    pooled = 0.25 * lax.dot_general(
        grad_wide[...], widen[...], (((1,), (1,)), ((), ())), preferred_element_type=f32
    )
    high = pooled.astype(bf16)
    rest = (pooled - high.astype(f32)).astype(bf16)
    total = lax.dot_general(grad[...], merge[wide:, :], (((1,), (1,)), ((), ())), preferred_element_type=f32)
    total = total + jnp.dot(members[...], high, preferred_element_type=f32)
    grad_skip[...] = total + jnp.dot(members[...], rest, preferred_element_type=f32)


def mlp_backward_kernel(
    size,
    upstream,
    mixed,
    slope,
    sea,
    scales,
    up,
    down,
    grad_branch,
    grad_hidden,
    grad_normed,
    sums,
    down_sums,
    up_sums,
):
    @pl.when(pl.program_id(0) == 0)
    def _():
        sums[...] = jnp.zeros_like(sums)
        down_sums[...] = jnp.zeros_like(down_sums)
        up_sums[...] = jnp.zeros_like(up_sums)

    mask = spread(sea[...], upstream.shape[1])
    low = (mask * upstream[...].astype(f32)).astype(bf16)
    grad_branch[...] = low
    down_sums[...] += jnp.sum(low.astype(f32), axis=0, keepdims=True)
    normed = None
    for a, b in chunks_of(up.shape[1], size):
        grad_active = lax.dot_general(low, down[a:b, :], (((1,), (1,)), ((), ())), preferred_element_type=f32)
        hidden = (grad_active * slope[:, a:b].astype(f32)).astype(bf16)
        grad_hidden[:, a:b] = hidden
        up_sums[:, a:b] += jnp.sum(hidden.astype(f32), axis=0, keepdims=True)
        part = lax.dot_general(hidden, up[:, a:b], (((1,), (1,)), ((), ())), preferred_element_type=f32)
        normed = part if normed is None else normed + part
    grad_normed[...] = normed
    unit = (mixed[...] - scales[0:1]) * scales[1:2]
    sums[0:1] += jnp.sum(normed, axis=0, keepdims=True)
    sums[1:2] += jnp.sum(normed * unit, axis=0, keepdims=True)


def tall(rows, width):
    return pl.BlockSpec((rows, width), lambda i: (i, 0))


def fixed(array):
    return pl.BlockSpec(array.shape, lambda i: (0, 0), pipeline_mode=pl.Buffered(1))


def by_rows(parts, array):
    return tall(array.shape[0] // parts, array.shape[1])


def mlp_forward(mixed, source, sea, scales, up, up_bias, down, down_bias, pooling=()):
    pixels, channels = mixed.shape
    wide = up.shape[1]
    rows = math.gcd(pixels, 384)
    parts = pixels // rows
    shapes = [(pixels, width) for width in (channels, wide, wide, channels)]
    if pooling:
        shapes += [(pixels // 4, channels), (pixels // 4, pooling[1].shape[1])]
    outs = [jax.ShapeDtypeStruct(shape, bf16) for shape in shapes]
    return pl.pallas_call(
        functools.partial(mlp_forward_kernel, 512),
        grid=(parts,),
        in_specs=[by_rows(parts, array) for array in (mixed, source, sea)]
        + [fixed(array) for array in (scales, up, up_bias, down, down_bias, *pooling)],
        out_specs=[by_rows(parts, out) for out in outs],
        out_shape=outs,
        compiler_params=room,
        name="mlp_forward",
    )(mixed, source, sea, scales, up, up_bias, down, down_bias, *pooling)


def merge_forward(coarse, skip, merge, bias, members, parts):
    merged = jax.ShapeDtypeStruct(skip.shape, bf16)
    return pl.pallas_call(
        merge_forward_kernel,
        grid=(parts,),
        in_specs=[by_rows(parts, array) for array in (coarse, skip)]
        + [fixed(array) for array in (merge, bias, members)],
        out_specs=by_rows(parts, merged),
        out_shape=merged,
        compiler_params=room,
        name="merge_forward",
    )(coarse, skip, merge, bias, members)


def merge_backward(grad, merge, blocks, wide, parts):
    pixels, channels = grad.shape
    block_sums = jax.ShapeDtypeStruct((pixels // 4, channels), bf16)
    grad_coarse = jax.ShapeDtypeStruct((pixels // 4, wide), f32)
    return pl.pallas_call(
        merge_backward_kernel,
        grid=(parts,),
        in_specs=[by_rows(parts, grad), fixed(merge), fixed(blocks)],
        out_specs=[by_rows(parts, block_sums), by_rows(parts, grad_coarse)],
        out_shape=[block_sums, grad_coarse],
        compiler_params=room,
        name="merge_backward",
    )(grad, merge, blocks)


def skip_backward(grad, grad_wide, merge, widen, members, parts):
    grad_skip = jax.ShapeDtypeStruct(grad.shape, f32)
    return pl.pallas_call(
        skip_backward_kernel,
        grid=(parts,),
        in_specs=[by_rows(parts, array) for array in (grad, grad_wide)]
        + [fixed(array) for array in (merge, widen, members)],
        out_specs=by_rows(parts, grad_skip),
        out_shape=grad_skip,
        compiler_params=room,
        name="skip_backward",
    )(grad, grad_wide, merge, widen, members)


def mlp_backward(upstream, mixed, slope, sea, scales, up, down):
    pixels, channels = mixed.shape
    wide = up.shape[1]
    rows = math.gcd(pixels, 384)
    sums = [jax.ShapeDtypeStruct(shape, f32) for shape in ((2, channels), (1, channels), (1, wide))]
    return pl.pallas_call(
        functools.partial(mlp_backward_kernel, 512),
        grid=(pixels // rows,),
        in_specs=[tall(rows, channels), tall(rows, channels), tall(rows, wide), tall(rows, lanes)]
        + [fixed(array) for array in (scales, up, down)],
        out_specs=[tall(rows, channels), tall(rows, wide), tall(rows, channels)]
        + [pl.BlockSpec(array.shape, lambda i: (0, 0)) for array in sums],
        out_shape=[
            jax.ShapeDtypeStruct((pixels, channels), bf16),
            jax.ShapeDtypeStruct((pixels, wide), bf16),
            jax.ShapeDtypeStruct((pixels, channels), f32),
        ]
        + sums,
        compiler_params=room,
        name="mlp_backward",
    )(upstream, mixed, slope, sea, scales, up, down)


def weight_grads_kernel(grad_branch, normed, active, grad_hidden, out, branch_ref, normed_ref):
    @pl.when(pl.program_id(0) == 0)
    def _():
        branch_ref[...] = grad_branch[...].T
        normed_ref[...] = normed[...].T

    up = jnp.dot(normed_ref[...], grad_hidden[...], preferred_element_type=f32).astype(bf16)
    down = jnp.dot(branch_ref[...], active[...], preferred_element_type=f32).astype(bf16)
    for part in range(out.shape[1]):
        out[0, part] = up[:, part * lanes : (part + 1) * lanes]
        out[1, part] = down[:, part * lanes : (part + 1) * lanes]


def weight_grads(grad_branch, normed, active, grad_hidden):
    pixels, channels = normed.shape
    hidden = active.shape[1]
    tiles = pl.cdiv(hidden, lanes)
    parts = next(count for count in (5, 4, 3, 2, 1) if count == 2 or tiles % count == 0)
    return pl.pallas_call(
        weight_grads_kernel,
        grid=(pl.cdiv(tiles, parts),),
        in_specs=[fixed(grad_branch), fixed(normed)]
        + [pl.BlockSpec((pixels, parts * lanes), lambda tile: (0, tile))] * 2,
        out_specs=pl.BlockSpec((2, parts, channels, lanes), lambda tile: (0, tile, 0, 0)),
        out_shape=jax.ShapeDtypeStruct((2, tiles, channels, lanes), bf16),
        scratch_shapes=[pltpu.VMEM((channels, pixels), bf16)] * 2,
        compiler_params=room,
        name="weight_grads",
    )(grad_branch, normed, active, grad_hidden)


def unpack_kernel(core, own, other, up, down):
    mine, theirs = own[...].astype(f32), other[...].astype(f32)
    first = core[0] == 0
    up[...] = jnp.where(first, mine, theirs)
    down[...] = jnp.where(first, theirs, mine)


def unpack(core, own, other, channels, hidden):
    block = pl.BlockSpec((channels, lanes), lambda tile, core: (tile, 0))
    return pl.pallas_call(
        unpack_kernel,
        grid_spec=pltpu.PrefetchScalarGridSpec(
            num_scalar_prefetch=1,
            grid=(pl.cdiv(hidden, lanes),),
            in_specs=[block, block],
            out_specs=[pl.BlockSpec((channels, lanes), lambda tile, core: (0, tile))] * 2,
        ),
        out_shape=[jax.ShapeDtypeStruct((channels, hidden), f32)] * 2,
        compiler_params=room,
        name="unpack",
    )(core, own, other)


def swap(array, axis, step):
    return lax.ppermute(array, axis, [(i, i ^ step) for i in range(lax.axis_size(axis))])


def take(stacked, index):
    return lax.dynamic_index_in_dim(stacked, index, 0, keepdims=False)


def exchange_add(stacked, axis, own, scale):
    count = stacked.shape[0]
    got = [swap(take(stacked, own ^ step), axis, scale * step) for step in range(1, count)]
    total = take(stacked, own).astype(f32)
    for piece in got:
        total = total + piece.astype(f32)
    return total.astype(bf16)


def exchange_all(piece, axis, own, scale, count):
    got = jnp.stack([piece] + [swap(piece, axis, scale * step) for step in range(1, count)])
    return jnp.concatenate([take(got, own ^ place) for place in range(count)], axis=0)


def kept_and_sent(array, bit):
    pieces = array.reshape(2, -1, lanes)
    return take(pieces, bit), take(pieces, 1 - bit)


def low_sum(kept, got):
    return (kept.astype(f32) + got.astype(f32)).astype(bf16)


def in_order(bit, own, other):
    return jnp.where(bit == 0, jnp.concatenate([own, other]), jnp.concatenate([other, own]))


def reduce_over_cores(pair):
    unit = 16 * lax.axis_size("lat") * lax.axis_size("lon") // 2
    rows = pair.shape[1]
    pair = jnp.pad(pair, ((0, 0), (0, -rows % unit), (0, 0)))
    core = lax.axis_index("lon") % 2
    return low_sum(take(pair, core), swap(take(pair, 1 - core), "lon", 1))


def reduce_first(half):
    tile = lax.axis_index("lat")
    parts = []
    for share, step in zip((half[: half.shape[0] // 2], half[half.shape[0] // 2 :]), (1, 2)):
        kept, sent = kept_and_sent(share, tile // step % 2)
        parts.append((kept, swap(sent, "lat", step)))
    return [low_sum(kept, got) for kept, got in parts]


def reduce_second(shares):
    tile = lax.axis_index("lat")
    parts = []
    for share, step in zip(shares, (2, 1)):
        kept, sent = kept_and_sent(share, tile // step % 2)
        parts.append((kept, swap(sent, "lat", step)))
    return jnp.stack([low_sum(kept, got) for kept, got in parts])


def reduce_columns(shares):
    columns = lax.axis_size("lon") // 2
    column = lax.axis_index("lon") // 2
    pieces = shares.reshape(shares.shape[0], columns, -1, lanes).swapaxes(0, 1)
    return exchange_add(pieces, "lon", column, 2)


def spread_columns(share):
    columns = lax.axis_size("lon") // 2
    column = lax.axis_index("lon") // 2
    got = jnp.stack([share] + [swap(share, "lon", 2 * step) for step in range(1, columns)])
    whole = jnp.stack([take(got, column ^ place) for place in range(columns)], axis=1)
    return whole.reshape(share.shape[0], -1, lanes)


def spread_second(shares):
    tile = lax.axis_index("lat")
    return [
        in_order(tile // step % 2, share, swap(share, "lat", step)) for share, step in zip(shares, (2, 1))
    ]


def spread_first(shares):
    tile = lax.axis_index("lat")
    parts = [
        in_order(tile // step % 2, share, swap(share, "lat", step)) for share, step in zip(shares, (1, 2))
    ]
    return jnp.concatenate(parts)


def reduce_tiles(half):
    tiles = lax.axis_size("lat")
    return exchange_add(half.reshape(tiles, -1, lanes), "lat", lax.axis_index("lat"), 1)[None]


def spread_tiles(share):
    return exchange_all(share[0], "lat", lax.axis_index("lat"), 1, lax.axis_size("lat"))


def group_stages():
    two_by_two = lax.axis_size("lat") == 4
    return (
        [reduce_over_cores]
        + ([reduce_first, reduce_second] if two_by_two else [reduce_tiles])
        + [reduce_columns, spread_columns]
        + ([spread_second, spread_first] if two_by_two else [spread_tiles])
        + [lambda half: (half, swap(half, "lon", 1))]
    )


def sum_small(flat):
    count = lax.axis_size(both)
    rows = flat.shape[0]
    padded = -(-rows // (8 * count)) * 8 * count
    pieces = jnp.pad(flat, ((0, padded - rows), (0, 0))).reshape(count, -1, lanes)
    share = jnp.sum(lax.all_to_all(pieces, both, 0, 0, tiled=False), axis=0)
    copies = jnp.broadcast_to(share[None], pieces.shape)
    return lax.all_to_all(copies, both, 0, 0, tiled=False).reshape(padded, lanes)[:rows]


def cross_rows(former, latter):
    return lax.dot_general(former, latter, (((0,), (0,)), ((), ())), preferred_element_type=f32)


def by_transpose(former, latter):
    return lax.dot_general(former, latter, (((1,), (1,)), ((), ())), preferred_element_type=f32)


def block_mix(source, params, sea, ocean, dates):
    kernel, gain, shift = params[:3]
    channels = source.shape[2]
    taps = kernel.astype(f32).reshape(49, channels)
    edges = borders(source, dates)
    mixed, local = stencil_forward(source, edges, taps, sea)
    first, square, ocean = sum_all(jnp.concatenate([local, jnp.broadcast_to(ocean, (1, channels))]))
    mean = first / ocean
    factor = lax.rsqrt(square / ocean - mean * mean + epsilon)
    scales = jnp.stack([mean, factor, gain.astype(f32), shift.astype(f32)])
    return source, edges, taps, mixed.reshape(-1, channels), scales, ocean


def block_forward(mix, params, sea, pooling=()):
    source, edges, taps, mixed, scales, ocean = mix
    up, up_bias, down, down_bias = params[3:]
    channels = source.shape[2]
    output, active, slope, normed, *coarse = mlp_forward(
        mixed,
        source.reshape(-1, channels),
        sea.reshape(-1, lanes),
        scales,
        up,
        up_bias.astype(f32)[None],
        down,
        down_bias.astype(f32)[None],
        pooling,
    )
    return output, coarse, mix + (normed, slope, active)


def block_hidden(upstream, params, sea, stored):
    scales, mixed, slope = stored[4], stored[3], stored[7]
    return mlp_backward(upstream, mixed, slope, sea.reshape(-1, lanes), scales, params[3], params[5])


def block_norm(grad_normed, local, sea, stored, dates):
    source, edges, taps, mixed, scales, ocean = stored[:6]
    channels = source.shape[2]
    grad_shift, grad_gain = sum_all(local)
    mean, factor, gain = scales[0], scales[1], scales[2]
    unit = (mixed - mean) * factor
    weight = spread(sea.reshape(-1, lanes), channels) / ocean
    grad_mixed = factor * (gain * grad_normed - weight * (gain * grad_shift + unit * (gain * grad_gain)))
    grad_mixed = grad_mixed.astype(bf16).reshape(source.shape)
    return grad_mixed, borders(grad_mixed, dates), grad_gain, grad_shift


def block_source(grad_mixed, grad_edges, upstream, sea, stored):
    source, taps = stored[0], stored[2]
    grad_source, sums = stencil_backward(grad_mixed, grad_edges, taps, sea, upstream.reshape(source.shape))
    return grad_source.reshape(-1, source.shape[2]), sums


def shards(
    fine_map,
    ocean_mask,
    out_grad,
    encode_depth,
    encode_gain,
    encode_shift,
    encode_up,
    encode_up_bias,
    encode_down,
    encode_down_bias,
    widen_weight,
    widen_bias,
    bottle_depth,
    bottle_gain,
    bottle_shift,
    bottle_up,
    bottle_up_bias,
    bottle_down,
    bottle_down_bias,
    merge_weight,
    merge_bias,
    decode_depth,
    decode_gain,
    decode_shift,
    decode_up,
    decode_up_bias,
    decode_down,
    decode_down_bias,
):
    dates, tile_rows, breadth, channels = fine_map.shape
    wide = bottle_depth.shape[2]
    extra = jnp.swapaxes(ocean_mask, 1, 2).astype(bf16)[:, None]
    extra = jnp.pad(extra, ((0, 0), (0, 0), (0, 0), (0, channels - tile_rows)))
    packed = to_dates(jnp.concatenate([fine_map, extra], axis=1)).reshape(dates, tile_rows + 1, breadth, channels)
    fine = packed[:, :tile_rows].reshape(-1, breadth, channels)
    ocean_band = jnp.swapaxes(packed[:, tile_rows, :, :tile_rows], 1, 2).reshape(-1, breadth).astype(f32)
    height = fine.shape[0]
    half_height, half_breadth = height // 2, breadth // 2

    encode_rows = encode_up.size // channels
    encode_pack = jnp.concatenate([encode_up.reshape(-1, channels), encode_down])
    encode_pack = gathered(encode_pack).reshape(lax.axis_size("lat"), -1, channels)
    encode_up = encode_pack[:, :encode_rows].reshape(channels, -1)
    encode_down = encode_pack[:, encode_rows:].reshape(-1, channels)
    bottle_up = lax.all_gather(bottle_up, "lat", axis=0, tiled=True)
    bottle_down = lax.all_gather(bottle_down, "lat", axis=0, tiled=True)
    decode_rows = decode_down.shape[0]
    decode_pack = lax.all_gather(jnp.concatenate([decode_down, merge_weight]), "lat", axis=0, tiled=False)
    decode_down = decode_pack[:, :decode_rows].reshape(-1, channels)
    merge_weight = decode_pack[:, decode_rows:].reshape(-1, channels)
    decode_up = lax.all_gather(decode_up, "lat", axis=0, tiled=True)

    coarse_band = jnp.max(ocean_band.reshape(half_height, 2, half_breadth, 2), axis=(1, 3))
    sea_fine = jnp.broadcast_to(ocean_band[..., None], (height, breadth, lanes))
    sea_coarse = jnp.broadcast_to(coarse_band[..., None], (half_height, half_breadth, lanes))
    encode = (encode_depth, encode_gain, encode_shift, encode_up, encode_up_bias, encode_down, encode_down_bias)
    bottle = (bottle_depth, bottle_gain, bottle_shift, bottle_up, bottle_up_bias, bottle_down, bottle_down_bias)
    decode = (decode_depth, decode_gain, decode_shift, decode_up, decode_up_bias, decode_down, decode_down_bias)
    ocean_fine = jnp.sum(ocean_band)
    ocean_coarse = jnp.sum(coarse_band)
    parts = height * breadth // math.gcd(height * breadth, 384)
    pixel = np.arange(height * breadth // parts)
    block = pixel // breadth // 2 * half_breadth + pixel % breadth // 2
    members = jnp.asarray(block[:, None] == np.arange(pixel.size // 4), dtype=bf16)
    blocks = jnp.asarray(np.arange(pixel.size // 4)[:, None] == block, dtype=bf16)

    mix = block_mix(fine, encode, sea_fine, ocean_fine, dates)
    widen_weight = gathered(after(widen_weight, mix[3]))
    skip_rows, (pooled, coarse_in), encode_stored = block_forward(
        mix, encode, sea_fine, (blocks, widen_weight, widen_bias.astype(f32)[None])
    )
    coarse_in = coarse_in.reshape(half_height, half_breadth, wide)
    mix = block_mix(coarse_in, bottle, sea_coarse, ocean_coarse, dates)
    coarse_low, _, coarse_stored = block_forward(mix, bottle, sea_coarse)
    upstream = to_dates(after(out_grad, mix[3])).reshape(-1, channels)
    merged = merge_forward(coarse_low, skip_rows, merge_weight, merge_bias.astype(f32)[None], members, parts)
    mix = block_mix(merged.reshape(fine.shape), decode, sea_fine, ocean_fine, dates)
    decode_rows, _, decode_stored = block_forward(mix, decode, sea_fine)
    result = from_dates(decode_rows.reshape(fine.shape), dates)

    grad_branch, grad_hidden, grad_normed, local, *decode_small = block_hidden(upstream, decode, sea_fine, decode_stored)
    early = [
        cross_rows(decode_stored[6], grad_hidden),
        cross_rows(grad_branch, decode_stored[8]),
    ]
    grad_mixed, grad_edges, *decode_norm = block_norm(grad_normed, local, sea_fine, decode_stored, dates)
    decode_kernel = kernel_grad(*decode_stored[:2], grad_mixed)
    grad_merged, merge_sums = block_source(grad_mixed, grad_edges, upstream, sea_fine, decode_stored)

    block_sums, grad_coarse = merge_backward(grad_merged, merge_weight, blocks, wide, parts)
    early += [cross_rows(block_sums, coarse_low), cross_rows(grad_merged, skip_rows)]
    early = lax.psum([part.astype(bf16) for part in early], both)
    early = [total.astype(f32) for total in early]
    decode_up_sum, decode_down_sum = early[0], early[1].T
    merge_sum = jnp.concatenate(early[2:], axis=1).T

    stages = group_stages()
    grad_branch, grad_hidden, grad_normed, local, *bottle_small = block_hidden(
        grad_coarse, bottle, sea_coarse, coarse_stored
    )
    pair = weight_grads(grad_branch, coarse_stored[6], coarse_stored[8], grad_hidden).reshape(2, -1, lanes)
    grad_mixed, grad_edges, *bottle_norm = block_norm(grad_normed, local, sea_coarse, coarse_stored, dates)
    bottle_kernel = kernel_grad(*coarse_stored[:2], grad_mixed)
    state = stages[0](pair)
    grad_mixed = after(grad_mixed, state)
    grad_wide, widen_sums = block_source(grad_mixed, grad_edges, grad_coarse, sea_coarse, coarse_stored)
    grad_skip = skip_backward(grad_merged, grad_wide, merge_weight, widen_weight, members, parts)

    grad_branch, grad_hidden, grad_normed, local, *encode_small = block_hidden(
        grad_skip, encode, sea_fine, encode_stored
    )
    state = stages[1](state)
    grad_hidden = after(grad_hidden, state)
    encode_pair = weight_grads(grad_branch, encode_stored[6], encode_stored[8], grad_hidden).reshape(2, -1, lanes)
    grad_mixed, grad_edges, *encode_norm = block_norm(grad_normed, local, sea_fine, encode_stored, dates)
    if len(stages) > 6:
        state = stages[2](state)
        grad_mixed = after(grad_mixed, state)
    encode_kernel = kernel_grad(*encode_stored[:2], grad_mixed)
    grad_fine, _ = block_source(grad_mixed, grad_edges, grad_skip, sea_fine, encode_stored)
    for stage in stages[-5:]:
        state = stage(state)
    core = (lax.axis_index("lon") % 2).astype(jnp.int32)[None]
    bottle_up_sum, bottle_down_sum = unpack(core, *state, wide, bottle_up.shape[1])
    bottle_down_sum = bottle_down_sum.T

    grad_widen = cross_rows(pooled, grad_wide).astype(bf16)
    widen_tiles = pl.cdiv(wide, 2 * lanes)
    grad_widen = jnp.pad(grad_widen, ((0, 0), (0, 2 * widen_tiles * lanes - wide)))
    grad_widen = grad_widen.reshape(channels, 2, widen_tiles, lanes).transpose(1, 2, 0, 3).reshape(2, -1, lanes)
    fine_grad = from_dates(grad_fine.reshape(fine.shape), dates)
    state = jnp.concatenate([encode_pair, grad_widen], axis=1)
    for stage in stages:
        state = stage(state)
    own, other = state
    encode_up_sum, encode_down_sum = unpack(core, own, other, channels, encode_up.shape[1])
    encode_down_sum = encode_down_sum.T
    start = encode_pair.shape[1]
    lower = jnp.where(core == 0, own[start : start + grad_widen.shape[1]], other[start : start + grad_widen.shape[1]])
    upper = jnp.where(core == 0, other[start : start + grad_widen.shape[1]], own[start : start + grad_widen.shape[1]])
    widen_sum = jnp.stack([lower, upper]).reshape(2 * widen_tiles, channels, lanes).astype(f32)
    widen_sum = widen_sum.transpose(1, 0, 2).reshape(channels, -1)[:, :wide]

    kernels = [encode_kernel, bottle_kernel, decode_kernel]
    rows = [encode_small, (widen_sums,), bottle_small, (merge_sums,), decode_small]
    rows = [row for group in rows for row in group]
    padded = [jnp.pad(row, ((0, 0), (0, -row.shape[1] % lanes))) for row in rows]
    line = jnp.concatenate(padded, axis=1)
    small = sum_small(jnp.concatenate([array.reshape(-1, lanes) for array in kernels] + [line.reshape(-1, lanes)]))
    kernel_sums, at = [], 0
    for array, shape in zip(kernels, (encode_depth.shape, bottle_depth.shape, decode_depth.shape)):
        count = array.shape[0] * 56
        total = small[at : at + count].reshape(array.shape)[:, :49].transpose(1, 0, 2).reshape(49, -1)
        kernel_sums.append(total[:, : shape[2]].reshape(shape))
        at += count
    line = small[at:].reshape(-1)
    row_sums, at = [], 0
    for row, wider in zip(rows, padded):
        row_sums.append(line[at : at + row.shape[1]])
        at += wider.shape[1]
    (encode_upb, encode_downb, widen_b, bottle_upb, bottle_downb, bottle_merge_b, decode_upb, decode_downb) = (
        row_sums[1],
        row_sums[0],
        row_sums[2],
        row_sums[4],
        row_sums[3],
        row_sums[5],
        row_sums[7],
        row_sums[6],
    )
    return (
        result,
        fine_grad,
        kernel_sums[0],
        encode_norm[0],
        encode_norm[1],
        encode_up_sum,
        encode_upb,
        encode_down_sum,
        encode_downb,
        widen_sum,
        widen_b,
        kernel_sums[1],
        bottle_norm[0],
        bottle_norm[1],
        bottle_up_sum,
        bottle_upb,
        bottle_down_sum,
        bottle_downb,
        merge_sum,
        bottle_merge_b,
        kernel_sums[2],
        decode_norm[0],
        decode_norm[1],
        decode_up_sum,
        decode_upb,
        decode_down_sum,
        decode_downb,
    )


def solution(mesh):
    whole = P()
    rows = P("lat", None)
    tile = P(None, "lat", "lon", None)
    block = (whole, whole, whole, rows, whole, rows, whole)
    placed = (tile, P(None, "lat", "lon"), tile) + block + (rows, whole) + block + (rows, whole) + block
    return jax.shard_map(
        shards,
        mesh=mesh,
        in_specs=placed,
        out_specs=(tile, tile) + (whole,) * 25,
        check_vma=False,
    )
```

```python
import functools
import math

import jax
import jax.numpy as jnp
import numpy as np
from jax import lax
from jax.experimental import pallas as pl
from jax.experimental.pallas import tpu as pltpu
from jax.sharding import PartitionSpec as P

epsilon = 1e-05
both = ("lat", "lon")
bf16 = jnp.bfloat16
f32 = jnp.float32
lanes = 128
strip = 12
room = pltpu.CompilerParams(vmem_limit_bytes=56 << 20)


def exchange_pairs(count, group, step):
    return [(i, (i // group) * group + ((i % group) ^ step)) for i in range(count)]


def send_dates(tiles):
    dates, count = tiles.shape[0], lax.axis_size("lat")
    own = lax.axis_index("lat") % dates
    pieces = [lax.dynamic_index_in_dim(tiles, own, 0, keepdims=False)]
    for step in range(1, dates):
        pieces.append(
            lax.ppermute(
                lax.dynamic_index_in_dim(tiles, own ^ step, 0, keepdims=False),
                "lat",
                exchange_pairs(count, dates, step),
            )
        )
    return pieces


def to_dates(pieces):
    dates = len(pieces)
    own = lax.axis_index("lat") % dates
    stacked = jnp.stack(pieces)
    ordered = [lax.dynamic_index_in_dim(stacked, own ^ tile, 0, keepdims=False) for tile in range(dates)]
    return jnp.concatenate(ordered, axis=0)


def from_dates(band, dates):
    count = lax.axis_size("lat")
    own = lax.axis_index("lat") % dates
    tiles = band.reshape((dates, band.shape[0] // dates) + band.shape[1:])
    pieces = [lax.dynamic_index_in_dim(tiles, own, 0, keepdims=False)]
    for step in range(1, dates):
        pieces.append(
            lax.ppermute(
                lax.dynamic_index_in_dim(tiles, own ^ step, 0, keepdims=False),
                "lat",
                exchange_pairs(count, dates, step),
            )
        )
    stacked = jnp.stack(pieces)
    return jnp.stack([lax.dynamic_index_in_dim(stacked, own ^ date, 0, keepdims=False) for date in range(dates)])


def after(array, event):
    return lax.optimization_barrier((array, event))[0]


def gathered(shard, event=None):
    return exchange_all(shard, "lat", lax.axis_index("lat"), 1, lax.axis_size("lat"), event)


def assemble(kernel, name, shape, arrays, copies):
    tile, core = lax.axis_index("lat"), lax.axis_index("lon") % 2
    return pl.pallas_call(
        kernel,
        in_specs=[pl.BlockSpec(memory_space=pltpu.SMEM)] + [pl.BlockSpec(memory_space=pl.ANY)] * len(arrays),
        out_specs=pl.BlockSpec(memory_space=pltpu.VMEM),
        out_shape=jax.ShapeDtypeStruct(shape, bf16),
        scratch_shapes=[pltpu.SemaphoreType.DMA((copies,))],
        compiler_params=room,
        name=name,
    )(jnp.stack([tile, core]).astype(jnp.int32), *arrays)


def finish(copies):
    for copy in copies:
        copy.start()
    for copy in copies:
        copy.wait()


def assemble_rows_kernel(place, shard, mine, theirs, out, sems):
    tile, core = place[0], place[1]
    rows = shard.shape[0]
    half = rows // 2
    copies = [(shard, tile * rows, rows)]
    for step in range(1, mine.shape[0] + 1):
        start = (tile ^ step) * rows
        copies.append((mine.at[step - 1], start + core * half, half))
        copies.append((theirs.at[step - 1], start + (1 - core) * half, half))
    finish(
        [
            pltpu.make_async_copy(source, out.at[pl.ds(pl.multiple_of(start, 8), count)], sems.at[index])
            for index, (source, start, count) in enumerate(copies)
        ]
    )


def assemble_columns_kernel(place, mine, theirs, out, sems):
    start = out.shape[1] - mine.shape[1]

    def join(low, high):
        finish(
            [
                pltpu.make_async_copy(low.at[:, :start], out.at[:, :start], sems.at[0]),
                pltpu.make_async_copy(high, out.at[:, start:], sems.at[1]),
            ]
        )

    @pl.when(place[1] == 0)
    def _():
        join(mine, theirs)

    @pl.when(place[1] != 0)
    def _():
        join(theirs, mine)


def gathered_by_rows(shard, event):
    tiles = lax.axis_size("lat")
    half = take(shard.reshape(2, -1, shard.shape[1]), lax.axis_index("lon") % 2)
    mine = jnp.stack(after([swap(half, "lat", step) for step in range(1, tiles)], event))
    shape = (tiles * shard.shape[0], shard.shape[1])
    return assemble(assemble_rows_kernel, "assemble_rows", shape, (shard, mine, swap(mine, "lon", 1)), 2 * tiles - 1)


def gathered_by_columns(shard):
    columns = shard.shape[1]
    start = columns // 2 // lanes * lanes
    half = lax.dynamic_slice_in_dim(shard, lax.axis_index("lon") % 2 * start, columns - start, axis=1)
    mine = lax.all_gather(half, "lat", axis=0, tiled=True)
    return assemble(
        assemble_columns_kernel, "assemble_columns", (mine.shape[0], columns), (mine, swap(mine, "lon", 1)), 2
    )


def gathered_pair(up, down, start, event):
    channels = down.shape[1]
    first = lax.axis_index("lon") % 2 == 0
    shard = jnp.where(first, up.reshape(-1, channels), down)
    mine = gathered(after(shard, start), event)
    theirs = swap(mine, "lon", 1)
    return jnp.where(first, mine, theirs).reshape(-1, up.shape[1]), jnp.where(first, theirs, mine)


def borders(source, dates):
    count = lax.axis_size("lon")
    forward = [(i, (i + 1) % count) for i in range(count)]
    backward = [(target, origin) for origin, target in forward]
    left = lax.ppermute(source[:, -3:], "lon", forward)
    right = lax.ppermute(source[:, :3], "lon", backward)
    tiles = lax.axis_size("lat")
    if tiles == dates:
        return left, right
    down = [(i, i + dates) for i in range(tiles - dates)]
    up = [(target, origin) for origin, target in down]
    last = jnp.concatenate([left[-3:], source[-3:], right[-3:]], axis=1)
    first = jnp.concatenate([left[:3], source[:3], right[:3]], axis=1)
    return left, right, lax.ppermute(last, "lat", down), lax.ppermute(first, "lat", up)


def sum_all(local):
    count = lax.axis_size(both)
    copies = jnp.broadcast_to(local[None], (count,) + local.shape)
    return jnp.sum(lax.all_to_all(copies, both, 0, 0, tiled=False), axis=0)


def fill_extended(wide_ref, centre, edges):
    rows, columns = centre.shape[0], centre.shape[1]
    blank = jnp.zeros((3, columns + 16, lanes), f32)
    wide_ref[0:3] = blank
    wide_ref[rows + 3 :] = blank
    wide_ref[3 : rows + 3, 8 : columns + 8] = centre[...].astype(f32)
    wide_ref[3 : rows + 3, 5:8] = edges[0][...].astype(f32)
    wide_ref[3 : rows + 3, columns + 8 : columns + 11] = edges[1][...].astype(f32)
    if len(edges) > 2:
        wide_ref[0:3, 5 : columns + 11] = edges[2][...].astype(f32)
        wide_ref[rows + 3 :, 5 : columns + 11] = edges[3][...].astype(f32)


def strip_sum(wide_ref, taps, top, start, flipped):
    total = None
    for column in range(7):
        window = wide_ref[pl.ds(top, strip + 6), start + 5 + column : start + 13 + column, :]
        for across in range(7):
            place = 7 * across + column
            tap = taps[pl.ds(48 - place if flipped else place, 8, stride=0), :]
            term = window[across : across + strip] * tap[None]
            total = term if total is None else total + term
    return total


def stencil_forward_kernel(edge_count, source, *refs):
    edges = refs[:edge_count]
    taps, sea, mixed, sums, wide_ref = refs[edge_count:]
    rows, columns = source.shape[0], source.shape[1]
    fill_extended(wide_ref, source, edges)

    def step(index, carry):
        first, square = carry
        top = index * strip
        for start in range(0, columns, 8):
            here = (pl.ds(top, strip), slice(start, start + 8))
            total = strip_sum(wide_ref, taps, top, start, False)
            mixed[here] = total
            masked = total * sea[here]
            first = first + jnp.sum(masked, axis=0)
            square = square + jnp.sum(masked * total, axis=0)
        return first, square

    zero = jnp.zeros((8, lanes), f32)
    first, square = lax.fori_loop(0, rows // strip, step, (zero, zero))
    sums[0:1] = jnp.sum(first, axis=0, keepdims=True)
    sums[1:2] = jnp.sum(square, axis=0, keepdims=True)


def stencil_backward_kernel(edge_count, grad, *refs):
    edges = refs[:edge_count]
    taps, sea, upstream, out, sums, wide_ref = refs[edge_count:]
    rows, columns = grad.shape[0], grad.shape[1]
    fill_extended(wide_ref, grad, edges)

    def step(index, first):
        top = index * strip
        for start in range(0, columns, 8):
            here = (pl.ds(top, strip), slice(start, start + 8))
            total = strip_sum(wide_ref, taps, top, start, True)
            low = (total + upstream[here].astype(f32) * sea[here]).astype(bf16)
            out[here] = low
            first = first + jnp.sum(low.astype(f32), axis=0)
        return first

    first = lax.fori_loop(0, rows // strip, step, jnp.zeros((8, lanes), f32))
    sums[...] = jnp.sum(first, axis=0, keepdims=True)


def kernel_grad_kernel(edge_count, source, *refs):
    edges = refs[:edge_count]
    grad, out, wide_ref, sums_ref = refs[edge_count:]
    rows, columns = source.shape[0], source.shape[1]
    fill_extended(wide_ref, source, edges)
    sums_ref[...] = jnp.zeros_like(sums_ref)

    def step(index, carry):
        top = index * strip
        for start in range(0, columns, 8):
            upstream = grad[pl.ds(top, strip), start : start + 8, :].astype(f32)
            for column in range(7):
                window = wide_ref[pl.ds(top, strip + 6), start + 5 + column : start + 13 + column, :]
                for across in range(7):
                    sums_ref[7 * across + column] += jnp.sum(window[across : across + strip] * upstream, axis=0)
        return carry

    lax.fori_loop(0, rows // strip, step, 0)
    out[0, 0:49] = jnp.sum(sums_ref[...], axis=1)
    out[0, 49:56] = jnp.zeros((7, lanes), f32)


def by_channel(array):
    rest = array.shape[:-1]
    return pl.BlockSpec(rest + (lanes,), lambda tile: (0,) * len(rest) + (tile,))


def same_block(array):
    return pl.BlockSpec(array.shape, lambda tile: (0,) * array.ndim)


def wide_scratch(rows, columns):
    return pltpu.VMEM((rows + 6, columns + 16, lanes), f32)


def stencil_forward(source, edges, taps, sea):
    rows, columns, channels = source.shape
    sums = jax.ShapeDtypeStruct((2, channels), f32)
    mixed = jax.ShapeDtypeStruct(source.shape, f32)
    return pl.pallas_call(
        functools.partial(stencil_forward_kernel, len(edges)),
        grid=(pl.cdiv(channels, lanes),),
        in_specs=[by_channel(array) for array in (source, *edges, taps)] + [same_block(sea)],
        out_specs=[by_channel(mixed), by_channel(sums)],
        out_shape=[mixed, sums],
        scratch_shapes=[wide_scratch(rows, columns)],
        compiler_params=room,
        name="stencil_forward",
    )(source, *edges, taps, sea)


def stencil_backward(grad, edges, taps, sea, upstream):
    rows, columns, channels = grad.shape
    out = jax.ShapeDtypeStruct(grad.shape, bf16)
    sums = jax.ShapeDtypeStruct((1, channels), f32)
    return pl.pallas_call(
        functools.partial(stencil_backward_kernel, len(edges)),
        grid=(pl.cdiv(channels, lanes),),
        in_specs=[by_channel(array) for array in (grad, *edges, taps)] + [same_block(sea), by_channel(upstream)],
        out_specs=[by_channel(out), by_channel(sums)],
        out_shape=[out, sums],
        scratch_shapes=[wide_scratch(rows, columns)],
        compiler_params=room,
        name="stencil_backward",
    )(grad, *edges, taps, sea, upstream)


def kernel_grad(source, edges, grad):
    rows, columns, channels = source.shape
    tiles = pl.cdiv(channels, lanes)
    out = jax.ShapeDtypeStruct((tiles, 56, lanes), f32)
    return pl.pallas_call(
        functools.partial(kernel_grad_kernel, len(edges)),
        grid=(tiles,),
        in_specs=[by_channel(array) for array in (source, *edges, grad)],
        out_specs=pl.BlockSpec((1, 56, lanes), lambda tile: (tile, 0, 0)),
        out_shape=out,
        scratch_shapes=[wide_scratch(rows, columns), pltpu.VMEM((49, 8, lanes), f32)],
        compiler_params=room,
        name="kernel_grad",
    )(source, *edges, grad)


def chunks_of(width, size):
    edges = list(range(0, width, size))
    if len(edges) > 1 and width - edges[-1] < size // 2:
        edges.pop()
    return list(zip(edges, edges[1:] + [width]))


def spread(sea, channels):
    return jnp.concatenate([sea] * pl.cdiv(channels, lanes), axis=1)[:, :channels]


def gelu_pair(hidden):
    below = 0.5 + 0.5 * lax.erf(hidden * math.sqrt(0.5))
    density = jnp.exp(-0.5 * hidden * hidden) * (1.0 / math.sqrt(2.0 * math.pi))
    return hidden * below, below + hidden * density


def mlp_forward_kernel(
    size, mixed, source, sea, scales, up, up_bias, down, down_bias, *refs
):
    unit = (mixed[...] - scales[0:1]) * scales[1:2]
    low = (unit * scales[2:3] + scales[3:4]).astype(bf16)
    out, active, slope, normed = refs[-4:] if len(refs) == 4 else refs[3:7]
    normed[...] = low
    branch = down_bias[...]
    for a, b in chunks_of(up.shape[1], size):
        hidden = jnp.dot(low, up[:, a:b], preferred_element_type=f32) + up_bias[:, a:b]
        value, rise = gelu_pair(hidden)
        value = value.astype(bf16)
        active[:, a:b] = value
        slope[:, a:b] = rise.astype(bf16)
        branch = branch + jnp.dot(value, down[a:b, :], preferred_element_type=f32)
    mask = spread(sea[...], out.shape[1])
    result = (mask * (source[...].astype(f32) + branch)).astype(bf16)
    out[...] = result
    if len(refs) > 4:
        blocks, widen, widen_bias = refs[:3]
        pooled, coarse = refs[7:]
        mean = (0.25 * jnp.dot(blocks[...], result, preferred_element_type=f32)).astype(bf16)
        pooled[...] = mean
        coarse[...] = (jnp.dot(mean, widen[...], preferred_element_type=f32) + widen_bias[...]).astype(bf16)


def merge_forward_kernel(coarse, skip, merge, bias, members, merged):
    wide = coarse.shape[1]
    upper = jnp.dot(coarse[...], merge[:wide, :], preferred_element_type=f32)
    high = upper.astype(bf16)
    rest = (upper - high.astype(f32)).astype(bf16)
    total = jnp.dot(members[...], high, preferred_element_type=f32)
    total = total + jnp.dot(members[...], rest, preferred_element_type=f32)
    total = total + jnp.dot(skip[...], merge[wide:, :], preferred_element_type=f32)
    merged[...] = (total + bias[...]).astype(bf16)


def merge_backward_kernel(grad, merge, blocks, block_sums, grad_coarse):
    wide = grad_coarse.shape[1]
    low = jnp.dot(blocks[...], grad[...], preferred_element_type=f32).astype(bf16)
    block_sums[...] = low
    grad_coarse[...] = lax.dot_general(
        low, merge[:wide, :], (((1,), (1,)), ((), ())), preferred_element_type=f32
    )


def skip_backward_kernel(grad, grad_wide, merge, widen, members, grad_skip):
    wide = grad_wide.shape[1]
    pooled = 0.25 * lax.dot_general(
        grad_wide[...], widen[...], (((1,), (1,)), ((), ())), preferred_element_type=f32
    )
    high = pooled.astype(bf16)
    rest = (pooled - high.astype(f32)).astype(bf16)
    total = lax.dot_general(grad[...], merge[wide:, :], (((1,), (1,)), ((), ())), preferred_element_type=f32)
    total = total + jnp.dot(members[...], high, preferred_element_type=f32)
    grad_skip[...] = total + jnp.dot(members[...], rest, preferred_element_type=f32)


def mlp_backward_kernel(
    size,
    upstream,
    mixed,
    slope,
    sea,
    scales,
    up,
    down,
    grad_branch,
    grad_hidden,
    grad_normed,
    sums,
    down_sums,
    up_sums,
):
    @pl.when(pl.program_id(0) == 0)
    def _():
        sums[...] = jnp.zeros_like(sums)
        down_sums[...] = jnp.zeros_like(down_sums)
        up_sums[...] = jnp.zeros_like(up_sums)

    mask = spread(sea[...], upstream.shape[1])
    low = (mask * upstream[...].astype(f32)).astype(bf16)
    grad_branch[...] = low
    down_sums[...] += jnp.sum(low.astype(f32), axis=0, keepdims=True)
    normed = None
    for a, b in chunks_of(up.shape[1], size):
        grad_active = lax.dot_general(low, down[a:b, :], (((1,), (1,)), ((), ())), preferred_element_type=f32)
        hidden = (grad_active * slope[:, a:b].astype(f32)).astype(bf16)
        grad_hidden[:, a:b] = hidden
        up_sums[:, a:b] += jnp.sum(hidden.astype(f32), axis=0, keepdims=True)
        part = lax.dot_general(hidden, up[:, a:b], (((1,), (1,)), ((), ())), preferred_element_type=f32)
        normed = part if normed is None else normed + part
    grad_normed[...] = normed
    unit = (mixed[...] - scales[0:1]) * scales[1:2]
    sums[0:1] += jnp.sum(normed, axis=0, keepdims=True)
    sums[1:2] += jnp.sum(normed * unit, axis=0, keepdims=True)


def tall(rows, width):
    return pl.BlockSpec((rows, width), lambda i: (i, 0))


def fixed(array):
    return pl.BlockSpec(array.shape, lambda i: (0, 0), pipeline_mode=pl.Buffered(1))


def by_rows(parts, array):
    return tall(array.shape[0] // parts, array.shape[1])


def mlp_forward(mixed, source, sea, scales, up, up_bias, down, down_bias, pooling=()):
    pixels, channels = mixed.shape
    wide = up.shape[1]
    rows = math.gcd(pixels, 384)
    parts = pixels // rows
    shapes = [(pixels, width) for width in (channels, wide, wide, channels)]
    if pooling:
        shapes += [(pixels // 4, channels), (pixels // 4, pooling[1].shape[1])]
    outs = [jax.ShapeDtypeStruct(shape, bf16) for shape in shapes]
    return pl.pallas_call(
        functools.partial(mlp_forward_kernel, 512),
        grid=(parts,),
        in_specs=[by_rows(parts, array) for array in (mixed, source, sea)]
        + [fixed(array) for array in (scales, up, up_bias, down, down_bias, *pooling)],
        out_specs=[by_rows(parts, out) for out in outs],
        out_shape=outs,
        compiler_params=room,
        name="mlp_forward",
    )(mixed, source, sea, scales, up, up_bias, down, down_bias, *pooling)


def merge_forward(coarse, skip, merge, bias, members, parts):
    merged = jax.ShapeDtypeStruct(skip.shape, bf16)
    return pl.pallas_call(
        merge_forward_kernel,
        grid=(parts,),
        in_specs=[by_rows(parts, array) for array in (coarse, skip)]
        + [fixed(array) for array in (merge, bias, members)],
        out_specs=by_rows(parts, merged),
        out_shape=merged,
        compiler_params=room,
        name="merge_forward",
    )(coarse, skip, merge, bias, members)


def merge_backward(grad, merge, blocks, wide, parts):
    pixels, channels = grad.shape
    block_sums = jax.ShapeDtypeStruct((pixels // 4, channels), bf16)
    grad_coarse = jax.ShapeDtypeStruct((pixels // 4, wide), f32)
    return pl.pallas_call(
        merge_backward_kernel,
        grid=(parts,),
        in_specs=[by_rows(parts, grad), fixed(merge), fixed(blocks)],
        out_specs=[by_rows(parts, block_sums), by_rows(parts, grad_coarse)],
        out_shape=[block_sums, grad_coarse],
        compiler_params=room,
        name="merge_backward",
    )(grad, merge, blocks)


def skip_backward(grad, grad_wide, merge, widen, members, parts):
    grad_skip = jax.ShapeDtypeStruct(grad.shape, f32)
    return pl.pallas_call(
        skip_backward_kernel,
        grid=(parts,),
        in_specs=[by_rows(parts, array) for array in (grad, grad_wide)]
        + [fixed(array) for array in (merge, widen, members)],
        out_specs=by_rows(parts, grad_skip),
        out_shape=grad_skip,
        compiler_params=room,
        name="skip_backward",
    )(grad, grad_wide, merge, widen, members)


def mlp_backward(upstream, mixed, slope, sea, scales, up, down):
    pixels, channels = mixed.shape
    wide = up.shape[1]
    rows = math.gcd(pixels, 384)
    sums = [jax.ShapeDtypeStruct(shape, f32) for shape in ((2, channels), (1, channels), (1, wide))]
    return pl.pallas_call(
        functools.partial(mlp_backward_kernel, 512),
        grid=(pixels // rows,),
        in_specs=[tall(rows, channels), tall(rows, channels), tall(rows, wide), tall(rows, lanes)]
        + [fixed(array) for array in (scales, up, down)],
        out_specs=[tall(rows, channels), tall(rows, wide), tall(rows, channels)]
        + [pl.BlockSpec(array.shape, lambda i: (0, 0)) for array in sums],
        out_shape=[
            jax.ShapeDtypeStruct((pixels, channels), bf16),
            jax.ShapeDtypeStruct((pixels, wide), bf16),
            jax.ShapeDtypeStruct((pixels, channels), f32),
        ]
        + sums,
        compiler_params=room,
        name="mlp_backward",
    )(upstream, mixed, slope, sea, scales, up, down)


def weight_grads_kernel(grad_branch, normed, active, grad_hidden, out, branch_ref, normed_ref):
    @pl.when(pl.program_id(0) == 0)
    def _():
        branch_ref[...] = grad_branch[...].T
        normed_ref[...] = normed[...].T

    up = jnp.dot(normed_ref[...], grad_hidden[...], preferred_element_type=f32).astype(bf16)
    down = jnp.dot(branch_ref[...], active[...], preferred_element_type=f32).astype(bf16)
    for part in range(out.shape[1]):
        out[0, part] = up[:, part * lanes : (part + 1) * lanes]
        out[1, part] = down[:, part * lanes : (part + 1) * lanes]


def weight_grads(grad_branch, normed, active, grad_hidden):
    pixels, channels = normed.shape
    hidden = active.shape[1]
    tiles = pl.cdiv(hidden, lanes)
    parts = next(count for count in (5, 4, 3, 2, 1) if count == 2 or tiles % count == 0)
    return pl.pallas_call(
        weight_grads_kernel,
        grid=(pl.cdiv(tiles, parts),),
        in_specs=[fixed(grad_branch), fixed(normed)]
        + [pl.BlockSpec((pixels, parts * lanes), lambda tile: (0, tile))] * 2,
        out_specs=pl.BlockSpec((2, parts, channels, lanes), lambda tile: (0, tile, 0, 0)),
        out_shape=jax.ShapeDtypeStruct((2, tiles, channels, lanes), bf16),
        scratch_shapes=[pltpu.VMEM((channels, pixels), bf16)] * 2,
        compiler_params=room,
        name="weight_grads",
    )(grad_branch, normed, active, grad_hidden)


def unpack_kernel(core, own, other, up, down):
    mine, theirs = own[...].astype(f32), other[...].astype(f32)
    first = core[0] == 0
    up[...] = jnp.where(first, mine, theirs)
    down[...] = jnp.where(first, theirs, mine)


def unpack(core, own, other, channels, hidden):
    block = pl.BlockSpec((channels, lanes), lambda tile, core: (tile, 0))
    return pl.pallas_call(
        unpack_kernel,
        grid_spec=pltpu.PrefetchScalarGridSpec(
            num_scalar_prefetch=1,
            grid=(pl.cdiv(hidden, lanes),),
            in_specs=[block, block],
            out_specs=[pl.BlockSpec((channels, lanes), lambda tile, core: (0, tile))] * 2,
        ),
        out_shape=[jax.ShapeDtypeStruct((channels, hidden), f32)] * 2,
        compiler_params=room,
        name="unpack",
    )(core, own, other)


def swap(array, axis, step):
    return lax.ppermute(array, axis, [(i, i ^ step) for i in range(lax.axis_size(axis))])


def take(stacked, index):
    return lax.dynamic_index_in_dim(stacked, index, 0, keepdims=False)


def exchange_add(stacked, axis, own, scale):
    count = stacked.shape[0]
    got = [swap(take(stacked, own ^ step), axis, scale * step) for step in range(1, count)]
    total = take(stacked, own).astype(f32)
    for piece in got:
        total = total + piece.astype(f32)
    return total.astype(bf16)


def exchange_all(piece, axis, own, scale, count, event=None):
    got = [swap(piece, axis, scale * step) for step in range(1, count)]
    got = jnp.stack([piece] + (got if event is None else after(got, event)))
    return jnp.concatenate([take(got, own ^ place) for place in range(count)], axis=0)


def kept_and_sent(array, bit):
    pieces = array.reshape(2, -1, lanes)
    return take(pieces, bit), take(pieces, 1 - bit)


def low_sum(kept, got):
    return (kept.astype(f32) + got.astype(f32)).astype(bf16)


def in_order(bit, own, other):
    return jnp.where(bit == 0, jnp.concatenate([own, other]), jnp.concatenate([other, own]))


def reduce_over_cores(pair):
    unit = 16 * lax.axis_size("lat") * lax.axis_size("lon") // 2
    rows = pair.shape[1]
    pair = jnp.pad(pair, ((0, 0), (0, -rows % unit), (0, 0)))
    core = lax.axis_index("lon") % 2
    return low_sum(take(pair, core), swap(take(pair, 1 - core), "lon", 1))


def reduce_first(half):
    tile = lax.axis_index("lat")
    parts = []
    for share, step in zip((half[: half.shape[0] // 2], half[half.shape[0] // 2 :]), (1, 2)):
        kept, sent = kept_and_sent(share, tile // step % 2)
        parts.append((kept, swap(sent, "lat", step)))
    return [low_sum(kept, got) for kept, got in parts]


def reduce_second(shares):
    tile = lax.axis_index("lat")
    parts = []
    for share, step in zip(shares, (2, 1)):
        kept, sent = kept_and_sent(share, tile // step % 2)
        parts.append((kept, swap(sent, "lat", step)))
    return jnp.stack([low_sum(kept, got) for kept, got in parts])


def reduce_columns(shares):
    columns = lax.axis_size("lon") // 2
    column = lax.axis_index("lon") // 2
    pieces = shares.reshape(shares.shape[0], columns, -1, lanes).swapaxes(0, 1)
    return exchange_add(pieces, "lon", column, 2)


def spread_columns(share):
    columns = lax.axis_size("lon") // 2
    column = lax.axis_index("lon") // 2
    got = jnp.stack([share] + [swap(share, "lon", 2 * step) for step in range(1, columns)])
    whole = jnp.stack([take(got, column ^ place) for place in range(columns)], axis=1)
    return whole.reshape(share.shape[0], -1, lanes)


def spread_second(shares):
    tile = lax.axis_index("lat")
    return [
        in_order(tile // step % 2, share, swap(share, "lat", step)) for share, step in zip(shares, (2, 1))
    ]


def spread_first(shares):
    tile = lax.axis_index("lat")
    parts = [
        in_order(tile // step % 2, share, swap(share, "lat", step)) for share, step in zip(shares, (1, 2))
    ]
    return jnp.concatenate(parts)


def reduce_tiles(half):
    tiles = lax.axis_size("lat")
    return exchange_add(half.reshape(tiles, -1, lanes), "lat", lax.axis_index("lat"), 1)[None]


def spread_tiles(share):
    return exchange_all(share[0], "lat", lax.axis_index("lat"), 1, lax.axis_size("lat"))


def group_stages():
    two_by_two = lax.axis_size("lat") == 4
    return (
        [reduce_over_cores]
        + ([reduce_first, reduce_second] if two_by_two else [reduce_tiles])
        + [reduce_columns, spread_columns]
        + ([spread_second, spread_first] if two_by_two else [spread_tiles])
        + [lambda half: (half, swap(half, "lon", 1))]
    )


def sum_small(flat):
    count = lax.axis_size(both)
    rows = flat.shape[0]
    padded = -(-rows // (8 * count)) * 8 * count
    pieces = jnp.pad(flat, ((0, padded - rows), (0, 0))).reshape(count, -1, lanes)
    share = jnp.sum(lax.all_to_all(pieces, both, 0, 0, tiled=False), axis=0)
    copies = jnp.broadcast_to(share[None], pieces.shape)
    return lax.all_to_all(copies, both, 0, 0, tiled=False).reshape(padded, lanes)[:rows]


def cross_rows(former, latter):
    return lax.dot_general(former, latter, (((0,), (0,)), ((), ())), preferred_element_type=f32)


def by_transpose(former, latter):
    return lax.dot_general(former, latter, (((1,), (1,)), ((), ())), preferred_element_type=f32)


def block_mix(source, params, sea, ocean, dates):
    taps, gain, shift = params[:3]
    channels = source.shape[2]
    edges = borders(source, dates)
    mixed, local = stencil_forward(source, edges, taps, sea)
    first, square, ocean = sum_all(jnp.concatenate([local, jnp.broadcast_to(ocean, (1, channels))]))
    mean = first / ocean
    factor = lax.rsqrt(square / ocean - mean * mean + epsilon)
    scales = jnp.stack([mean, factor, gain, shift])
    return source, edges, taps, mixed.reshape(-1, channels), scales, ocean


def block_forward(mix, params, sea, pooling=()):
    source, edges, taps, mixed, scales, ocean = mix
    up, up_bias, down, down_bias = params[3:]
    channels = source.shape[2]
    output, active, slope, normed, *coarse = mlp_forward(
        mixed,
        source.reshape(-1, channels),
        sea.reshape(-1, lanes),
        scales,
        up,
        up_bias,
        down,
        down_bias,
        pooling,
    )
    return output, coarse, mix + (normed, slope, active)


def block_hidden(upstream, params, sea, stored):
    scales, mixed, slope = stored[4], stored[3], stored[7]
    return mlp_backward(upstream, mixed, slope, sea.reshape(-1, lanes), scales, params[3], params[5])


def block_norm(grad_normed, local, sea, stored, dates):
    source, edges, taps, mixed, scales, ocean = stored[:6]
    channels = source.shape[2]
    grad_shift, grad_gain = sum_all(local)
    mean, factor, gain = scales[0], scales[1], scales[2]
    unit = (mixed - mean) * factor
    weight = spread(sea.reshape(-1, lanes), channels) / ocean
    grad_mixed = factor * (gain * grad_normed - weight * (gain * grad_shift + unit * (gain * grad_gain)))
    grad_mixed = grad_mixed.astype(bf16).reshape(source.shape)
    return grad_mixed, borders(grad_mixed, dates), grad_gain, grad_shift


def block_source(grad_mixed, grad_edges, upstream, sea, stored):
    source, taps = stored[0], stored[2]
    grad_source, sums = stencil_backward(grad_mixed, grad_edges, taps, sea, upstream.reshape(source.shape))
    return grad_source.reshape(-1, source.shape[2]), sums


def shards(
    fine_map,
    ocean_mask,
    out_grad,
    encode_depth,
    encode_gain,
    encode_shift,
    encode_up,
    encode_up_bias,
    encode_down,
    encode_down_bias,
    widen_weight,
    widen_bias,
    bottle_depth,
    bottle_gain,
    bottle_shift,
    bottle_up,
    bottle_up_bias,
    bottle_down,
    bottle_down_bias,
    merge_weight,
    merge_bias,
    decode_depth,
    decode_gain,
    decode_shift,
    decode_up,
    decode_up_bias,
    decode_down,
    decode_down_bias,
):
    dates, tile_rows, breadth, channels = fine_map.shape
    wide = bottle_depth.shape[2]
    extra = jnp.swapaxes(ocean_mask, 1, 2).astype(bf16)[:, None]
    extra = jnp.pad(extra, ((0, 0), (0, 0), (0, 0), (0, channels - tile_rows)))
    pieces = send_dates(jnp.concatenate([fine_map, extra], axis=1))
    kernels = (encode_depth, bottle_depth, decode_depth)
    rows = (encode_up_bias, encode_down_bias, bottle_up_bias, bottle_down_bias, decode_up_bias, decode_down_bias)
    small = (
        [kernel.astype(f32).reshape(49, -1) for kernel in kernels],
        [row.astype(f32)[None] for row in rows + (widen_bias, merge_bias)],
        [row.astype(f32) for row in (encode_gain, encode_shift, bottle_gain, bottle_shift, decode_gain, decode_shift)],
    )
    pieces, (taps, rows, norms) = lax.optimization_barrier((pieces, small))
    encode_up_bias, encode_down_bias, bottle_up_bias, bottle_down_bias, decode_up_bias, decode_down_bias = rows[:6]
    widen_bias, merge_bias = rows[6:]
    encode_norm, bottle_norm, decode_norm = [(taps[i], norms[2 * i], norms[2 * i + 1]) for i in range(3)]
    packed = to_dates(pieces).reshape(dates, tile_rows + 1, breadth, channels)
    fine = packed[:, :tile_rows].reshape(-1, breadth, channels)
    ocean_band = jnp.swapaxes(packed[:, tile_rows, :, :tile_rows], 1, 2).reshape(-1, breadth).astype(f32)
    height = fine.shape[0]
    half_height, half_breadth = height // 2, breadth // 2

    bottle_up = gathered_by_columns(bottle_up)

    coarse_band = jnp.max(ocean_band.reshape(half_height, 2, half_breadth, 2), axis=(1, 3))
    sea_fine = jnp.broadcast_to(ocean_band[..., None], (height, breadth, lanes))
    sea_coarse = jnp.broadcast_to(coarse_band[..., None], (half_height, half_breadth, lanes))
    ocean_fine = jnp.sum(ocean_band)
    ocean_coarse = jnp.sum(coarse_band)
    parts = height * breadth // math.gcd(height * breadth, 384)
    pixel = np.arange(height * breadth // parts)
    block = pixel // breadth // 2 * half_breadth + pixel % breadth // 2
    members = jnp.asarray(block[:, None] == np.arange(pixel.size // 4), dtype=bf16)
    blocks = jnp.asarray(np.arange(pixel.size // 4)[:, None] == block, dtype=bf16)

    mix = block_mix(fine, encode_norm, sea_fine, ocean_fine, dates)
    encode_up, encode_down = gathered_pair(encode_up, encode_down, fine, mix[3])
    encode = encode_norm + (encode_up, encode_up_bias, encode_down, encode_down_bias)
    widen_weight = gathered(after(widen_weight, mix[3]))
    skip_rows, (pooled, coarse_in), encode_stored = block_forward(
        mix, encode, sea_fine, (blocks, widen_weight, widen_bias)
    )
    decode_up = lax.all_gather(after(decode_up, skip_rows), "lat", axis=0, tiled=True)
    decode_down = lax.all_gather(after(decode_down, skip_rows), "lat", axis=0, tiled=True)
    decode = decode_norm + (decode_up, decode_up_bias, decode_down, decode_down_bias)
    bottle_down = gathered_by_rows(after(bottle_down, encode_stored[3]), skip_rows)
    bottle = bottle_norm + (bottle_up, bottle_up_bias, bottle_down, bottle_down_bias)
    coarse_in = coarse_in.reshape(half_height, half_breadth, wide)
    mix = block_mix(coarse_in, bottle, sea_coarse, ocean_coarse, dates)
    coarse_low, _, coarse_stored = block_forward(mix, bottle, sea_coarse)
    merge_rows = merge_weight.shape[0]
    merge_weight = jnp.pad(after(merge_weight, skip_rows), ((0, -merge_rows % 16), (0, 0)))
    merge_weight = gathered(merge_weight, coarse_low).reshape(-1, merge_rows + -merge_rows % 16, channels)
    merge_weight = merge_weight[:, :merge_rows].reshape(-1, channels)
    upstream = send_dates(after(out_grad, mix[3]))
    merged = merge_forward(coarse_low, skip_rows, merge_weight, merge_bias, members, parts)
    mix = block_mix(merged.reshape(fine.shape), decode, sea_fine, ocean_fine, dates)
    upstream = to_dates(after(upstream, mix[3])).reshape(-1, channels)
    decode_rows, _, decode_stored = block_forward(mix, decode, sea_fine)
    result = from_dates(decode_rows.reshape(fine.shape), dates)

    grad_branch, grad_hidden, grad_normed, local, *decode_small = block_hidden(upstream, decode, sea_fine, decode_stored)
    early = [
        cross_rows(decode_stored[6], grad_hidden),
        cross_rows(grad_branch, decode_stored[8]),
    ]
    grad_mixed, grad_edges, *decode_total = block_norm(grad_normed, local, sea_fine, decode_stored, dates)
    decode_mixed = grad_mixed
    grad_merged, merge_sums = block_source(grad_mixed, grad_edges, upstream, sea_fine, decode_stored)

    block_sums, grad_coarse = merge_backward(grad_merged, merge_weight, blocks, wide, parts)
    early += [cross_rows(block_sums, coarse_low), cross_rows(grad_merged, skip_rows)]

    grad_branch, grad_hidden, grad_normed, local, *bottle_small = block_hidden(
        grad_coarse, bottle, sea_coarse, coarse_stored
    )
    decode_kernel = kernel_grad(*decode_stored[:2], after(decode_mixed, local))
    early += [cross_rows(coarse_stored[6], grad_hidden), cross_rows(grad_branch, coarse_stored[8])]
    early = lax.psum([part.astype(bf16) for part in early], both)
    early = [total.astype(f32) for total in early]
    decode_up_sum, decode_down_sum, bottle_up_sum, bottle_down_sum = early[0], early[1].T, early[4], early[5].T
    merge_sum = jnp.concatenate(early[2:4], axis=1).T
    grad_mixed, grad_edges, *bottle_total = block_norm(grad_normed, local, sea_coarse, coarse_stored, dates)
    bottle_kernel = kernel_grad(*coarse_stored[:2], grad_mixed)
    grad_wide, widen_sums = block_source(grad_mixed, grad_edges, grad_coarse, sea_coarse, coarse_stored)
    grad_skip = skip_backward(grad_merged, grad_wide, merge_weight, widen_weight, members, parts)

    grad_branch, grad_hidden, grad_normed, local, *encode_small = block_hidden(
        grad_skip, encode, sea_fine, encode_stored
    )
    encode_pair = weight_grads(grad_branch, encode_stored[6], encode_stored[8], grad_hidden).reshape(2, -1, lanes)
    grad_mixed, grad_edges, *encode_total = block_norm(grad_normed, local, sea_fine, encode_stored, dates)
    encode_kernel = kernel_grad(*encode_stored[:2], grad_mixed)
    grad_fine, _ = block_source(grad_mixed, grad_edges, grad_skip, sea_fine, encode_stored)
    core = (lax.axis_index("lon") % 2).astype(jnp.int32)[None]
    grad_widen = cross_rows(pooled, grad_wide).astype(bf16)
    widen_tiles = pl.cdiv(wide, 2 * lanes)
    grad_widen = jnp.pad(grad_widen, ((0, 0), (0, 2 * widen_tiles * lanes - wide)))
    grad_widen = grad_widen.reshape(channels, 2, widen_tiles, lanes).transpose(1, 2, 0, 3).reshape(2, -1, lanes)
    fine_grad = from_dates(grad_fine.reshape(fine.shape), dates)
    state = jnp.concatenate([encode_pair, grad_widen], axis=1)
    for stage in group_stages():
        state = stage(state)
    own, other = state
    encode_up_sum, encode_down_sum = unpack(core, own, other, channels, encode_up.shape[1])
    encode_down_sum = encode_down_sum.T
    start = encode_pair.shape[1]
    lower = jnp.where(core == 0, own[start : start + grad_widen.shape[1]], other[start : start + grad_widen.shape[1]])
    upper = jnp.where(core == 0, other[start : start + grad_widen.shape[1]], own[start : start + grad_widen.shape[1]])
    widen_sum = jnp.stack([lower, upper]).reshape(2 * widen_tiles, channels, lanes).astype(f32)
    widen_sum = widen_sum.transpose(1, 0, 2).reshape(channels, -1)[:, :wide]

    kernels = [encode_kernel, bottle_kernel, decode_kernel]
    rows = [encode_small, (widen_sums,), bottle_small, (merge_sums,), decode_small]
    rows = [row for group in rows for row in group]
    padded = [jnp.pad(row, ((0, 0), (0, -row.shape[1] % lanes))) for row in rows]
    line = jnp.concatenate(padded, axis=1)
    small = sum_small(jnp.concatenate([array.reshape(-1, lanes) for array in kernels] + [line.reshape(-1, lanes)]))
    kernel_sums, at = [], 0
    for array, shape in zip(kernels, (encode_depth.shape, bottle_depth.shape, decode_depth.shape)):
        count = array.shape[0] * 56
        total = small[at : at + count].reshape(array.shape)[:, :49].transpose(1, 0, 2).reshape(49, -1)
        kernel_sums.append(total[:, : shape[2]].reshape(shape))
        at += count
    line = small[at:].reshape(-1)
    row_sums, at = [], 0
    for row, wider in zip(rows, padded):
        row_sums.append(line[at : at + row.shape[1]])
        at += wider.shape[1]
    (encode_upb, encode_downb, widen_b, bottle_upb, bottle_downb, bottle_merge_b, decode_upb, decode_downb) = (
        row_sums[1],
        row_sums[0],
        row_sums[2],
        row_sums[4],
        row_sums[3],
        row_sums[5],
        row_sums[7],
        row_sums[6],
    )
    return (
        result,
        fine_grad,
        kernel_sums[0],
        encode_total[0],
        encode_total[1],
        encode_up_sum,
        encode_upb,
        encode_down_sum,
        encode_downb,
        widen_sum,
        widen_b,
        kernel_sums[1],
        bottle_total[0],
        bottle_total[1],
        bottle_up_sum,
        bottle_upb,
        bottle_down_sum,
        bottle_downb,
        merge_sum,
        bottle_merge_b,
        kernel_sums[2],
        decode_total[0],
        decode_total[1],
        decode_up_sum,
        decode_upb,
        decode_down_sum,
        decode_downb,
    )


def solution(mesh):
    whole = P()
    rows = P("lat", None)
    tile = P(None, "lat", "lon", None)
    block = (whole, whole, whole, rows, whole, rows, whole)
    placed = (tile, P(None, "lat", "lon"), tile) + block + (rows, whole) + block + (rows, whole) + block
    return jax.shard_map(
        shards,
        mesh=mesh,
        in_specs=placed,
        out_specs=(tile, tile) + (whole,) * 25,
        check_vma=False,
    )
```

```python
import functools
import math

import jax
import jax.numpy as jnp
import numpy as np
from jax import lax
from jax.experimental import pallas as pl
from jax.experimental.pallas import tpu as pltpu
from jax.sharding import PartitionSpec as P

epsilon = 1e-05
both = ("lat", "lon")
bf16 = jnp.bfloat16
f32 = jnp.float32
lanes = 128
strip = 12
room = pltpu.CompilerParams(vmem_limit_bytes=56 << 20)


def exchange_pairs(count, group, step):
    return [(i, (i // group) * group + ((i % group) ^ step)) for i in range(count)]


def send_dates(tiles):
    dates, count = tiles.shape[0], lax.axis_size("lat")
    own = lax.axis_index("lat") % dates
    pieces = [lax.dynamic_index_in_dim(tiles, own, 0, keepdims=False)]
    for step in range(1, dates):
        pieces.append(
            lax.ppermute(
                lax.dynamic_index_in_dim(tiles, own ^ step, 0, keepdims=False),
                "lat",
                exchange_pairs(count, dates, step),
            )
        )
    return pieces


def to_dates(pieces):
    dates = len(pieces)
    own = lax.axis_index("lat") % dates
    stacked = jnp.stack(pieces)
    ordered = [lax.dynamic_index_in_dim(stacked, own ^ tile, 0, keepdims=False) for tile in range(dates)]
    return jnp.concatenate(ordered, axis=0)


def from_dates(band, dates):
    count = lax.axis_size("lat")
    own = lax.axis_index("lat") % dates
    tiles = band.reshape((dates, band.shape[0] // dates) + band.shape[1:])
    pieces = [lax.dynamic_index_in_dim(tiles, own, 0, keepdims=False)]
    for step in range(1, dates):
        pieces.append(
            lax.ppermute(
                lax.dynamic_index_in_dim(tiles, own ^ step, 0, keepdims=False),
                "lat",
                exchange_pairs(count, dates, step),
            )
        )
    stacked = jnp.stack(pieces)
    return jnp.stack([lax.dynamic_index_in_dim(stacked, own ^ date, 0, keepdims=False) for date in range(dates)])


def after(array, event):
    return lax.optimization_barrier((array, event))[0]


def gathered(shard, event=None):
    return exchange_all(shard, "lat", lax.axis_index("lat"), 1, lax.axis_size("lat"), event)


def assemble(kernel, name, shape, arrays, copies):
    tile, core = lax.axis_index("lat"), lax.axis_index("lon") % 2
    return pl.pallas_call(
        kernel,
        in_specs=[pl.BlockSpec(memory_space=pltpu.SMEM)] + [pl.BlockSpec(memory_space=pl.ANY)] * len(arrays),
        out_specs=pl.BlockSpec(memory_space=pltpu.VMEM),
        out_shape=jax.ShapeDtypeStruct(shape, bf16),
        scratch_shapes=[pltpu.SemaphoreType.DMA((copies,))],
        compiler_params=room,
        name=name,
    )(jnp.stack([tile, core]).astype(jnp.int32), *arrays)


def finish(copies):
    for copy in copies:
        copy.start()
    for copy in copies:
        copy.wait()


def assemble_rows_kernel(place, shard, mine, theirs, out, sems):
    tile, core = place[0], place[1]
    rows = shard.shape[0]
    half = rows // 2
    copies = [(shard, tile * rows, rows)]
    for step in range(1, mine.shape[0] + 1):
        start = (tile ^ step) * rows
        copies.append((mine.at[step - 1], start + core * half, half))
        copies.append((theirs.at[step - 1], start + (1 - core) * half, half))
    finish(
        [
            pltpu.make_async_copy(source, out.at[pl.ds(pl.multiple_of(start, 8), count)], sems.at[index])
            for index, (source, start, count) in enumerate(copies)
        ]
    )


def assemble_columns_kernel(place, mine, theirs, out, sems):
    start = out.shape[1] - mine.shape[1]

    def join(low, high):
        finish(
            [
                pltpu.make_async_copy(low.at[:, :start], out.at[:, :start], sems.at[0]),
                pltpu.make_async_copy(high, out.at[:, start:], sems.at[1]),
            ]
        )

    @pl.when(place[1] == 0)
    def _():
        join(mine, theirs)

    @pl.when(place[1] != 0)
    def _():
        join(theirs, mine)


def gathered_by_rows(shard, event):
    tiles = lax.axis_size("lat")
    half = take(shard.reshape(2, -1, shard.shape[1]), lax.axis_index("lon") % 2)
    mine = jnp.stack(after([swap(half, "lat", step) for step in range(1, tiles)], event))
    shape = (tiles * shard.shape[0], shard.shape[1])
    return assemble(assemble_rows_kernel, "assemble_rows", shape, (shard, mine, swap(mine, "lon", 1)), 2 * tiles - 1)


def gathered_by_columns(shard):
    columns = shard.shape[1]
    start = columns // 2 // lanes * lanes
    half = lax.dynamic_slice_in_dim(shard, lax.axis_index("lon") % 2 * start, columns - start, axis=1)
    mine = lax.all_gather(half, "lat", axis=0, tiled=True)
    return assemble(
        assemble_columns_kernel, "assemble_columns", (mine.shape[0], columns), (mine, swap(mine, "lon", 1)), 2
    )


def gathered_pair(up, down):
    channels = down.shape[1]
    first = lax.axis_index("lon") % 2 == 0
    mine = lax.all_gather(jnp.where(first, up.reshape(-1, channels), down), "lat", axis=0, tiled=True)
    theirs = swap(mine, "lon", 1)
    return jnp.where(first, mine, theirs).reshape(-1, up.shape[1]), jnp.where(first, theirs, mine)


def borders(source, dates):
    count = lax.axis_size("lon")
    forward = [(i, (i + 1) % count) for i in range(count)]
    backward = [(target, origin) for origin, target in forward]
    left = lax.ppermute(source[:, -3:], "lon", forward)
    right = lax.ppermute(source[:, :3], "lon", backward)
    tiles = lax.axis_size("lat")
    if tiles == dates:
        return left, right
    down = [(i, i + dates) for i in range(tiles - dates)]
    up = [(target, origin) for origin, target in down]
    last = jnp.concatenate([left[-3:], source[-3:], right[-3:]], axis=1)
    first = jnp.concatenate([left[:3], source[:3], right[:3]], axis=1)
    return left, right, lax.ppermute(last, "lat", down), lax.ppermute(first, "lat", up)


def sum_all(local, event=()):
    count = lax.axis_size(both)
    copies = jnp.broadcast_to(local[None], (count,) + local.shape)
    return jnp.sum(after(lax.all_to_all(copies, both, 0, 0, tiled=False), event), axis=0)


def fill_extended(wide_ref, centre, edges):
    rows, columns = centre.shape[0], centre.shape[1]
    blank = jnp.zeros((3, columns + 16, lanes), f32)
    wide_ref[0:3] = blank
    wide_ref[rows + 3 :] = blank
    wide_ref[3 : rows + 3, 8 : columns + 8] = centre[...].astype(f32)
    wide_ref[3 : rows + 3, 5:8] = edges[0][...].astype(f32)
    wide_ref[3 : rows + 3, columns + 8 : columns + 11] = edges[1][...].astype(f32)
    if len(edges) > 2:
        wide_ref[0:3, 5 : columns + 11] = edges[2][...].astype(f32)
        wide_ref[rows + 3 :, 5 : columns + 11] = edges[3][...].astype(f32)


def strip_sum(wide_ref, taps, top, start, flipped):
    total = None
    for column in range(7):
        window = wide_ref[pl.ds(top, strip + 6), start + 5 + column : start + 13 + column, :]
        for across in range(7):
            place = 7 * across + column
            tap = taps[pl.ds(48 - place if flipped else place, 8, stride=0), :]
            term = window[across : across + strip] * tap[None]
            total = term if total is None else total + term
    return total


def stencil_forward_kernel(edge_count, source, *refs):
    edges = refs[:edge_count]
    taps, sea, mixed, sums, wide_ref = refs[edge_count:]
    rows, columns = source.shape[0], source.shape[1]
    fill_extended(wide_ref, source, edges)

    def step(index, carry):
        first, square = carry
        top = index * strip
        for start in range(0, columns, 8):
            here = (pl.ds(top, strip), slice(start, start + 8))
            total = strip_sum(wide_ref, taps, top, start, False)
            mixed[here] = total
            masked = total * sea[here]
            first = first + jnp.sum(masked, axis=0)
            square = square + jnp.sum(masked * total, axis=0)
        return first, square

    zero = jnp.zeros((8, lanes), f32)
    first, square = lax.fori_loop(0, rows // strip, step, (zero, zero))
    sums[0:1] = jnp.sum(first, axis=0, keepdims=True)
    sums[1:2] = jnp.sum(square, axis=0, keepdims=True)


def stencil_backward_kernel(edge_count, grad, *refs):
    edges = refs[:edge_count]
    taps, sea, upstream, out, sums, wide_ref = refs[edge_count:]
    rows, columns = grad.shape[0], grad.shape[1]
    fill_extended(wide_ref, grad, edges)

    def step(index, first):
        top = index * strip
        for start in range(0, columns, 8):
            here = (pl.ds(top, strip), slice(start, start + 8))
            total = strip_sum(wide_ref, taps, top, start, True)
            low = (total + upstream[here].astype(f32) * sea[here]).astype(bf16)
            out[here] = low
            first = first + jnp.sum(low.astype(f32), axis=0)
        return first

    first = lax.fori_loop(0, rows // strip, step, jnp.zeros((8, lanes), f32))
    sums[...] = jnp.sum(first, axis=0, keepdims=True)


def kernel_grad_kernel(edge_count, source, *refs):
    edges = refs[:edge_count]
    grad, out, wide_ref, sums_ref = refs[edge_count:]
    rows, columns = source.shape[0], source.shape[1]
    fill_extended(wide_ref, source, edges)
    sums_ref[...] = jnp.zeros_like(sums_ref)

    def step(index, carry):
        top = index * strip
        for start in range(0, columns, 8):
            upstream = grad[pl.ds(top, strip), start : start + 8, :].astype(f32)
            for column in range(7):
                window = wide_ref[pl.ds(top, strip + 6), start + 5 + column : start + 13 + column, :]
                for across in range(7):
                    sums_ref[7 * across + column] += jnp.sum(window[across : across + strip] * upstream, axis=0)
        return carry

    lax.fori_loop(0, rows // strip, step, 0)
    out[0, 0:49] = jnp.sum(sums_ref[...], axis=1)
    out[0, 49:56] = jnp.zeros((7, lanes), f32)


def by_channel(array):
    rest = array.shape[:-1]
    return pl.BlockSpec(rest + (lanes,), lambda tile: (0,) * len(rest) + (tile,))


def same_block(array):
    return pl.BlockSpec(array.shape, lambda tile: (0,) * array.ndim)


def wide_scratch(rows, columns):
    return pltpu.VMEM((rows + 6, columns + 16, lanes), f32)


def stencil_forward(source, edges, taps, sea):
    rows, columns, channels = source.shape
    sums = jax.ShapeDtypeStruct((2, channels), f32)
    mixed = jax.ShapeDtypeStruct(source.shape, f32)
    return pl.pallas_call(
        functools.partial(stencil_forward_kernel, len(edges)),
        grid=(pl.cdiv(channels, lanes),),
        in_specs=[by_channel(array) for array in (source, *edges, taps)] + [same_block(sea)],
        out_specs=[by_channel(mixed), by_channel(sums)],
        out_shape=[mixed, sums],
        scratch_shapes=[wide_scratch(rows, columns)],
        compiler_params=room,
        name="stencil_forward",
    )(source, *edges, taps, sea)


def stencil_backward(grad, edges, taps, sea, upstream):
    rows, columns, channels = grad.shape
    out = jax.ShapeDtypeStruct(grad.shape, bf16)
    sums = jax.ShapeDtypeStruct((1, channels), f32)
    return pl.pallas_call(
        functools.partial(stencil_backward_kernel, len(edges)),
        grid=(pl.cdiv(channels, lanes),),
        in_specs=[by_channel(array) for array in (grad, *edges, taps)] + [same_block(sea), by_channel(upstream)],
        out_specs=[by_channel(out), by_channel(sums)],
        out_shape=[out, sums],
        scratch_shapes=[wide_scratch(rows, columns)],
        compiler_params=room,
        name="stencil_backward",
    )(grad, *edges, taps, sea, upstream)


def kernel_grad(source, edges, grad):
    rows, columns, channels = source.shape
    tiles = pl.cdiv(channels, lanes)
    out = jax.ShapeDtypeStruct((tiles, 56, lanes), f32)
    return pl.pallas_call(
        functools.partial(kernel_grad_kernel, len(edges)),
        grid=(tiles,),
        in_specs=[by_channel(array) for array in (source, *edges, grad)],
        out_specs=pl.BlockSpec((1, 56, lanes), lambda tile: (tile, 0, 0)),
        out_shape=out,
        scratch_shapes=[wide_scratch(rows, columns), pltpu.VMEM((49, 8, lanes), f32)],
        compiler_params=room,
        name="kernel_grad",
    )(source, *edges, grad)


def chunks_of(width, size):
    edges = list(range(0, width, size))
    if len(edges) > 1 and width - edges[-1] < size // 2:
        edges.pop()
    return list(zip(edges, edges[1:] + [width]))


def spread(sea, channels):
    return jnp.concatenate([sea] * pl.cdiv(channels, lanes), axis=1)[:, :channels]


def gelu_pair(hidden):
    below = 0.5 + 0.5 * lax.erf(hidden * math.sqrt(0.5))
    density = jnp.exp(-0.5 * hidden * hidden) * (1.0 / math.sqrt(2.0 * math.pi))
    return hidden * below, below + hidden * density


def mlp_forward_kernel(
    size, mixed, source, sea, scales, up, up_bias, down, down_bias, *refs
):
    unit = (mixed[...] - scales[0:1]) * scales[1:2]
    low = (unit * scales[2:3] + scales[3:4]).astype(bf16)
    out, active, slope, normed = refs[-4:] if len(refs) == 4 else refs[3:7]
    normed[...] = low
    branch = down_bias[...]
    for a, b in chunks_of(up.shape[1], size):
        hidden = jnp.dot(low, up[:, a:b], preferred_element_type=f32) + up_bias[:, a:b]
        value, rise = gelu_pair(hidden)
        value = value.astype(bf16)
        active[:, a:b] = value
        slope[:, a:b] = rise.astype(bf16)
        branch = branch + jnp.dot(value, down[a:b, :], preferred_element_type=f32)
    mask = spread(sea[...], out.shape[1])
    result = (mask * (source[...].astype(f32) + branch)).astype(bf16)
    out[...] = result
    if len(refs) > 4:
        blocks, widen, widen_bias = refs[:3]
        pooled, coarse = refs[7:]
        mean = (0.25 * jnp.dot(blocks[...], result, preferred_element_type=f32)).astype(bf16)
        pooled[...] = mean
        coarse[...] = (jnp.dot(mean, widen[...], preferred_element_type=f32) + widen_bias[...]).astype(bf16)


def merge_forward_kernel(coarse, skip, merge, bias, members, merged):
    wide = coarse.shape[1]
    upper = jnp.dot(coarse[...], merge[:wide, :], preferred_element_type=f32)
    high = upper.astype(bf16)
    rest = (upper - high.astype(f32)).astype(bf16)
    total = jnp.dot(members[...], high, preferred_element_type=f32)
    total = total + jnp.dot(members[...], rest, preferred_element_type=f32)
    total = total + jnp.dot(skip[...], merge[wide:, :], preferred_element_type=f32)
    merged[...] = (total + bias[...]).astype(bf16)


def merge_backward_kernel(grad, merge, blocks, block_sums, grad_coarse):
    wide = grad_coarse.shape[1]
    low = jnp.dot(blocks[...], grad[...], preferred_element_type=f32).astype(bf16)
    block_sums[...] = low
    grad_coarse[...] = lax.dot_general(
        low, merge[:wide, :], (((1,), (1,)), ((), ())), preferred_element_type=f32
    )


def skip_backward_kernel(grad, grad_wide, merge, widen, members, grad_skip):
    wide = grad_wide.shape[1]
    pooled = 0.25 * lax.dot_general(
        grad_wide[...], widen[...], (((1,), (1,)), ((), ())), preferred_element_type=f32
    )
    high = pooled.astype(bf16)
    rest = (pooled - high.astype(f32)).astype(bf16)
    total = lax.dot_general(grad[...], merge[wide:, :], (((1,), (1,)), ((), ())), preferred_element_type=f32)
    total = total + jnp.dot(members[...], high, preferred_element_type=f32)
    grad_skip[...] = total + jnp.dot(members[...], rest, preferred_element_type=f32)


def mlp_backward_kernel(
    size,
    upstream,
    mixed,
    slope,
    sea,
    scales,
    up,
    down,
    grad_branch,
    grad_hidden,
    grad_normed,
    sums,
    down_sums,
    up_sums,
):
    @pl.when(pl.program_id(0) == 0)
    def _():
        sums[...] = jnp.zeros_like(sums)
        down_sums[...] = jnp.zeros_like(down_sums)
        up_sums[...] = jnp.zeros_like(up_sums)

    mask = spread(sea[...], upstream.shape[1])
    low = (mask * upstream[...].astype(f32)).astype(bf16)
    grad_branch[...] = low
    down_sums[...] += jnp.sum(low.astype(f32), axis=0, keepdims=True)
    normed = None
    for a, b in chunks_of(up.shape[1], size):
        grad_active = lax.dot_general(low, down[a:b, :], (((1,), (1,)), ((), ())), preferred_element_type=f32)
        hidden = (grad_active * slope[:, a:b].astype(f32)).astype(bf16)
        grad_hidden[:, a:b] = hidden
        up_sums[:, a:b] += jnp.sum(hidden.astype(f32), axis=0, keepdims=True)
        part = lax.dot_general(hidden, up[:, a:b], (((1,), (1,)), ((), ())), preferred_element_type=f32)
        normed = part if normed is None else normed + part
    grad_normed[...] = normed
    unit = (mixed[...] - scales[0:1]) * scales[1:2]
    sums[0:1] += jnp.sum(normed, axis=0, keepdims=True)
    sums[1:2] += jnp.sum(normed * unit, axis=0, keepdims=True)


def tall(rows, width):
    return pl.BlockSpec((rows, width), lambda i: (i, 0))


def fixed(array):
    return pl.BlockSpec(array.shape, lambda i: (0, 0), pipeline_mode=pl.Buffered(1))


def by_rows(parts, array):
    return tall(array.shape[0] // parts, array.shape[1])


def mlp_forward(mixed, source, sea, scales, up, up_bias, down, down_bias, pooling=()):
    pixels, channels = mixed.shape
    wide = up.shape[1]
    rows = math.gcd(pixels, 384)
    parts = pixels // rows
    shapes = [(pixels, width) for width in (channels, wide, wide, channels)]
    if pooling:
        shapes += [(pixels // 4, channels), (pixels // 4, pooling[1].shape[1])]
    outs = [jax.ShapeDtypeStruct(shape, bf16) for shape in shapes]
    return pl.pallas_call(
        functools.partial(mlp_forward_kernel, 512),
        grid=(parts,),
        in_specs=[by_rows(parts, array) for array in (mixed, source, sea)]
        + [fixed(array) for array in (scales, up, up_bias, down, down_bias, *pooling)],
        out_specs=[by_rows(parts, out) for out in outs],
        out_shape=outs,
        compiler_params=room,
        name="mlp_forward",
    )(mixed, source, sea, scales, up, up_bias, down, down_bias, *pooling)


def merge_forward(coarse, skip, merge, bias, members, parts):
    merged = jax.ShapeDtypeStruct(skip.shape, bf16)
    return pl.pallas_call(
        merge_forward_kernel,
        grid=(parts,),
        in_specs=[by_rows(parts, array) for array in (coarse, skip)]
        + [fixed(array) for array in (merge, bias, members)],
        out_specs=by_rows(parts, merged),
        out_shape=merged,
        compiler_params=room,
        name="merge_forward",
    )(coarse, skip, merge, bias, members)


def merge_backward(grad, merge, blocks, wide, parts):
    pixels, channels = grad.shape
    block_sums = jax.ShapeDtypeStruct((pixels // 4, channels), bf16)
    grad_coarse = jax.ShapeDtypeStruct((pixels // 4, wide), f32)
    return pl.pallas_call(
        merge_backward_kernel,
        grid=(parts,),
        in_specs=[by_rows(parts, grad), fixed(merge), fixed(blocks)],
        out_specs=[by_rows(parts, block_sums), by_rows(parts, grad_coarse)],
        out_shape=[block_sums, grad_coarse],
        compiler_params=room,
        name="merge_backward",
    )(grad, merge, blocks)


def skip_backward(grad, grad_wide, merge, widen, members, parts):
    grad_skip = jax.ShapeDtypeStruct(grad.shape, f32)
    return pl.pallas_call(
        skip_backward_kernel,
        grid=(parts,),
        in_specs=[by_rows(parts, array) for array in (grad, grad_wide)]
        + [fixed(array) for array in (merge, widen, members)],
        out_specs=by_rows(parts, grad_skip),
        out_shape=grad_skip,
        compiler_params=room,
        name="skip_backward",
    )(grad, grad_wide, merge, widen, members)


def mlp_backward(upstream, mixed, slope, sea, scales, up, down):
    pixels, channels = mixed.shape
    wide = up.shape[1]
    rows = math.gcd(pixels, 384)
    sums = [jax.ShapeDtypeStruct(shape, f32) for shape in ((2, channels), (1, channels), (1, wide))]
    return pl.pallas_call(
        functools.partial(mlp_backward_kernel, 512),
        grid=(pixels // rows,),
        in_specs=[tall(rows, channels), tall(rows, channels), tall(rows, wide), tall(rows, lanes)]
        + [fixed(array) for array in (scales, up, down)],
        out_specs=[tall(rows, channels), tall(rows, wide), tall(rows, channels)]
        + [pl.BlockSpec(array.shape, lambda i: (0, 0)) for array in sums],
        out_shape=[
            jax.ShapeDtypeStruct((pixels, channels), bf16),
            jax.ShapeDtypeStruct((pixels, wide), bf16),
            jax.ShapeDtypeStruct((pixels, channels), f32),
        ]
        + sums,
        compiler_params=room,
        name="mlp_backward",
    )(upstream, mixed, slope, sea, scales, up, down)


def weight_grads_kernel(grad_branch, normed, active, grad_hidden, out, branch_ref, normed_ref):
    @pl.when(pl.program_id(0) == 0)
    def _():
        branch_ref[...] = grad_branch[...].T
        normed_ref[...] = normed[...].T

    up = jnp.dot(normed_ref[...], grad_hidden[...], preferred_element_type=f32).astype(bf16)
    down = jnp.dot(branch_ref[...], active[...], preferred_element_type=f32).astype(bf16)
    for part in range(out.shape[1]):
        out[0, part] = up[:, part * lanes : (part + 1) * lanes]
        out[1, part] = down[:, part * lanes : (part + 1) * lanes]


def weight_grads(grad_branch, normed, active, grad_hidden):
    pixels, channels = normed.shape
    hidden = active.shape[1]
    tiles = pl.cdiv(hidden, lanes)
    parts = next(count for count in (5, 4, 3, 2, 1) if count == 2 or tiles % count == 0)
    return pl.pallas_call(
        weight_grads_kernel,
        grid=(pl.cdiv(tiles, parts),),
        in_specs=[fixed(grad_branch), fixed(normed)]
        + [pl.BlockSpec((pixels, parts * lanes), lambda tile: (0, tile))] * 2,
        out_specs=pl.BlockSpec((2, parts, channels, lanes), lambda tile: (0, tile, 0, 0)),
        out_shape=jax.ShapeDtypeStruct((2, tiles, channels, lanes), bf16),
        scratch_shapes=[pltpu.VMEM((channels, pixels), bf16)] * 2,
        compiler_params=room,
        name="weight_grads",
    )(grad_branch, normed, active, grad_hidden)


def unpack_kernel(core, own, other, up, down):
    mine, theirs = own[...].astype(f32), other[...].astype(f32)
    first = core[0] == 0
    up[...] = jnp.where(first, mine, theirs)
    down[...] = jnp.where(first, theirs, mine)


def unpack(core, own, other, channels, hidden):
    block = pl.BlockSpec((channels, lanes), lambda tile, core: (tile, 0))
    return pl.pallas_call(
        unpack_kernel,
        grid_spec=pltpu.PrefetchScalarGridSpec(
            num_scalar_prefetch=1,
            grid=(pl.cdiv(hidden, lanes),),
            in_specs=[block, block],
            out_specs=[pl.BlockSpec((channels, lanes), lambda tile, core: (0, tile))] * 2,
        ),
        out_shape=[jax.ShapeDtypeStruct((channels, hidden), f32)] * 2,
        compiler_params=room,
        name="unpack",
    )(core, own, other)


def swap(array, axis, step):
    return lax.ppermute(array, axis, [(i, i ^ step) for i in range(lax.axis_size(axis))])


def take(stacked, index):
    return lax.dynamic_index_in_dim(stacked, index, 0, keepdims=False)


def exchange_add(stacked, axis, own, scale):
    count = stacked.shape[0]
    got = [swap(take(stacked, own ^ step), axis, scale * step) for step in range(1, count)]
    total = take(stacked, own).astype(f32)
    for piece in got:
        total = total + piece.astype(f32)
    return total.astype(bf16)


def exchange_all(piece, axis, own, scale, count, event=None):
    got = [swap(piece, axis, scale * step) for step in range(1, count)]
    got = jnp.stack([piece] + (got if event is None else after(got, event)))
    return jnp.concatenate([take(got, own ^ place) for place in range(count)], axis=0)


def kept_and_sent(array, bit):
    pieces = array.reshape(2, -1, lanes)
    return take(pieces, bit), take(pieces, 1 - bit)


def low_sum(kept, got):
    return (kept.astype(f32) + got.astype(f32)).astype(bf16)


def in_order(bit, own, other):
    return jnp.where(bit == 0, jnp.concatenate([own, other]), jnp.concatenate([other, own]))


def reduce_over_cores(pair):
    unit = 16 * lax.axis_size("lat") * lax.axis_size("lon") // 2
    rows = pair.shape[1]
    pair = jnp.pad(pair, ((0, 0), (0, -rows % unit), (0, 0)))
    core = lax.axis_index("lon") % 2
    return low_sum(take(pair, core), swap(take(pair, 1 - core), "lon", 1))


def reduce_first(half):
    tile = lax.axis_index("lat")
    parts = []
    for share, step in zip((half[: half.shape[0] // 2], half[half.shape[0] // 2 :]), (1, 2)):
        kept, sent = kept_and_sent(share, tile // step % 2)
        parts.append((kept, swap(sent, "lat", step)))
    return [low_sum(kept, got) for kept, got in parts]


def reduce_second(shares):
    tile = lax.axis_index("lat")
    parts = []
    for share, step in zip(shares, (2, 1)):
        kept, sent = kept_and_sent(share, tile // step % 2)
        parts.append((kept, swap(sent, "lat", step)))
    return jnp.stack([low_sum(kept, got) for kept, got in parts])


def reduce_columns(shares):
    columns = lax.axis_size("lon") // 2
    column = lax.axis_index("lon") // 2
    pieces = shares.reshape(shares.shape[0], columns, -1, lanes).swapaxes(0, 1)
    return exchange_add(pieces, "lon", column, 2)


def spread_columns(share):
    columns = lax.axis_size("lon") // 2
    column = lax.axis_index("lon") // 2
    got = jnp.stack([share] + [swap(share, "lon", 2 * step) for step in range(1, columns)])
    whole = jnp.stack([take(got, column ^ place) for place in range(columns)], axis=1)
    return whole.reshape(share.shape[0], -1, lanes)


def spread_second(shares):
    tile = lax.axis_index("lat")
    return [
        in_order(tile // step % 2, share, swap(share, "lat", step)) for share, step in zip(shares, (2, 1))
    ]


def spread_first(shares):
    tile = lax.axis_index("lat")
    parts = [
        in_order(tile // step % 2, share, swap(share, "lat", step)) for share, step in zip(shares, (1, 2))
    ]
    return jnp.concatenate(parts)


def reduce_tiles(half):
    tiles = lax.axis_size("lat")
    return exchange_add(half.reshape(tiles, -1, lanes), "lat", lax.axis_index("lat"), 1)[None]


def spread_tiles(share):
    return exchange_all(share[0], "lat", lax.axis_index("lat"), 1, lax.axis_size("lat"))


def group_stages():
    two_by_two = lax.axis_size("lat") == 4
    return (
        [reduce_over_cores]
        + ([reduce_first, reduce_second] if two_by_two else [reduce_tiles])
        + [reduce_columns, spread_columns]
        + ([spread_second, spread_first] if two_by_two else [spread_tiles])
        + [lambda half: (half, swap(half, "lon", 1))]
    )


def sum_small(flat):
    count = lax.axis_size(both)
    rows = flat.shape[0]
    padded = -(-rows // (8 * count)) * 8 * count
    pieces = jnp.pad(flat, ((0, padded - rows), (0, 0))).reshape(count, -1, lanes)
    share = jnp.sum(lax.all_to_all(pieces, both, 0, 0, tiled=False), axis=0)
    copies = jnp.broadcast_to(share[None], pieces.shape)
    return lax.all_to_all(copies, both, 0, 0, tiled=False).reshape(padded, lanes)[:rows]


def cross_rows(former, latter):
    return lax.dot_general(former, latter, (((0,), (0,)), ((), ())), preferred_element_type=f32)


def by_transpose(former, latter):
    return lax.dot_general(former, latter, (((1,), (1,)), ((), ())), preferred_element_type=f32)


def block_mix(source, params, sea, ocean, dates, event=()):
    taps, gain, shift = params[:3]
    channels = source.shape[2]
    edges = borders(source, dates)
    mixed, local = stencil_forward(source, edges, taps, sea)
    totals = sum_all(jnp.concatenate([local, jnp.broadcast_to(ocean, (1, channels))]), event)
    first, square, ocean = totals
    mean = first / ocean
    factor = lax.rsqrt(square / ocean - mean * mean + epsilon)
    scales = jnp.stack([mean, factor, gain, shift])
    return source, edges, taps, mixed.reshape(-1, channels), scales, ocean


def block_forward(mix, params, sea, pooling=()):
    source, edges, taps, mixed, scales, ocean = mix
    up, up_bias, down, down_bias = params[3:]
    channels = source.shape[2]
    output, active, slope, normed, *coarse = mlp_forward(
        mixed,
        source.reshape(-1, channels),
        sea.reshape(-1, lanes),
        scales,
        up,
        up_bias,
        down,
        down_bias,
        pooling,
    )
    return output, coarse, mix + (normed, slope, active)


def block_hidden(upstream, params, sea, stored):
    scales, mixed, slope = stored[4], stored[3], stored[7]
    return mlp_backward(upstream, mixed, slope, sea.reshape(-1, lanes), scales, params[3], params[5])


def block_norm(grad_normed, local, sea, stored, dates):
    source, edges, taps, mixed, scales, ocean = stored[:6]
    channels = source.shape[2]
    grad_shift, grad_gain = sum_all(local)
    mean, factor, gain = scales[0], scales[1], scales[2]
    unit = (mixed - mean) * factor
    weight = spread(sea.reshape(-1, lanes), channels) / ocean
    grad_mixed = factor * (gain * grad_normed - weight * (gain * grad_shift + unit * (gain * grad_gain)))
    grad_mixed = grad_mixed.astype(bf16).reshape(source.shape)
    return grad_mixed, borders(grad_mixed, dates), grad_gain, grad_shift


def block_source(grad_mixed, grad_edges, upstream, sea, stored):
    source, taps = stored[0], stored[2]
    grad_source, sums = stencil_backward(grad_mixed, grad_edges, taps, sea, upstream.reshape(source.shape))
    return grad_source.reshape(-1, source.shape[2]), sums


def shards(
    fine_map,
    ocean_mask,
    out_grad,
    encode_depth,
    encode_gain,
    encode_shift,
    encode_up,
    encode_up_bias,
    encode_down,
    encode_down_bias,
    widen_weight,
    widen_bias,
    bottle_depth,
    bottle_gain,
    bottle_shift,
    bottle_up,
    bottle_up_bias,
    bottle_down,
    bottle_down_bias,
    merge_weight,
    merge_bias,
    decode_depth,
    decode_gain,
    decode_shift,
    decode_up,
    decode_up_bias,
    decode_down,
    decode_down_bias,
):
    dates, tile_rows, breadth, channels = fine_map.shape
    wide = bottle_depth.shape[2]
    extra = jnp.swapaxes(ocean_mask, 1, 2).astype(bf16)[:, None]
    extra = jnp.pad(extra, ((0, 0), (0, 0), (0, 0), (0, channels - tile_rows)))
    pieces = send_dates(jnp.concatenate([fine_map, extra], axis=1))
    kernels = (encode_depth, bottle_depth, decode_depth)
    rows = (encode_up_bias, encode_down_bias, bottle_up_bias, bottle_down_bias, decode_up_bias, decode_down_bias)
    small = (
        [kernel.astype(f32).reshape(49, -1) for kernel in kernels],
        [row.astype(f32)[None] for row in rows + (widen_bias, merge_bias)],
        [row.astype(f32) for row in (encode_gain, encode_shift, bottle_gain, bottle_shift, decode_gain, decode_shift)],
    )
    pieces, (taps, rows, norms) = lax.optimization_barrier((pieces, small))
    encode_up_bias, encode_down_bias, bottle_up_bias, bottle_down_bias, decode_up_bias, decode_down_bias = rows[:6]
    widen_bias, merge_bias = rows[6:]
    encode_norm, bottle_norm, decode_norm = [(taps[i], norms[2 * i], norms[2 * i + 1]) for i in range(3)]
    packed = to_dates(pieces).reshape(dates, tile_rows + 1, breadth, channels)
    fine = packed[:, :tile_rows].reshape(-1, breadth, channels)
    ocean_band = jnp.swapaxes(packed[:, tile_rows, :, :tile_rows], 1, 2).reshape(-1, breadth).astype(f32)
    height = fine.shape[0]
    half_height, half_breadth = height // 2, breadth // 2

    encode_up, encode_down = gathered_pair(encode_up, encode_down)
    bottle_up = gathered_by_columns(bottle_up)

    coarse_band = jnp.max(ocean_band.reshape(half_height, 2, half_breadth, 2), axis=(1, 3))
    sea_fine = jnp.broadcast_to(ocean_band[..., None], (height, breadth, lanes))
    sea_coarse = jnp.broadcast_to(coarse_band[..., None], (half_height, half_breadth, lanes))
    ocean_fine = jnp.sum(ocean_band)
    ocean_coarse = jnp.sum(coarse_band)
    parts = height * breadth // math.gcd(height * breadth, 384)
    pixel = np.arange(height * breadth // parts)
    block = pixel // breadth // 2 * half_breadth + pixel % breadth // 2
    members = jnp.asarray(block[:, None] == np.arange(pixel.size // 4), dtype=bf16)
    blocks = jnp.asarray(np.arange(pixel.size // 4)[:, None] == block, dtype=bf16)

    mix = block_mix(fine, encode_norm, sea_fine, ocean_fine, dates)
    encode = encode_norm + (encode_up, encode_up_bias, encode_down, encode_down_bias)
    widen_weight = gathered(after(widen_weight, mix[3]))
    skip_rows, (pooled, coarse_in), encode_stored = block_forward(
        mix, encode, sea_fine, (blocks, widen_weight, widen_bias)
    )
    decode_up = lax.all_gather(after(decode_up, skip_rows), "lat", axis=0, tiled=True)
    decode_down = lax.all_gather(after(decode_down, skip_rows), "lat", axis=0, tiled=True)
    decode = decode_norm + (decode_up, decode_up_bias, decode_down, decode_down_bias)
    bottle_down = gathered_by_rows(after(bottle_down, encode_stored[3]), skip_rows)
    bottle = bottle_norm + (bottle_up, bottle_up_bias, bottle_down, bottle_down_bias)
    coarse_in = coarse_in.reshape(half_height, half_breadth, wide)
    mix = block_mix(coarse_in, bottle, sea_coarse, ocean_coarse, dates, (bottle_up, bottle_down))
    coarse_low, _, coarse_stored = block_forward(mix, bottle, sea_coarse)
    merge_rows = merge_weight.shape[0]
    merge_weight = jnp.pad(after(merge_weight, skip_rows), ((0, -merge_rows % 16), (0, 0)))
    merge_weight = gathered(merge_weight, coarse_low).reshape(-1, merge_rows + -merge_rows % 16, channels)
    merge_weight = merge_weight[:, :merge_rows].reshape(-1, channels)
    upstream = send_dates(after(out_grad, mix[3]))
    merged = merge_forward(coarse_low, skip_rows, merge_weight, merge_bias, members, parts)
    mix = block_mix(merged.reshape(fine.shape), decode, sea_fine, ocean_fine, dates)
    upstream = to_dates(after(upstream, mix[3])).reshape(-1, channels)
    decode_rows, _, decode_stored = block_forward(mix, decode, sea_fine)
    result = from_dates(decode_rows.reshape(fine.shape), dates)

    grad_branch, grad_hidden, grad_normed, local, *decode_small = block_hidden(upstream, decode, sea_fine, decode_stored)
    early = [
        cross_rows(decode_stored[6], grad_hidden),
        cross_rows(grad_branch, decode_stored[8]),
    ]
    grad_mixed, grad_edges, *decode_total = block_norm(grad_normed, local, sea_fine, decode_stored, dates)
    decode_mixed = grad_mixed
    grad_merged, merge_sums = block_source(grad_mixed, grad_edges, upstream, sea_fine, decode_stored)

    block_sums, grad_coarse = merge_backward(grad_merged, merge_weight, blocks, wide, parts)
    early += [cross_rows(block_sums, coarse_low), cross_rows(grad_merged, skip_rows)]

    grad_branch, grad_hidden, grad_normed, local, *bottle_small = block_hidden(
        grad_coarse, bottle, sea_coarse, coarse_stored
    )
    decode_kernel = kernel_grad(*decode_stored[:2], after(decode_mixed, local))
    early += [cross_rows(coarse_stored[6], grad_hidden), cross_rows(grad_branch, coarse_stored[8])]
    early = lax.psum([part.astype(bf16) for part in early], both)
    early = [total.astype(f32) for total in early]
    decode_up_sum, decode_down_sum, bottle_up_sum, bottle_down_sum = early[0], early[1].T, early[4], early[5].T
    merge_sum = jnp.concatenate(early[2:4], axis=1).T
    grad_mixed, grad_edges, *bottle_total = block_norm(grad_normed, local, sea_coarse, coarse_stored, dates)
    bottle_kernel = kernel_grad(*coarse_stored[:2], grad_mixed)
    grad_wide, widen_sums = block_source(grad_mixed, grad_edges, grad_coarse, sea_coarse, coarse_stored)
    grad_skip = skip_backward(grad_merged, grad_wide, merge_weight, widen_weight, members, parts)

    grad_branch, grad_hidden, grad_normed, local, *encode_small = block_hidden(
        grad_skip, encode, sea_fine, encode_stored
    )
    encode_pair = weight_grads(grad_branch, encode_stored[6], encode_stored[8], grad_hidden).reshape(2, -1, lanes)
    grad_mixed, grad_edges, *encode_total = block_norm(grad_normed, local, sea_fine, encode_stored, dates)
    encode_kernel = kernel_grad(*encode_stored[:2], grad_mixed)
    grad_fine, _ = block_source(grad_mixed, grad_edges, grad_skip, sea_fine, encode_stored)
    core = (lax.axis_index("lon") % 2).astype(jnp.int32)[None]
    grad_widen = cross_rows(pooled, grad_wide).astype(bf16)
    widen_tiles = pl.cdiv(wide, 2 * lanes)
    grad_widen = jnp.pad(grad_widen, ((0, 0), (0, 2 * widen_tiles * lanes - wide)))
    grad_widen = grad_widen.reshape(channels, 2, widen_tiles, lanes).transpose(1, 2, 0, 3).reshape(2, -1, lanes)
    fine_grad = from_dates(grad_fine.reshape(fine.shape), dates)
    state = jnp.concatenate([encode_pair, grad_widen], axis=1)
    for stage in group_stages():
        state = stage(state)
    own, other = state
    encode_up_sum, encode_down_sum = unpack(core, own, other, channels, encode_up.shape[1])
    encode_down_sum = encode_down_sum.T
    start = encode_pair.shape[1]
    lower = jnp.where(core == 0, own[start : start + grad_widen.shape[1]], other[start : start + grad_widen.shape[1]])
    upper = jnp.where(core == 0, other[start : start + grad_widen.shape[1]], own[start : start + grad_widen.shape[1]])
    widen_sum = jnp.stack([lower, upper]).reshape(2 * widen_tiles, channels, lanes).astype(f32)
    widen_sum = widen_sum.transpose(1, 0, 2).reshape(channels, -1)[:, :wide]

    kernels = [encode_kernel, bottle_kernel, decode_kernel]
    rows = [encode_small, (widen_sums,), bottle_small, (merge_sums,), decode_small]
    rows = [row for group in rows for row in group]
    padded = [jnp.pad(row, ((0, 0), (0, -row.shape[1] % lanes))) for row in rows]
    line = jnp.concatenate(padded, axis=1)
    small = sum_small(jnp.concatenate([array.reshape(-1, lanes) for array in kernels] + [line.reshape(-1, lanes)]))
    kernel_sums, at = [], 0
    for array, shape in zip(kernels, (encode_depth.shape, bottle_depth.shape, decode_depth.shape)):
        count = array.shape[0] * 56
        total = small[at : at + count].reshape(array.shape)[:, :49].transpose(1, 0, 2).reshape(49, -1)
        kernel_sums.append(total[:, : shape[2]].reshape(shape))
        at += count
    line = small[at:].reshape(-1)
    row_sums, at = [], 0
    for row, wider in zip(rows, padded):
        row_sums.append(line[at : at + row.shape[1]])
        at += wider.shape[1]
    (encode_upb, encode_downb, widen_b, bottle_upb, bottle_downb, bottle_merge_b, decode_upb, decode_downb) = (
        row_sums[1],
        row_sums[0],
        row_sums[2],
        row_sums[4],
        row_sums[3],
        row_sums[5],
        row_sums[7],
        row_sums[6],
    )
    return (
        result,
        fine_grad,
        kernel_sums[0],
        encode_total[0],
        encode_total[1],
        encode_up_sum,
        encode_upb,
        encode_down_sum,
        encode_downb,
        widen_sum,
        widen_b,
        kernel_sums[1],
        bottle_total[0],
        bottle_total[1],
        bottle_up_sum,
        bottle_upb,
        bottle_down_sum,
        bottle_downb,
        merge_sum,
        bottle_merge_b,
        kernel_sums[2],
        decode_total[0],
        decode_total[1],
        decode_up_sum,
        decode_upb,
        decode_down_sum,
        decode_downb,
    )


def solution(mesh):
    whole = P()
    rows = P("lat", None)
    tile = P(None, "lat", "lon", None)
    block = (whole, whole, whole, rows, whole, rows, whole)
    placed = (tile, P(None, "lat", "lon"), tile) + block + (rows, whole) + block + (rows, whole) + block
    return jax.shard_map(
        shards,
        mesh=mesh,
        in_specs=placed,
        out_specs=(tile, tile) + (whole,) * 25,
        check_vma=False,
    )
```

```python
import functools
import math

import jax
import jax.numpy as jnp
import numpy as np
from jax import lax
from jax.experimental import pallas as pl
from jax.experimental.pallas import tpu as pltpu
from jax.sharding import PartitionSpec as P

epsilon = 1e-05
both = ("lat", "lon")
bf16 = jnp.bfloat16
f32 = jnp.float32
lanes = 128
strip = 12
room = pltpu.CompilerParams(vmem_limit_bytes=56 << 20)


def exchange_pairs(count, group, step):
    return [(i, (i // group) * group + ((i % group) ^ step)) for i in range(count)]


def send_dates(tiles):
    dates, count = tiles.shape[0], lax.axis_size("lat")
    own = lax.axis_index("lat") % dates
    pieces = [lax.dynamic_index_in_dim(tiles, own, 0, keepdims=False)]
    for step in range(1, dates):
        pieces.append(
            lax.ppermute(
                lax.dynamic_index_in_dim(tiles, own ^ step, 0, keepdims=False),
                "lat",
                exchange_pairs(count, dates, step),
            )
        )
    return pieces


def to_dates(pieces):
    dates = len(pieces)
    own = lax.axis_index("lat") % dates
    stacked = jnp.stack(pieces)
    ordered = [lax.dynamic_index_in_dim(stacked, own ^ tile, 0, keepdims=False) for tile in range(dates)]
    return jnp.concatenate(ordered, axis=0)


def from_dates(band, dates):
    count = lax.axis_size("lat")
    own = lax.axis_index("lat") % dates
    tiles = band.reshape((dates, band.shape[0] // dates) + band.shape[1:])
    pieces = [lax.dynamic_index_in_dim(tiles, own, 0, keepdims=False)]
    for step in range(1, dates):
        pieces.append(
            lax.ppermute(
                lax.dynamic_index_in_dim(tiles, own ^ step, 0, keepdims=False),
                "lat",
                exchange_pairs(count, dates, step),
            )
        )
    stacked = jnp.stack(pieces)
    return jnp.stack([lax.dynamic_index_in_dim(stacked, own ^ date, 0, keepdims=False) for date in range(dates)])


def after(array, event):
    return lax.optimization_barrier((array, event))[0]


def gathered(shard, event=None):
    return exchange_all(shard, "lat", lax.axis_index("lat"), 1, lax.axis_size("lat"), event)


def assemble(kernel, name, shape, arrays, copies):
    tile, core = lax.axis_index("lat"), lax.axis_index("lon") % 2
    return pl.pallas_call(
        kernel,
        in_specs=[pl.BlockSpec(memory_space=pltpu.SMEM)] + [pl.BlockSpec(memory_space=pl.ANY)] * len(arrays),
        out_specs=pl.BlockSpec(memory_space=pltpu.VMEM),
        out_shape=jax.ShapeDtypeStruct(shape, bf16),
        scratch_shapes=[pltpu.SemaphoreType.DMA((copies,))],
        compiler_params=room,
        name=name,
    )(jnp.stack([tile, core]).astype(jnp.int32), *arrays)


def finish(copies):
    for copy in copies:
        copy.start()
    for copy in copies:
        copy.wait()


def assemble_rows_kernel(place, shard, mine, theirs, out, sems):
    tile, core = place[0], place[1]
    rows = shard.shape[0]
    half = rows // 2
    copies = [(shard, tile * rows, rows)]
    for step in range(1, mine.shape[0] + 1):
        start = (tile ^ step) * rows
        copies.append((mine.at[step - 1], start + core * half, half))
        copies.append((theirs.at[step - 1], start + (1 - core) * half, half))
    finish(
        [
            pltpu.make_async_copy(source, out.at[pl.ds(pl.multiple_of(start, 8), count)], sems.at[index])
            for index, (source, start, count) in enumerate(copies)
        ]
    )


def assemble_columns_kernel(place, mine, theirs, out, sems):
    start = out.shape[1] - mine.shape[1]

    def join(low, high):
        finish(
            [
                pltpu.make_async_copy(low.at[:, :start], out.at[:, :start], sems.at[0]),
                pltpu.make_async_copy(high, out.at[:, start:], sems.at[1]),
            ]
        )

    @pl.when(place[1] == 0)
    def _():
        join(mine, theirs)

    @pl.when(place[1] != 0)
    def _():
        join(theirs, mine)


def gathered_by_rows(shard, event):
    tiles = lax.axis_size("lat")
    half = take(shard.reshape(2, -1, shard.shape[1]), lax.axis_index("lon") % 2)
    mine = jnp.stack(after([swap(half, "lat", step) for step in range(1, tiles)], event))
    shape = (tiles * shard.shape[0], shard.shape[1])
    return assemble(assemble_rows_kernel, "assemble_rows", shape, (shard, mine, swap(mine, "lon", 1)), 2 * tiles - 1)


def gathered_by_columns(shard, event):
    columns = shard.shape[1]
    start = columns // 2 // lanes * lanes
    half = lax.dynamic_slice_in_dim(shard, lax.axis_index("lon") % 2 * start, columns - start, axis=1)
    mine = after(lax.all_gather(half, "lat", axis=0, tiled=True), event)
    return assemble(
        assemble_columns_kernel, "assemble_columns", (mine.shape[0], columns), (mine, swap(mine, "lon", 1)), 2
    )


def gathered_pair(up, down, event):
    channels = down.shape[1]
    first = lax.axis_index("lon") % 2 == 0
    mine = lax.all_gather(jnp.where(first, up.reshape(-1, channels), down), "lat", axis=0, tiled=True)
    mine = after(mine, event)
    theirs = swap(mine, "lon", 1)
    return jnp.where(first, mine, theirs).reshape(-1, up.shape[1]), jnp.where(first, theirs, mine)


def borders(source, dates):
    count = lax.axis_size("lon")
    forward = [(i, (i + 1) % count) for i in range(count)]
    backward = [(target, origin) for origin, target in forward]
    left = lax.ppermute(source[:, -3:], "lon", forward)
    right = lax.ppermute(source[:, :3], "lon", backward)
    tiles = lax.axis_size("lat")
    if tiles == dates:
        return left, right
    down = [(i, i + dates) for i in range(tiles - dates)]
    up = [(target, origin) for origin, target in down]
    last = jnp.concatenate([left[-3:], source[-3:], right[-3:]], axis=1)
    first = jnp.concatenate([left[:3], source[:3], right[:3]], axis=1)
    return left, right, lax.ppermute(last, "lat", down), lax.ppermute(first, "lat", up)


def sum_all(local, event=()):
    count = lax.axis_size(both)
    copies = jnp.broadcast_to(local[None], (count,) + local.shape)
    return jnp.sum(after(lax.all_to_all(copies, both, 0, 0, tiled=False), event), axis=0)


def fill_extended(wide_ref, centre, edges):
    rows, columns = centre.shape[0], centre.shape[1]
    blank = jnp.zeros((3, columns + 16, lanes), f32)
    wide_ref[0:3] = blank
    wide_ref[rows + 3 :] = blank
    wide_ref[3 : rows + 3, 8 : columns + 8] = centre[...].astype(f32)
    wide_ref[3 : rows + 3, 5:8] = edges[0][...].astype(f32)
    wide_ref[3 : rows + 3, columns + 8 : columns + 11] = edges[1][...].astype(f32)
    if len(edges) > 2:
        wide_ref[0:3, 5 : columns + 11] = edges[2][...].astype(f32)
        wide_ref[rows + 3 :, 5 : columns + 11] = edges[3][...].astype(f32)


def strip_sum(wide_ref, taps, top, start, flipped):
    total = None
    for column in range(7):
        window = wide_ref[pl.ds(top, strip + 6), start + 5 + column : start + 13 + column, :]
        for across in range(7):
            place = 7 * across + column
            tap = taps[pl.ds(48 - place if flipped else place, 8, stride=0), :]
            term = window[across : across + strip] * tap[None]
            total = term if total is None else total + term
    return total


def stencil_forward_kernel(edge_count, source, *refs):
    edges = refs[:edge_count]
    taps, sea, mixed, sums, wide_ref = refs[edge_count:]
    rows, columns = source.shape[0], source.shape[1]
    fill_extended(wide_ref, source, edges)

    def step(index, carry):
        first, square = carry
        top = index * strip
        for start in range(0, columns, 8):
            here = (pl.ds(top, strip), slice(start, start + 8))
            total = strip_sum(wide_ref, taps, top, start, False)
            mixed[here] = total
            masked = total * sea[here]
            first = first + jnp.sum(masked, axis=0)
            square = square + jnp.sum(masked * total, axis=0)
        return first, square

    zero = jnp.zeros((8, lanes), f32)
    first, square = lax.fori_loop(0, rows // strip, step, (zero, zero))
    sums[0:1] = jnp.sum(first, axis=0, keepdims=True)
    sums[1:2] = jnp.sum(square, axis=0, keepdims=True)


def stencil_backward_kernel(edge_count, grad, *refs):
    edges = refs[:edge_count]
    taps, sea, upstream, out, sums, wide_ref = refs[edge_count:]
    rows, columns = grad.shape[0], grad.shape[1]
    fill_extended(wide_ref, grad, edges)

    def step(index, first):
        top = index * strip
        for start in range(0, columns, 8):
            here = (pl.ds(top, strip), slice(start, start + 8))
            total = strip_sum(wide_ref, taps, top, start, True)
            low = (total + upstream[here].astype(f32) * sea[here]).astype(bf16)
            out[here] = low
            first = first + jnp.sum(low.astype(f32), axis=0)
        return first

    first = lax.fori_loop(0, rows // strip, step, jnp.zeros((8, lanes), f32))
    sums[...] = jnp.sum(first, axis=0, keepdims=True)


def kernel_grad_kernel(edge_count, source, *refs):
    edges = refs[:edge_count]
    grad, out, wide_ref, sums_ref = refs[edge_count:]
    rows, columns = source.shape[0], source.shape[1]
    fill_extended(wide_ref, source, edges)
    sums_ref[...] = jnp.zeros_like(sums_ref)

    def step(index, carry):
        top = index * strip
        for start in range(0, columns, 8):
            upstream = grad[pl.ds(top, strip), start : start + 8, :].astype(f32)
            for column in range(7):
                window = wide_ref[pl.ds(top, strip + 6), start + 5 + column : start + 13 + column, :]
                for across in range(7):
                    sums_ref[7 * across + column] += jnp.sum(window[across : across + strip] * upstream, axis=0)
        return carry

    lax.fori_loop(0, rows // strip, step, 0)
    out[0, 0:49] = jnp.sum(sums_ref[...], axis=1)
    out[0, 49:56] = jnp.zeros((7, lanes), f32)


def by_channel(array):
    rest = array.shape[:-1]
    return pl.BlockSpec(rest + (lanes,), lambda tile: (0,) * len(rest) + (tile,))


def same_block(array):
    return pl.BlockSpec(array.shape, lambda tile: (0,) * array.ndim)


def wide_scratch(rows, columns):
    return pltpu.VMEM((rows + 6, columns + 16, lanes), f32)


def stencil_forward(source, edges, taps, sea):
    rows, columns, channels = source.shape
    sums = jax.ShapeDtypeStruct((2, channels), f32)
    mixed = jax.ShapeDtypeStruct(source.shape, f32)
    return pl.pallas_call(
        functools.partial(stencil_forward_kernel, len(edges)),
        grid=(pl.cdiv(channels, lanes),),
        in_specs=[by_channel(array) for array in (source, *edges, taps)] + [same_block(sea)],
        out_specs=[by_channel(mixed), by_channel(sums)],
        out_shape=[mixed, sums],
        scratch_shapes=[wide_scratch(rows, columns)],
        compiler_params=room,
        name="stencil_forward",
    )(source, *edges, taps, sea)


def stencil_backward(grad, edges, taps, sea, upstream):
    rows, columns, channels = grad.shape
    out = jax.ShapeDtypeStruct(grad.shape, bf16)
    sums = jax.ShapeDtypeStruct((1, channels), f32)
    return pl.pallas_call(
        functools.partial(stencil_backward_kernel, len(edges)),
        grid=(pl.cdiv(channels, lanes),),
        in_specs=[by_channel(array) for array in (grad, *edges, taps)] + [same_block(sea), by_channel(upstream)],
        out_specs=[by_channel(out), by_channel(sums)],
        out_shape=[out, sums],
        scratch_shapes=[wide_scratch(rows, columns)],
        compiler_params=room,
        name="stencil_backward",
    )(grad, *edges, taps, sea, upstream)


def kernel_grad(source, edges, grad):
    rows, columns, channels = source.shape
    tiles = pl.cdiv(channels, lanes)
    out = jax.ShapeDtypeStruct((tiles, 56, lanes), f32)
    return pl.pallas_call(
        functools.partial(kernel_grad_kernel, len(edges)),
        grid=(tiles,),
        in_specs=[by_channel(array) for array in (source, *edges, grad)],
        out_specs=pl.BlockSpec((1, 56, lanes), lambda tile: (tile, 0, 0)),
        out_shape=out,
        scratch_shapes=[wide_scratch(rows, columns), pltpu.VMEM((49, 8, lanes), f32)],
        compiler_params=room,
        name="kernel_grad",
    )(source, *edges, grad)


def chunks_of(width, size):
    edges = list(range(0, width, size))
    if len(edges) > 1 and width - edges[-1] < size // 2:
        edges.pop()
    return list(zip(edges, edges[1:] + [width]))


def spread(sea, channels):
    return jnp.concatenate([sea] * pl.cdiv(channels, lanes), axis=1)[:, :channels]


def gelu_pair(hidden):
    below = 0.5 + 0.5 * lax.erf(hidden * math.sqrt(0.5))
    density = jnp.exp(-0.5 * hidden * hidden) * (1.0 / math.sqrt(2.0 * math.pi))
    return hidden * below, below + hidden * density


def mlp_forward_kernel(
    size, mixed, source, sea, scales, up, up_bias, down, down_bias, *refs
):
    unit = (mixed[...] - scales[0:1]) * scales[1:2]
    low = (unit * scales[2:3] + scales[3:4]).astype(bf16)
    out, active, slope, normed = refs[-4:] if len(refs) == 4 else refs[3:7]
    normed[...] = low
    branch = down_bias[...]
    for a, b in chunks_of(up.shape[1], size):
        hidden = jnp.dot(low, up[:, a:b], preferred_element_type=f32) + up_bias[:, a:b]
        value, rise = gelu_pair(hidden)
        value = value.astype(bf16)
        active[:, a:b] = value
        slope[:, a:b] = rise.astype(bf16)
        branch = branch + jnp.dot(value, down[a:b, :], preferred_element_type=f32)
    mask = spread(sea[...], out.shape[1])
    result = (mask * (source[...].astype(f32) + branch)).astype(bf16)
    out[...] = result
    if len(refs) > 4:
        blocks, widen, widen_bias = refs[:3]
        pooled, coarse = refs[7:]
        mean = (0.25 * jnp.dot(blocks[...], result, preferred_element_type=f32)).astype(bf16)
        pooled[...] = mean
        coarse[...] = (jnp.dot(mean, widen[...], preferred_element_type=f32) + widen_bias[...]).astype(bf16)


def merge_forward_kernel(coarse, skip, merge, bias, members, merged):
    wide = coarse.shape[1]
    upper = jnp.dot(coarse[...], merge[:wide, :], preferred_element_type=f32)
    high = upper.astype(bf16)
    rest = (upper - high.astype(f32)).astype(bf16)
    total = jnp.dot(members[...], high, preferred_element_type=f32)
    total = total + jnp.dot(members[...], rest, preferred_element_type=f32)
    total = total + jnp.dot(skip[...], merge[wide:, :], preferred_element_type=f32)
    merged[...] = (total + bias[...]).astype(bf16)


def merge_backward_kernel(grad, merge, blocks, block_sums, grad_coarse):
    wide = grad_coarse.shape[1]
    low = jnp.dot(blocks[...], grad[...], preferred_element_type=f32).astype(bf16)
    block_sums[...] = low
    grad_coarse[...] = lax.dot_general(
        low, merge[:wide, :], (((1,), (1,)), ((), ())), preferred_element_type=f32
    )


def skip_backward_kernel(grad, grad_wide, merge, widen, members, grad_skip):
    wide = grad_wide.shape[1]
    pooled = 0.25 * lax.dot_general(
        grad_wide[...], widen[...], (((1,), (1,)), ((), ())), preferred_element_type=f32
    )
    high = pooled.astype(bf16)
    rest = (pooled - high.astype(f32)).astype(bf16)
    total = lax.dot_general(grad[...], merge[wide:, :], (((1,), (1,)), ((), ())), preferred_element_type=f32)
    total = total + jnp.dot(members[...], high, preferred_element_type=f32)
    grad_skip[...] = total + jnp.dot(members[...], rest, preferred_element_type=f32)


def mlp_backward_kernel(
    size,
    upstream,
    mixed,
    slope,
    sea,
    scales,
    up,
    down,
    grad_branch,
    grad_hidden,
    grad_normed,
    sums,
    down_sums,
    up_sums,
):
    @pl.when(pl.program_id(0) == 0)
    def _():
        sums[...] = jnp.zeros_like(sums)
        down_sums[...] = jnp.zeros_like(down_sums)
        up_sums[...] = jnp.zeros_like(up_sums)

    mask = spread(sea[...], upstream.shape[1])
    low = (mask * upstream[...].astype(f32)).astype(bf16)
    grad_branch[...] = low
    down_sums[...] += jnp.sum(low.astype(f32), axis=0, keepdims=True)
    normed = None
    for a, b in chunks_of(up.shape[1], size):
        grad_active = lax.dot_general(low, down[a:b, :], (((1,), (1,)), ((), ())), preferred_element_type=f32)
        hidden = (grad_active * slope[:, a:b].astype(f32)).astype(bf16)
        grad_hidden[:, a:b] = hidden
        up_sums[:, a:b] += jnp.sum(hidden.astype(f32), axis=0, keepdims=True)
        part = lax.dot_general(hidden, up[:, a:b], (((1,), (1,)), ((), ())), preferred_element_type=f32)
        normed = part if normed is None else normed + part
    grad_normed[...] = normed
    unit = (mixed[...] - scales[0:1]) * scales[1:2]
    sums[0:1] += jnp.sum(normed, axis=0, keepdims=True)
    sums[1:2] += jnp.sum(normed * unit, axis=0, keepdims=True)


def tall(rows, width):
    return pl.BlockSpec((rows, width), lambda i: (i, 0))


def fixed(array):
    return pl.BlockSpec(array.shape, lambda i: (0, 0), pipeline_mode=pl.Buffered(1))


def by_rows(parts, array):
    return tall(array.shape[0] // parts, array.shape[1])


def mlp_forward(mixed, source, sea, scales, up, up_bias, down, down_bias, pooling=()):
    pixels, channels = mixed.shape
    wide = up.shape[1]
    rows = math.gcd(pixels, 384)
    parts = pixels // rows
    shapes = [(pixels, width) for width in (channels, wide, wide, channels)]
    if pooling:
        shapes += [(pixels // 4, channels), (pixels // 4, pooling[1].shape[1])]
    outs = [jax.ShapeDtypeStruct(shape, bf16) for shape in shapes]
    return pl.pallas_call(
        functools.partial(mlp_forward_kernel, 512),
        grid=(parts,),
        in_specs=[by_rows(parts, array) for array in (mixed, source, sea)]
        + [fixed(array) for array in (scales, up, up_bias, down, down_bias, *pooling)],
        out_specs=[by_rows(parts, out) for out in outs],
        out_shape=outs,
        compiler_params=room,
        name="mlp_forward",
    )(mixed, source, sea, scales, up, up_bias, down, down_bias, *pooling)


def merge_forward(coarse, skip, merge, bias, members, parts):
    merged = jax.ShapeDtypeStruct(skip.shape, bf16)
    return pl.pallas_call(
        merge_forward_kernel,
        grid=(parts,),
        in_specs=[by_rows(parts, array) for array in (coarse, skip)]
        + [fixed(array) for array in (merge, bias, members)],
        out_specs=by_rows(parts, merged),
        out_shape=merged,
        compiler_params=room,
        name="merge_forward",
    )(coarse, skip, merge, bias, members)


def merge_backward(grad, merge, blocks, wide, parts):
    pixels, channels = grad.shape
    block_sums = jax.ShapeDtypeStruct((pixels // 4, channels), bf16)
    grad_coarse = jax.ShapeDtypeStruct((pixels // 4, wide), f32)
    return pl.pallas_call(
        merge_backward_kernel,
        grid=(parts,),
        in_specs=[by_rows(parts, grad), fixed(merge), fixed(blocks)],
        out_specs=[by_rows(parts, block_sums), by_rows(parts, grad_coarse)],
        out_shape=[block_sums, grad_coarse],
        compiler_params=room,
        name="merge_backward",
    )(grad, merge, blocks)


def skip_backward(grad, grad_wide, merge, widen, members, parts):
    grad_skip = jax.ShapeDtypeStruct(grad.shape, f32)
    return pl.pallas_call(
        skip_backward_kernel,
        grid=(parts,),
        in_specs=[by_rows(parts, array) for array in (grad, grad_wide)]
        + [fixed(array) for array in (merge, widen, members)],
        out_specs=by_rows(parts, grad_skip),
        out_shape=grad_skip,
        compiler_params=room,
        name="skip_backward",
    )(grad, grad_wide, merge, widen, members)


def mlp_backward(upstream, mixed, slope, sea, scales, up, down):
    pixels, channels = mixed.shape
    wide = up.shape[1]
    rows = math.gcd(pixels, 384)
    sums = [jax.ShapeDtypeStruct(shape, f32) for shape in ((2, channels), (1, channels), (1, wide))]
    return pl.pallas_call(
        functools.partial(mlp_backward_kernel, 512),
        grid=(pixels // rows,),
        in_specs=[tall(rows, channels), tall(rows, channels), tall(rows, wide), tall(rows, lanes)]
        + [fixed(array) for array in (scales, up, down)],
        out_specs=[tall(rows, channels), tall(rows, wide), tall(rows, channels)]
        + [pl.BlockSpec(array.shape, lambda i: (0, 0)) for array in sums],
        out_shape=[
            jax.ShapeDtypeStruct((pixels, channels), bf16),
            jax.ShapeDtypeStruct((pixels, wide), bf16),
            jax.ShapeDtypeStruct((pixels, channels), f32),
        ]
        + sums,
        compiler_params=room,
        name="mlp_backward",
    )(upstream, mixed, slope, sea, scales, up, down)


def weight_grads_kernel(grad_branch, normed, active, grad_hidden, out, branch_ref, normed_ref):
    @pl.when(pl.program_id(0) == 0)
    def _():
        branch_ref[...] = grad_branch[...].T
        normed_ref[...] = normed[...].T

    up = jnp.dot(normed_ref[...], grad_hidden[...], preferred_element_type=f32).astype(bf16)
    down = jnp.dot(branch_ref[...], active[...], preferred_element_type=f32).astype(bf16)
    for part in range(out.shape[1]):
        out[0, part] = up[:, part * lanes : (part + 1) * lanes]
        out[1, part] = down[:, part * lanes : (part + 1) * lanes]


def weight_grads(grad_branch, normed, active, grad_hidden):
    pixels, channels = normed.shape
    hidden = active.shape[1]
    tiles = pl.cdiv(hidden, lanes)
    parts = next(count for count in (5, 4, 3, 2, 1) if count == 2 or tiles % count == 0)
    return pl.pallas_call(
        weight_grads_kernel,
        grid=(pl.cdiv(tiles, parts),),
        in_specs=[fixed(grad_branch), fixed(normed)]
        + [pl.BlockSpec((pixels, parts * lanes), lambda tile: (0, tile))] * 2,
        out_specs=pl.BlockSpec((2, parts, channels, lanes), lambda tile: (0, tile, 0, 0)),
        out_shape=jax.ShapeDtypeStruct((2, tiles, channels, lanes), bf16),
        scratch_shapes=[pltpu.VMEM((channels, pixels), bf16)] * 2,
        compiler_params=room,
        name="weight_grads",
    )(grad_branch, normed, active, grad_hidden)


def unpack_kernel(core, own, other, up, down):
    mine, theirs = own[...].astype(f32), other[...].astype(f32)
    first = core[0] == 0
    up[...] = jnp.where(first, mine, theirs)
    down[...] = jnp.where(first, theirs, mine)


def unpack(core, own, other, channels, hidden):
    block = pl.BlockSpec((channels, lanes), lambda tile, core: (tile, 0))
    return pl.pallas_call(
        unpack_kernel,
        grid_spec=pltpu.PrefetchScalarGridSpec(
            num_scalar_prefetch=1,
            grid=(pl.cdiv(hidden, lanes),),
            in_specs=[block, block],
            out_specs=[pl.BlockSpec((channels, lanes), lambda tile, core: (0, tile))] * 2,
        ),
        out_shape=[jax.ShapeDtypeStruct((channels, hidden), f32)] * 2,
        compiler_params=room,
        name="unpack",
    )(core, own, other)


def swap(array, axis, step):
    return lax.ppermute(array, axis, [(i, i ^ step) for i in range(lax.axis_size(axis))])


def take(stacked, index):
    return lax.dynamic_index_in_dim(stacked, index, 0, keepdims=False)


def exchange_add(stacked, axis, own, scale):
    count = stacked.shape[0]
    got = [swap(take(stacked, own ^ step), axis, scale * step) for step in range(1, count)]
    total = take(stacked, own).astype(f32)
    for piece in got:
        total = total + piece.astype(f32)
    return total.astype(bf16)


def exchange_all(piece, axis, own, scale, count, event=None):
    got = [swap(piece, axis, scale * step) for step in range(1, count)]
    got = jnp.stack([piece] + (got if event is None else after(got, event)))
    return jnp.concatenate([take(got, own ^ place) for place in range(count)], axis=0)


def kept_and_sent(array, bit):
    pieces = array.reshape(2, -1, lanes)
    return take(pieces, bit), take(pieces, 1 - bit)


def low_sum(kept, got):
    return (kept.astype(f32) + got.astype(f32)).astype(bf16)


def in_order(bit, own, other):
    return jnp.where(bit == 0, jnp.concatenate([own, other]), jnp.concatenate([other, own]))


def reduce_over_cores(pair):
    unit = 16 * lax.axis_size("lat") * lax.axis_size("lon") // 2
    rows = pair.shape[1]
    pair = jnp.pad(pair, ((0, 0), (0, -rows % unit), (0, 0)))
    core = lax.axis_index("lon") % 2
    return low_sum(take(pair, core), swap(take(pair, 1 - core), "lon", 1))


def reduce_first(half):
    tile = lax.axis_index("lat")
    parts = []
    for share, step in zip((half[: half.shape[0] // 2], half[half.shape[0] // 2 :]), (1, 2)):
        kept, sent = kept_and_sent(share, tile // step % 2)
        parts.append((kept, swap(sent, "lat", step)))
    return [low_sum(kept, got) for kept, got in parts]


def reduce_second(shares):
    tile = lax.axis_index("lat")
    parts = []
    for share, step in zip(shares, (2, 1)):
        kept, sent = kept_and_sent(share, tile // step % 2)
        parts.append((kept, swap(sent, "lat", step)))
    return jnp.stack([low_sum(kept, got) for kept, got in parts])


def reduce_columns(shares):
    columns = lax.axis_size("lon") // 2
    column = lax.axis_index("lon") // 2
    pieces = shares.reshape(shares.shape[0], columns, -1, lanes).swapaxes(0, 1)
    return exchange_add(pieces, "lon", column, 2)


def spread_columns(share):
    columns = lax.axis_size("lon") // 2
    column = lax.axis_index("lon") // 2
    got = jnp.stack([share] + [swap(share, "lon", 2 * step) for step in range(1, columns)])
    whole = jnp.stack([take(got, column ^ place) for place in range(columns)], axis=1)
    return whole.reshape(share.shape[0], -1, lanes)


def spread_second(shares):
    tile = lax.axis_index("lat")
    return [
        in_order(tile // step % 2, share, swap(share, "lat", step)) for share, step in zip(shares, (2, 1))
    ]


def spread_first(shares):
    tile = lax.axis_index("lat")
    parts = [
        in_order(tile // step % 2, share, swap(share, "lat", step)) for share, step in zip(shares, (1, 2))
    ]
    return jnp.concatenate(parts)


def reduce_tiles(half):
    tiles = lax.axis_size("lat")
    return exchange_add(half.reshape(tiles, -1, lanes), "lat", lax.axis_index("lat"), 1)[None]


def spread_tiles(share):
    return exchange_all(share[0], "lat", lax.axis_index("lat"), 1, lax.axis_size("lat"))


def group_stages():
    two_by_two = lax.axis_size("lat") == 4
    return (
        [reduce_over_cores]
        + ([reduce_first, reduce_second] if two_by_two else [reduce_tiles])
        + [reduce_columns, spread_columns]
        + ([spread_second, spread_first] if two_by_two else [spread_tiles])
        + [lambda half: (half, swap(half, "lon", 1))]
    )


def sum_small(flat):
    count = lax.axis_size(both)
    rows = flat.shape[0]
    padded = -(-rows // (8 * count)) * 8 * count
    pieces = jnp.pad(flat, ((0, padded - rows), (0, 0))).reshape(count, -1, lanes)
    share = jnp.sum(lax.all_to_all(pieces, both, 0, 0, tiled=False), axis=0)
    copies = jnp.broadcast_to(share[None], pieces.shape)
    return lax.all_to_all(copies, both, 0, 0, tiled=False).reshape(padded, lanes)[:rows]


def cross_rows(former, latter):
    return lax.dot_general(former, latter, (((0,), (0,)), ((), ())), preferred_element_type=f32)


def by_transpose(former, latter):
    return lax.dot_general(former, latter, (((1,), (1,)), ((), ())), preferred_element_type=f32)


def block_mix(source, params, sea, ocean, dates, event=()):
    taps, gain, shift = params[:3]
    channels = source.shape[2]
    edges = borders(source, dates)
    mixed, local = stencil_forward(source, edges, taps, sea)
    totals = sum_all(jnp.concatenate([local, jnp.broadcast_to(ocean, (1, channels))]), event)
    first, square, ocean = totals
    mean = first / ocean
    factor = lax.rsqrt(square / ocean - mean * mean + epsilon)
    scales = jnp.stack([mean, factor, gain, shift])
    return source, edges, taps, mixed.reshape(-1, channels), scales, ocean


def block_forward(mix, params, sea, pooling=()):
    source, edges, taps, mixed, scales, ocean = mix
    up, up_bias, down, down_bias = params[3:]
    channels = source.shape[2]
    output, active, slope, normed, *coarse = mlp_forward(
        mixed,
        source.reshape(-1, channels),
        sea.reshape(-1, lanes),
        scales,
        up,
        up_bias,
        down,
        down_bias,
        pooling,
    )
    return output, coarse, mix + (normed, slope, active)


def block_hidden(upstream, params, sea, stored):
    scales, mixed, slope = stored[4], stored[3], stored[7]
    return mlp_backward(upstream, mixed, slope, sea.reshape(-1, lanes), scales, params[3], params[5])


def block_norm(grad_normed, local, sea, stored, dates):
    source, edges, taps, mixed, scales, ocean = stored[:6]
    channels = source.shape[2]
    grad_shift, grad_gain = sum_all(local)
    mean, factor, gain = scales[0], scales[1], scales[2]
    unit = (mixed - mean) * factor
    weight = spread(sea.reshape(-1, lanes), channels) / ocean
    grad_mixed = factor * (gain * grad_normed - weight * (gain * grad_shift + unit * (gain * grad_gain)))
    grad_mixed = grad_mixed.astype(bf16).reshape(source.shape)
    return grad_mixed, borders(grad_mixed, dates), grad_gain, grad_shift


def block_source(grad_mixed, grad_edges, upstream, sea, stored):
    source, taps = stored[0], stored[2]
    grad_source, sums = stencil_backward(grad_mixed, grad_edges, taps, sea, upstream.reshape(source.shape))
    return grad_source.reshape(-1, source.shape[2]), sums


def shards(
    fine_map,
    ocean_mask,
    out_grad,
    encode_depth,
    encode_gain,
    encode_shift,
    encode_up,
    encode_up_bias,
    encode_down,
    encode_down_bias,
    widen_weight,
    widen_bias,
    bottle_depth,
    bottle_gain,
    bottle_shift,
    bottle_up,
    bottle_up_bias,
    bottle_down,
    bottle_down_bias,
    merge_weight,
    merge_bias,
    decode_depth,
    decode_gain,
    decode_shift,
    decode_up,
    decode_up_bias,
    decode_down,
    decode_down_bias,
):
    dates, tile_rows, breadth, channels = fine_map.shape
    wide = bottle_depth.shape[2]
    extra = jnp.swapaxes(ocean_mask, 1, 2).astype(bf16)[:, None]
    extra = jnp.pad(extra, ((0, 0), (0, 0), (0, 0), (0, channels - tile_rows)))
    pieces = send_dates(jnp.concatenate([fine_map, extra], axis=1))
    kernels = (encode_depth, bottle_depth, decode_depth)
    rows = (encode_up_bias, encode_down_bias, bottle_up_bias, bottle_down_bias, decode_up_bias, decode_down_bias)
    small = (
        [kernel.astype(f32).reshape(49, -1) for kernel in kernels],
        [row.astype(f32)[None] for row in rows + (widen_bias, merge_bias)],
        [row.astype(f32) for row in (encode_gain, encode_shift, bottle_gain, bottle_shift, decode_gain, decode_shift)],
    )
    pieces, (taps, rows, norms) = lax.optimization_barrier((pieces, small))
    encode_up_bias, encode_down_bias, bottle_up_bias, bottle_down_bias, decode_up_bias, decode_down_bias = rows[:6]
    widen_bias, merge_bias = rows[6:]
    encode_norm, bottle_norm, decode_norm = [(taps[i], norms[2 * i], norms[2 * i + 1]) for i in range(3)]
    packed = to_dates(pieces).reshape(dates, tile_rows + 1, breadth, channels)
    fine = packed[:, :tile_rows].reshape(-1, breadth, channels)
    ocean_band = jnp.swapaxes(packed[:, tile_rows, :, :tile_rows], 1, 2).reshape(-1, breadth).astype(f32)
    height = fine.shape[0]
    half_height, half_breadth = height // 2, breadth // 2


    coarse_band = jnp.max(ocean_band.reshape(half_height, 2, half_breadth, 2), axis=(1, 3))
    sea_fine = jnp.broadcast_to(ocean_band[..., None], (height, breadth, lanes))
    sea_coarse = jnp.broadcast_to(coarse_band[..., None], (half_height, half_breadth, lanes))
    ocean_fine = jnp.sum(ocean_band)
    ocean_coarse = jnp.sum(coarse_band)
    parts = height * breadth // math.gcd(height * breadth, 384)
    pixel = np.arange(height * breadth // parts)
    block = pixel // breadth // 2 * half_breadth + pixel % breadth // 2
    members = jnp.asarray(block[:, None] == np.arange(pixel.size // 4), dtype=bf16)
    blocks = jnp.asarray(np.arange(pixel.size // 4)[:, None] == block, dtype=bf16)

    mix = block_mix(fine, encode_norm, sea_fine, ocean_fine, dates)
    encode_up, encode_down = gathered_pair(encode_up, encode_down, mix[3])
    encode = encode_norm + (encode_up, encode_up_bias, encode_down, encode_down_bias)
    widen_weight = gathered(after(widen_weight, mix[3]))
    skip_rows, (pooled, coarse_in), encode_stored = block_forward(
        mix, encode, sea_fine, (blocks, widen_weight, widen_bias)
    )
    decode_up = lax.all_gather(after(decode_up, skip_rows), "lat", axis=0, tiled=True)
    decode_down = lax.all_gather(after(decode_down, skip_rows), "lat", axis=0, tiled=True)
    decode = decode_norm + (decode_up, decode_up_bias, decode_down, decode_down_bias)
    bottle_up = gathered_by_columns(bottle_up, skip_rows)
    bottle_down = gathered_by_rows(after(bottle_down, encode_stored[3]), skip_rows)
    bottle = bottle_norm + (bottle_up, bottle_up_bias, bottle_down, bottle_down_bias)
    coarse_in = coarse_in.reshape(half_height, half_breadth, wide)
    mix = block_mix(coarse_in, bottle, sea_coarse, ocean_coarse, dates, (bottle_up, bottle_down))
    coarse_low, _, coarse_stored = block_forward(mix, bottle, sea_coarse)
    merge_rows = merge_weight.shape[0]
    merge_weight = jnp.pad(after(merge_weight, skip_rows), ((0, -merge_rows % 16), (0, 0)))
    merge_weight = gathered(merge_weight, coarse_low).reshape(-1, merge_rows + -merge_rows % 16, channels)
    merge_weight = merge_weight[:, :merge_rows].reshape(-1, channels)
    upstream = send_dates(after(out_grad, mix[3]))
    merged = merge_forward(coarse_low, skip_rows, merge_weight, merge_bias, members, parts)
    mix = block_mix(merged.reshape(fine.shape), decode, sea_fine, ocean_fine, dates)
    upstream = to_dates(after(upstream, mix[3])).reshape(-1, channels)
    decode_rows, _, decode_stored = block_forward(mix, decode, sea_fine)
    result = from_dates(decode_rows.reshape(fine.shape), dates)

    grad_branch, grad_hidden, grad_normed, local, *decode_small = block_hidden(upstream, decode, sea_fine, decode_stored)
    early = [
        cross_rows(decode_stored[6], grad_hidden),
        cross_rows(grad_branch, decode_stored[8]),
    ]
    grad_mixed, grad_edges, *decode_total = block_norm(grad_normed, local, sea_fine, decode_stored, dates)
    decode_mixed = grad_mixed
    grad_merged, merge_sums = block_source(grad_mixed, grad_edges, upstream, sea_fine, decode_stored)

    block_sums, grad_coarse = merge_backward(grad_merged, merge_weight, blocks, wide, parts)
    early += [cross_rows(block_sums, coarse_low), cross_rows(grad_merged, skip_rows)]

    grad_branch, grad_hidden, grad_normed, local, *bottle_small = block_hidden(
        grad_coarse, bottle, sea_coarse, coarse_stored
    )
    decode_kernel = kernel_grad(*decode_stored[:2], after(decode_mixed, local))
    early += [cross_rows(coarse_stored[6], grad_hidden), cross_rows(grad_branch, coarse_stored[8])]
    early = lax.psum([part.astype(bf16) for part in early], both)
    early = [total.astype(f32) for total in early]
    decode_up_sum, decode_down_sum, bottle_up_sum, bottle_down_sum = early[0], early[1].T, early[4], early[5].T
    merge_sum = jnp.concatenate(early[2:4], axis=1).T
    grad_mixed, grad_edges, *bottle_total = block_norm(grad_normed, local, sea_coarse, coarse_stored, dates)
    bottle_kernel = kernel_grad(*coarse_stored[:2], grad_mixed)
    grad_wide, widen_sums = block_source(grad_mixed, grad_edges, grad_coarse, sea_coarse, coarse_stored)
    grad_skip = skip_backward(grad_merged, grad_wide, merge_weight, widen_weight, members, parts)

    grad_branch, grad_hidden, grad_normed, local, *encode_small = block_hidden(
        grad_skip, encode, sea_fine, encode_stored
    )
    encode_pair = weight_grads(grad_branch, encode_stored[6], encode_stored[8], grad_hidden).reshape(2, -1, lanes)
    grad_mixed, grad_edges, *encode_total = block_norm(grad_normed, local, sea_fine, encode_stored, dates)
    encode_kernel = kernel_grad(*encode_stored[:2], grad_mixed)
    grad_fine, _ = block_source(grad_mixed, grad_edges, grad_skip, sea_fine, encode_stored)
    core = (lax.axis_index("lon") % 2).astype(jnp.int32)[None]
    grad_widen = cross_rows(pooled, grad_wide).astype(bf16)
    widen_tiles = pl.cdiv(wide, 2 * lanes)
    grad_widen = jnp.pad(grad_widen, ((0, 0), (0, 2 * widen_tiles * lanes - wide)))
    grad_widen = grad_widen.reshape(channels, 2, widen_tiles, lanes).transpose(1, 2, 0, 3).reshape(2, -1, lanes)
    fine_grad = from_dates(grad_fine.reshape(fine.shape), dates)
    state = jnp.concatenate([encode_pair, grad_widen], axis=1)
    for stage in group_stages():
        state = stage(state)
    own, other = state
    encode_up_sum, encode_down_sum = unpack(core, own, other, channels, encode_up.shape[1])
    encode_down_sum = encode_down_sum.T
    start = encode_pair.shape[1]
    lower = jnp.where(core == 0, own[start : start + grad_widen.shape[1]], other[start : start + grad_widen.shape[1]])
    upper = jnp.where(core == 0, other[start : start + grad_widen.shape[1]], own[start : start + grad_widen.shape[1]])
    widen_sum = jnp.stack([lower, upper]).reshape(2 * widen_tiles, channels, lanes).astype(f32)
    widen_sum = widen_sum.transpose(1, 0, 2).reshape(channels, -1)[:, :wide]

    kernels = [encode_kernel, bottle_kernel, decode_kernel]
    rows = [encode_small, (widen_sums,), bottle_small, (merge_sums,), decode_small]
    rows = [row for group in rows for row in group]
    padded = [jnp.pad(row, ((0, 0), (0, -row.shape[1] % lanes))) for row in rows]
    line = jnp.concatenate(padded, axis=1)
    small = sum_small(jnp.concatenate([array.reshape(-1, lanes) for array in kernels] + [line.reshape(-1, lanes)]))
    kernel_sums, at = [], 0
    for array, shape in zip(kernels, (encode_depth.shape, bottle_depth.shape, decode_depth.shape)):
        count = array.shape[0] * 56
        total = small[at : at + count].reshape(array.shape)[:, :49].transpose(1, 0, 2).reshape(49, -1)
        kernel_sums.append(total[:, : shape[2]].reshape(shape))
        at += count
    line = small[at:].reshape(-1)
    row_sums, at = [], 0
    for row, wider in zip(rows, padded):
        row_sums.append(line[at : at + row.shape[1]])
        at += wider.shape[1]
    (encode_upb, encode_downb, widen_b, bottle_upb, bottle_downb, bottle_merge_b, decode_upb, decode_downb) = (
        row_sums[1],
        row_sums[0],
        row_sums[2],
        row_sums[4],
        row_sums[3],
        row_sums[5],
        row_sums[7],
        row_sums[6],
    )
    return (
        result,
        fine_grad,
        kernel_sums[0],
        encode_total[0],
        encode_total[1],
        encode_up_sum,
        encode_upb,
        encode_down_sum,
        encode_downb,
        widen_sum,
        widen_b,
        kernel_sums[1],
        bottle_total[0],
        bottle_total[1],
        bottle_up_sum,
        bottle_upb,
        bottle_down_sum,
        bottle_downb,
        merge_sum,
        bottle_merge_b,
        kernel_sums[2],
        decode_total[0],
        decode_total[1],
        decode_up_sum,
        decode_upb,
        decode_down_sum,
        decode_downb,
    )


def solution(mesh):
    whole = P()
    rows = P("lat", None)
    tile = P(None, "lat", "lon", None)
    block = (whole, whole, whole, rows, whole, rows, whole)
    placed = (tile, P(None, "lat", "lon"), tile) + block + (rows, whole) + block + (rows, whole) + block
    return jax.shard_map(
        shards,
        mesh=mesh,
        in_specs=placed,
        out_specs=(tile, tile) + (whole,) * 25,
        check_vma=False,
    )
```

```python
import functools
import math

import jax
import jax.numpy as jnp
import numpy as np
from jax import lax
from jax.experimental import pallas as pl
from jax.experimental.pallas import tpu as pltpu
from jax.sharding import PartitionSpec as P

epsilon = 1e-05
both = ("lat", "lon")
bf16 = jnp.bfloat16
f32 = jnp.float32
lanes = 128
strip = 12
room = pltpu.CompilerParams(vmem_limit_bytes=56 << 20)


def exchange_pairs(count, group, step):
    return [(i, (i // group) * group + ((i % group) ^ step)) for i in range(count)]


def send_dates(tiles):
    dates, count = tiles.shape[0], lax.axis_size("lat")
    own = lax.axis_index("lat") % dates
    pieces = [lax.dynamic_index_in_dim(tiles, own, 0, keepdims=False)]
    for step in range(1, dates):
        pieces.append(
            lax.ppermute(
                lax.dynamic_index_in_dim(tiles, own ^ step, 0, keepdims=False),
                "lat",
                exchange_pairs(count, dates, step),
            )
        )
    return pieces


def to_dates(pieces):
    dates = len(pieces)
    own = lax.axis_index("lat") % dates
    stacked = jnp.stack(pieces)
    ordered = [lax.dynamic_index_in_dim(stacked, own ^ tile, 0, keepdims=False) for tile in range(dates)]
    return jnp.concatenate(ordered, axis=0)


def from_dates(band, dates):
    count = lax.axis_size("lat")
    own = lax.axis_index("lat") % dates
    tiles = band.reshape((dates, band.shape[0] // dates) + band.shape[1:])
    pieces = [lax.dynamic_index_in_dim(tiles, own, 0, keepdims=False)]
    for step in range(1, dates):
        pieces.append(
            lax.ppermute(
                lax.dynamic_index_in_dim(tiles, own ^ step, 0, keepdims=False),
                "lat",
                exchange_pairs(count, dates, step),
            )
        )
    stacked = jnp.stack(pieces)
    return jnp.stack([lax.dynamic_index_in_dim(stacked, own ^ date, 0, keepdims=False) for date in range(dates)])


def after(array, event):
    return lax.optimization_barrier((array, event))[0]


def gathered(shard, event=None):
    return exchange_all(shard, "lat", lax.axis_index("lat"), 1, lax.axis_size("lat"), event)


def assemble(kernel, name, shape, arrays, copies):
    tile, core = lax.axis_index("lat"), lax.axis_index("lon") % 2
    return pl.pallas_call(
        kernel,
        in_specs=[pl.BlockSpec(memory_space=pltpu.SMEM)] + [pl.BlockSpec(memory_space=pl.ANY)] * len(arrays),
        out_specs=pl.BlockSpec(memory_space=pltpu.VMEM),
        out_shape=jax.ShapeDtypeStruct(shape, bf16),
        scratch_shapes=[pltpu.SemaphoreType.DMA((copies,))],
        compiler_params=room,
        name=name,
    )(jnp.stack([tile, core]).astype(jnp.int32), *arrays)


def finish(copies):
    for copy in copies:
        copy.start()
    for copy in copies:
        copy.wait()


def assemble_rows_kernel(place, shard, mine, theirs, out, sems):
    tile, core = place[0], place[1]
    rows = shard.shape[0]
    half = rows // 2
    copies = [(shard, tile * rows, rows)]
    for step in range(1, mine.shape[0] + 1):
        start = (tile ^ step) * rows
        copies.append((mine.at[step - 1], start + core * half, half))
        copies.append((theirs.at[step - 1], start + (1 - core) * half, half))
    finish(
        [
            pltpu.make_async_copy(source, out.at[pl.ds(pl.multiple_of(start, 8), count)], sems.at[index])
            for index, (source, start, count) in enumerate(copies)
        ]
    )


def assemble_columns_kernel(place, mine, theirs, out, sems):
    start = out.shape[1] - mine.shape[1]

    def join(low, high):
        finish(
            [
                pltpu.make_async_copy(low.at[:, :start], out.at[:, :start], sems.at[0]),
                pltpu.make_async_copy(high, out.at[:, start:], sems.at[1]),
            ]
        )

    @pl.when(place[1] == 0)
    def _():
        join(mine, theirs)

    @pl.when(place[1] != 0)
    def _():
        join(theirs, mine)


def gathered_by_rows(shard, event):
    tiles = lax.axis_size("lat")
    half = take(shard.reshape(2, -1, shard.shape[1]), lax.axis_index("lon") % 2)
    mine, event = lax.optimization_barrier(([swap(half, "lat", step) for step in range(1, tiles)], event))
    mine = jnp.stack(mine)
    arrays = (shard, mine, swap(mine, "lon", 1))
    shape = (tiles * shard.shape[0], shard.shape[1])
    return assemble(assemble_rows_kernel, "assemble_rows", shape, arrays, 2 * tiles - 1), event


def gathered_by_columns(shard, event):
    columns = shard.shape[1]
    start = columns // 2 // lanes * lanes
    half = lax.dynamic_slice_in_dim(shard, lax.axis_index("lon") % 2 * start, columns - start, axis=1)
    mine = after(lax.all_gather(half, "lat", axis=0, tiled=True), event)
    return assemble(
        assemble_columns_kernel, "assemble_columns", (mine.shape[0], columns), (mine, swap(mine, "lon", 1)), 2
    )


def gathered_pair(up, down, event):
    channels = down.shape[1]
    first = lax.axis_index("lon") % 2 == 0
    mine = lax.all_gather(jnp.where(first, up.reshape(-1, channels), down), "lat", axis=0, tiled=True)
    mine = after(mine, event)
    theirs = swap(mine, "lon", 1)
    return jnp.where(first, mine, theirs).reshape(-1, up.shape[1]), jnp.where(first, theirs, mine)


def borders(source, dates):
    count = lax.axis_size("lon")
    forward = [(i, (i + 1) % count) for i in range(count)]
    backward = [(target, origin) for origin, target in forward]
    left = lax.ppermute(source[:, -3:], "lon", forward)
    right = lax.ppermute(source[:, :3], "lon", backward)
    tiles = lax.axis_size("lat")
    if tiles == dates:
        return left, right
    down = [(i, i + dates) for i in range(tiles - dates)]
    up = [(target, origin) for origin, target in down]
    last = jnp.concatenate([left[-3:], source[-3:], right[-3:]], axis=1)
    first = jnp.concatenate([left[:3], source[:3], right[:3]], axis=1)
    return left, right, lax.ppermute(last, "lat", down), lax.ppermute(first, "lat", up)


def sum_all(local, event=()):
    count = lax.axis_size(both)
    copies = jnp.broadcast_to(local[None], (count,) + local.shape)
    return jnp.sum(after(lax.all_to_all(copies, both, 0, 0, tiled=False), event), axis=0)


def fill_extended(wide_ref, centre, edges):
    rows, columns = centre.shape[0], centre.shape[1]
    blank = jnp.zeros((3, columns + 16, lanes), f32)
    wide_ref[0:3] = blank
    wide_ref[rows + 3 :] = blank
    wide_ref[3 : rows + 3, 8 : columns + 8] = centre[...].astype(f32)
    wide_ref[3 : rows + 3, 5:8] = edges[0][...].astype(f32)
    wide_ref[3 : rows + 3, columns + 8 : columns + 11] = edges[1][...].astype(f32)
    if len(edges) > 2:
        wide_ref[0:3, 5 : columns + 11] = edges[2][...].astype(f32)
        wide_ref[rows + 3 :, 5 : columns + 11] = edges[3][...].astype(f32)


def strip_sum(wide_ref, taps, top, start, flipped):
    total = None
    for column in range(7):
        window = wide_ref[pl.ds(top, strip + 6), start + 5 + column : start + 13 + column, :]
        for across in range(7):
            place = 7 * across + column
            tap = taps[pl.ds(48 - place if flipped else place, 8, stride=0), :]
            term = window[across : across + strip] * tap[None]
            total = term if total is None else total + term
    return total


def stencil_forward_kernel(edge_count, source, *refs):
    edges = refs[:edge_count]
    taps, sea, mixed, sums, wide_ref = refs[edge_count:]
    rows, columns = source.shape[0], source.shape[1]
    fill_extended(wide_ref, source, edges)

    def step(index, carry):
        first, square = carry
        top = index * strip
        for start in range(0, columns, 8):
            here = (pl.ds(top, strip), slice(start, start + 8))
            total = strip_sum(wide_ref, taps, top, start, False)
            mixed[here] = total
            masked = total * sea[here]
            first = first + jnp.sum(masked, axis=0)
            square = square + jnp.sum(masked * total, axis=0)
        return first, square

    zero = jnp.zeros((8, lanes), f32)
    first, square = lax.fori_loop(0, rows // strip, step, (zero, zero))
    sums[0:1] = jnp.sum(first, axis=0, keepdims=True)
    sums[1:2] = jnp.sum(square, axis=0, keepdims=True)


def stencil_backward_kernel(edge_count, grad, *refs):
    edges = refs[:edge_count]
    taps, sea, upstream, out, sums, wide_ref = refs[edge_count:]
    rows, columns = grad.shape[0], grad.shape[1]
    fill_extended(wide_ref, grad, edges)

    def step(index, first):
        top = index * strip
        for start in range(0, columns, 8):
            here = (pl.ds(top, strip), slice(start, start + 8))
            total = strip_sum(wide_ref, taps, top, start, True)
            low = (total + upstream[here].astype(f32) * sea[here]).astype(bf16)
            out[here] = low
            first = first + jnp.sum(low.astype(f32), axis=0)
        return first

    first = lax.fori_loop(0, rows // strip, step, jnp.zeros((8, lanes), f32))
    sums[...] = jnp.sum(first, axis=0, keepdims=True)


def kernel_grad_kernel(edge_count, source, *refs):
    edges = refs[:edge_count]
    grad, out, wide_ref, sums_ref = refs[edge_count:]
    rows, columns = source.shape[0], source.shape[1]
    fill_extended(wide_ref, source, edges)
    sums_ref[...] = jnp.zeros_like(sums_ref)

    def step(index, carry):
        top = index * strip
        for start in range(0, columns, 8):
            upstream = grad[pl.ds(top, strip), start : start + 8, :].astype(f32)
            for column in range(7):
                window = wide_ref[pl.ds(top, strip + 6), start + 5 + column : start + 13 + column, :]
                for across in range(7):
                    sums_ref[7 * across + column] += jnp.sum(window[across : across + strip] * upstream, axis=0)
        return carry

    lax.fori_loop(0, rows // strip, step, 0)
    out[0, 0:49] = jnp.sum(sums_ref[...], axis=1)
    out[0, 49:56] = jnp.zeros((7, lanes), f32)


def by_channel(array):
    rest = array.shape[:-1]
    return pl.BlockSpec(rest + (lanes,), lambda tile: (0,) * len(rest) + (tile,))


def same_block(array):
    return pl.BlockSpec(array.shape, lambda tile: (0,) * array.ndim)


def wide_scratch(rows, columns):
    return pltpu.VMEM((rows + 6, columns + 16, lanes), f32)


def stencil_forward(source, edges, taps, sea):
    rows, columns, channels = source.shape
    sums = jax.ShapeDtypeStruct((2, channels), f32)
    mixed = jax.ShapeDtypeStruct(source.shape, f32)
    return pl.pallas_call(
        functools.partial(stencil_forward_kernel, len(edges)),
        grid=(pl.cdiv(channels, lanes),),
        in_specs=[by_channel(array) for array in (source, *edges, taps)] + [same_block(sea)],
        out_specs=[by_channel(mixed), by_channel(sums)],
        out_shape=[mixed, sums],
        scratch_shapes=[wide_scratch(rows, columns)],
        compiler_params=room,
        name="stencil_forward",
    )(source, *edges, taps, sea)


def stencil_backward(grad, edges, taps, sea, upstream):
    rows, columns, channels = grad.shape
    out = jax.ShapeDtypeStruct(grad.shape, bf16)
    sums = jax.ShapeDtypeStruct((1, channels), f32)
    return pl.pallas_call(
        functools.partial(stencil_backward_kernel, len(edges)),
        grid=(pl.cdiv(channels, lanes),),
        in_specs=[by_channel(array) for array in (grad, *edges, taps)] + [same_block(sea), by_channel(upstream)],
        out_specs=[by_channel(out), by_channel(sums)],
        out_shape=[out, sums],
        scratch_shapes=[wide_scratch(rows, columns)],
        compiler_params=room,
        name="stencil_backward",
    )(grad, *edges, taps, sea, upstream)


def kernel_grad(source, edges, grad):
    rows, columns, channels = source.shape
    tiles = pl.cdiv(channels, lanes)
    out = jax.ShapeDtypeStruct((tiles, 56, lanes), f32)
    return pl.pallas_call(
        functools.partial(kernel_grad_kernel, len(edges)),
        grid=(tiles,),
        in_specs=[by_channel(array) for array in (source, *edges, grad)],
        out_specs=pl.BlockSpec((1, 56, lanes), lambda tile: (tile, 0, 0)),
        out_shape=out,
        scratch_shapes=[wide_scratch(rows, columns), pltpu.VMEM((49, 8, lanes), f32)],
        compiler_params=room,
        name="kernel_grad",
    )(source, *edges, grad)


def chunks_of(width, size):
    edges = list(range(0, width, size))
    if len(edges) > 1 and width - edges[-1] < size // 2:
        edges.pop()
    return list(zip(edges, edges[1:] + [width]))


def spread(sea, channels):
    return jnp.concatenate([sea] * pl.cdiv(channels, lanes), axis=1)[:, :channels]


def gelu_pair(hidden):
    below = 0.5 + 0.5 * lax.erf(hidden * math.sqrt(0.5))
    density = jnp.exp(-0.5 * hidden * hidden) * (1.0 / math.sqrt(2.0 * math.pi))
    return hidden * below, below + hidden * density


def mlp_forward_kernel(
    size, mixed, source, sea, scales, up, up_bias, down, down_bias, *refs
):
    unit = (mixed[...] - scales[0:1]) * scales[1:2]
    low = (unit * scales[2:3] + scales[3:4]).astype(bf16)
    out, active, slope, normed = refs[-4:] if len(refs) == 4 else refs[3:7]
    normed[...] = low
    branch = down_bias[...]
    for a, b in chunks_of(up.shape[1], size):
        hidden = jnp.dot(low, up[:, a:b], preferred_element_type=f32) + up_bias[:, a:b]
        value, rise = gelu_pair(hidden)
        value = value.astype(bf16)
        active[:, a:b] = value
        slope[:, a:b] = rise.astype(bf16)
        branch = branch + jnp.dot(value, down[a:b, :], preferred_element_type=f32)
    mask = spread(sea[...], out.shape[1])
    result = (mask * (source[...].astype(f32) + branch)).astype(bf16)
    out[...] = result
    if len(refs) > 4:
        blocks, widen, widen_bias = refs[:3]
        pooled, coarse = refs[7:]
        mean = (0.25 * jnp.dot(blocks[...], result, preferred_element_type=f32)).astype(bf16)
        pooled[...] = mean
        coarse[...] = (jnp.dot(mean, widen[...], preferred_element_type=f32) + widen_bias[...]).astype(bf16)


def merge_forward_kernel(coarse, skip, merge, bias, members, merged):
    wide = coarse.shape[1]
    upper = jnp.dot(coarse[...], merge[:wide, :], preferred_element_type=f32)
    high = upper.astype(bf16)
    rest = (upper - high.astype(f32)).astype(bf16)
    total = jnp.dot(members[...], high, preferred_element_type=f32)
    total = total + jnp.dot(members[...], rest, preferred_element_type=f32)
    total = total + jnp.dot(skip[...], merge[wide:, :], preferred_element_type=f32)
    merged[...] = (total + bias[...]).astype(bf16)


def merge_backward_kernel(grad, merge, blocks, block_sums, grad_coarse):
    wide = grad_coarse.shape[1]
    low = jnp.dot(blocks[...], grad[...], preferred_element_type=f32).astype(bf16)
    block_sums[...] = low
    grad_coarse[...] = lax.dot_general(
        low, merge[:wide, :], (((1,), (1,)), ((), ())), preferred_element_type=f32
    )


def skip_backward_kernel(grad, grad_wide, merge, widen, members, grad_skip):
    wide = grad_wide.shape[1]
    pooled = 0.25 * lax.dot_general(
        grad_wide[...], widen[...], (((1,), (1,)), ((), ())), preferred_element_type=f32
    )
    high = pooled.astype(bf16)
    rest = (pooled - high.astype(f32)).astype(bf16)
    total = lax.dot_general(grad[...], merge[wide:, :], (((1,), (1,)), ((), ())), preferred_element_type=f32)
    total = total + jnp.dot(members[...], high, preferred_element_type=f32)
    grad_skip[...] = total + jnp.dot(members[...], rest, preferred_element_type=f32)


def mlp_backward_kernel(
    size,
    upstream,
    mixed,
    slope,
    sea,
    scales,
    up,
    down,
    grad_branch,
    grad_hidden,
    grad_normed,
    sums,
    down_sums,
    up_sums,
):
    @pl.when(pl.program_id(0) == 0)
    def _():
        sums[...] = jnp.zeros_like(sums)
        down_sums[...] = jnp.zeros_like(down_sums)
        up_sums[...] = jnp.zeros_like(up_sums)

    mask = spread(sea[...], upstream.shape[1])
    low = (mask * upstream[...].astype(f32)).astype(bf16)
    grad_branch[...] = low
    down_sums[...] += jnp.sum(low.astype(f32), axis=0, keepdims=True)
    normed = None
    for a, b in chunks_of(up.shape[1], size):
        grad_active = lax.dot_general(low, down[a:b, :], (((1,), (1,)), ((), ())), preferred_element_type=f32)
        hidden = (grad_active * slope[:, a:b].astype(f32)).astype(bf16)
        grad_hidden[:, a:b] = hidden
        up_sums[:, a:b] += jnp.sum(hidden.astype(f32), axis=0, keepdims=True)
        part = lax.dot_general(hidden, up[:, a:b], (((1,), (1,)), ((), ())), preferred_element_type=f32)
        normed = part if normed is None else normed + part
    grad_normed[...] = normed
    unit = (mixed[...] - scales[0:1]) * scales[1:2]
    sums[0:1] += jnp.sum(normed, axis=0, keepdims=True)
    sums[1:2] += jnp.sum(normed * unit, axis=0, keepdims=True)


def tall(rows, width):
    return pl.BlockSpec((rows, width), lambda i: (i, 0))


def fixed(array):
    return pl.BlockSpec(array.shape, lambda i: (0, 0), pipeline_mode=pl.Buffered(1))


def by_rows(parts, array):
    return tall(array.shape[0] // parts, array.shape[1])


def mlp_forward(mixed, source, sea, scales, up, up_bias, down, down_bias, pooling=()):
    pixels, channels = mixed.shape
    wide = up.shape[1]
    rows = math.gcd(pixels, 384)
    parts = pixels // rows
    shapes = [(pixels, width) for width in (channels, wide, wide, channels)]
    if pooling:
        shapes += [(pixels // 4, channels), (pixels // 4, pooling[1].shape[1])]
    outs = [jax.ShapeDtypeStruct(shape, bf16) for shape in shapes]
    return pl.pallas_call(
        functools.partial(mlp_forward_kernel, 512),
        grid=(parts,),
        in_specs=[by_rows(parts, array) for array in (mixed, source, sea)]
        + [fixed(array) for array in (scales, up, up_bias, down, down_bias, *pooling)],
        out_specs=[by_rows(parts, out) for out in outs],
        out_shape=outs,
        compiler_params=room,
        name="mlp_forward",
    )(mixed, source, sea, scales, up, up_bias, down, down_bias, *pooling)


def merge_forward(coarse, skip, merge, bias, members, parts):
    merged = jax.ShapeDtypeStruct(skip.shape, bf16)
    return pl.pallas_call(
        merge_forward_kernel,
        grid=(parts,),
        in_specs=[by_rows(parts, array) for array in (coarse, skip)]
        + [fixed(array) for array in (merge, bias, members)],
        out_specs=by_rows(parts, merged),
        out_shape=merged,
        compiler_params=room,
        name="merge_forward",
    )(coarse, skip, merge, bias, members)


def merge_backward(grad, merge, blocks, wide, parts):
    pixels, channels = grad.shape
    block_sums = jax.ShapeDtypeStruct((pixels // 4, channels), bf16)
    grad_coarse = jax.ShapeDtypeStruct((pixels // 4, wide), f32)
    return pl.pallas_call(
        merge_backward_kernel,
        grid=(parts,),
        in_specs=[by_rows(parts, grad), fixed(merge), fixed(blocks)],
        out_specs=[by_rows(parts, block_sums), by_rows(parts, grad_coarse)],
        out_shape=[block_sums, grad_coarse],
        compiler_params=room,
        name="merge_backward",
    )(grad, merge, blocks)


def skip_backward(grad, grad_wide, merge, widen, members, parts):
    grad_skip = jax.ShapeDtypeStruct(grad.shape, f32)
    return pl.pallas_call(
        skip_backward_kernel,
        grid=(parts,),
        in_specs=[by_rows(parts, array) for array in (grad, grad_wide)]
        + [fixed(array) for array in (merge, widen, members)],
        out_specs=by_rows(parts, grad_skip),
        out_shape=grad_skip,
        compiler_params=room,
        name="skip_backward",
    )(grad, grad_wide, merge, widen, members)


def mlp_backward(upstream, mixed, slope, sea, scales, up, down):
    pixels, channels = mixed.shape
    wide = up.shape[1]
    rows = math.gcd(pixels, 384)
    sums = [jax.ShapeDtypeStruct(shape, f32) for shape in ((2, channels), (1, channels), (1, wide))]
    return pl.pallas_call(
        functools.partial(mlp_backward_kernel, 512),
        grid=(pixels // rows,),
        in_specs=[tall(rows, channels), tall(rows, channels), tall(rows, wide), tall(rows, lanes)]
        + [fixed(array) for array in (scales, up, down)],
        out_specs=[tall(rows, channels), tall(rows, wide), tall(rows, channels)]
        + [pl.BlockSpec(array.shape, lambda i: (0, 0)) for array in sums],
        out_shape=[
            jax.ShapeDtypeStruct((pixels, channels), bf16),
            jax.ShapeDtypeStruct((pixels, wide), bf16),
            jax.ShapeDtypeStruct((pixels, channels), f32),
        ]
        + sums,
        compiler_params=room,
        name="mlp_backward",
    )(upstream, mixed, slope, sea, scales, up, down)


def weight_grads_kernel(grad_branch, normed, active, grad_hidden, out, branch_ref, normed_ref):
    @pl.when(pl.program_id(0) == 0)
    def _():
        branch_ref[...] = grad_branch[...].T
        normed_ref[...] = normed[...].T

    up = jnp.dot(normed_ref[...], grad_hidden[...], preferred_element_type=f32).astype(bf16)
    down = jnp.dot(branch_ref[...], active[...], preferred_element_type=f32).astype(bf16)
    for part in range(out.shape[1]):
        out[0, part] = up[:, part * lanes : (part + 1) * lanes]
        out[1, part] = down[:, part * lanes : (part + 1) * lanes]


def weight_grads(grad_branch, normed, active, grad_hidden):
    pixels, channels = normed.shape
    hidden = active.shape[1]
    tiles = pl.cdiv(hidden, lanes)
    parts = next(count for count in (5, 4, 3, 2, 1) if count == 2 or tiles % count == 0)
    return pl.pallas_call(
        weight_grads_kernel,
        grid=(pl.cdiv(tiles, parts),),
        in_specs=[fixed(grad_branch), fixed(normed)]
        + [pl.BlockSpec((pixels, parts * lanes), lambda tile: (0, tile))] * 2,
        out_specs=pl.BlockSpec((2, parts, channels, lanes), lambda tile: (0, tile, 0, 0)),
        out_shape=jax.ShapeDtypeStruct((2, tiles, channels, lanes), bf16),
        scratch_shapes=[pltpu.VMEM((channels, pixels), bf16)] * 2,
        compiler_params=room,
        name="weight_grads",
    )(grad_branch, normed, active, grad_hidden)


def unpack_kernel(core, own, other, up, down):
    mine, theirs = own[...].astype(f32), other[...].astype(f32)
    first = core[0] == 0
    up[...] = jnp.where(first, mine, theirs)
    down[...] = jnp.where(first, theirs, mine)


def unpack(core, own, other, channels, hidden):
    block = pl.BlockSpec((channels, lanes), lambda tile, core: (tile, 0))
    return pl.pallas_call(
        unpack_kernel,
        grid_spec=pltpu.PrefetchScalarGridSpec(
            num_scalar_prefetch=1,
            grid=(pl.cdiv(hidden, lanes),),
            in_specs=[block, block],
            out_specs=[pl.BlockSpec((channels, lanes), lambda tile, core: (0, tile))] * 2,
        ),
        out_shape=[jax.ShapeDtypeStruct((channels, hidden), f32)] * 2,
        compiler_params=room,
        name="unpack",
    )(core, own, other)


def swap(array, axis, step):
    return lax.ppermute(array, axis, [(i, i ^ step) for i in range(lax.axis_size(axis))])


def take(stacked, index):
    return lax.dynamic_index_in_dim(stacked, index, 0, keepdims=False)


def exchange_add(stacked, axis, own, scale):
    count = stacked.shape[0]
    got = [swap(take(stacked, own ^ step), axis, scale * step) for step in range(1, count)]
    total = take(stacked, own).astype(f32)
    for piece in got:
        total = total + piece.astype(f32)
    return total.astype(bf16)


def exchange_all(piece, axis, own, scale, count, event=None):
    got = [swap(piece, axis, scale * step) for step in range(1, count)]
    got = jnp.stack([piece] + (got if event is None else after(got, event)))
    return jnp.concatenate([take(got, own ^ place) for place in range(count)], axis=0)


def kept_and_sent(array, bit):
    pieces = array.reshape(2, -1, lanes)
    return take(pieces, bit), take(pieces, 1 - bit)


def low_sum(kept, got):
    return (kept.astype(f32) + got.astype(f32)).astype(bf16)


def in_order(bit, own, other):
    return jnp.where(bit == 0, jnp.concatenate([own, other]), jnp.concatenate([other, own]))


def reduce_over_cores(pair):
    unit = 16 * lax.axis_size("lat") * lax.axis_size("lon") // 2
    rows = pair.shape[1]
    pair = jnp.pad(pair, ((0, 0), (0, -rows % unit), (0, 0)))
    core = lax.axis_index("lon") % 2
    return low_sum(take(pair, core), swap(take(pair, 1 - core), "lon", 1))


def reduce_first(half):
    tile = lax.axis_index("lat")
    parts = []
    for share, step in zip((half[: half.shape[0] // 2], half[half.shape[0] // 2 :]), (1, 2)):
        kept, sent = kept_and_sent(share, tile // step % 2)
        parts.append((kept, swap(sent, "lat", step)))
    return [low_sum(kept, got) for kept, got in parts]


def reduce_second(shares):
    tile = lax.axis_index("lat")
    parts = []
    for share, step in zip(shares, (2, 1)):
        kept, sent = kept_and_sent(share, tile // step % 2)
        parts.append((kept, swap(sent, "lat", step)))
    return jnp.stack([low_sum(kept, got) for kept, got in parts])


def reduce_columns(shares):
    columns = lax.axis_size("lon") // 2
    column = lax.axis_index("lon") // 2
    pieces = shares.reshape(shares.shape[0], columns, -1, lanes).swapaxes(0, 1)
    return exchange_add(pieces, "lon", column, 2)


def spread_columns(share):
    columns = lax.axis_size("lon") // 2
    column = lax.axis_index("lon") // 2
    got = jnp.stack([share] + [swap(share, "lon", 2 * step) for step in range(1, columns)])
    whole = jnp.stack([take(got, column ^ place) for place in range(columns)], axis=1)
    return whole.reshape(share.shape[0], -1, lanes)


def spread_second(shares):
    tile = lax.axis_index("lat")
    return [
        in_order(tile // step % 2, share, swap(share, "lat", step)) for share, step in zip(shares, (2, 1))
    ]


def spread_first(shares):
    tile = lax.axis_index("lat")
    parts = [
        in_order(tile // step % 2, share, swap(share, "lat", step)) for share, step in zip(shares, (1, 2))
    ]
    return jnp.concatenate(parts)


def reduce_tiles(half):
    tiles = lax.axis_size("lat")
    return exchange_add(half.reshape(tiles, -1, lanes), "lat", lax.axis_index("lat"), 1)[None]


def spread_tiles(share):
    return exchange_all(share[0], "lat", lax.axis_index("lat"), 1, lax.axis_size("lat"))


def group_stages():
    two_by_two = lax.axis_size("lat") == 4
    return (
        [reduce_over_cores]
        + ([reduce_first, reduce_second] if two_by_two else [reduce_tiles])
        + [reduce_columns, spread_columns]
        + ([spread_second, spread_first] if two_by_two else [spread_tiles])
        + [lambda half: (half, swap(half, "lon", 1))]
    )


def sum_small(flat):
    count = lax.axis_size(both)
    rows = flat.shape[0]
    padded = -(-rows // (8 * count)) * 8 * count
    pieces = jnp.pad(flat, ((0, padded - rows), (0, 0))).reshape(count, -1, lanes)
    share = jnp.sum(lax.all_to_all(pieces, both, 0, 0, tiled=False), axis=0)
    copies = jnp.broadcast_to(share[None], pieces.shape)
    return lax.all_to_all(copies, both, 0, 0, tiled=False).reshape(padded, lanes)[:rows]


def cross_rows(former, latter):
    return lax.dot_general(former, latter, (((0,), (0,)), ((), ())), preferred_element_type=f32)


def by_transpose(former, latter):
    return lax.dot_general(former, latter, (((1,), (1,)), ((), ())), preferred_element_type=f32)


def block_mix(source, params, sea, ocean, dates, between=lambda mixed: ()):
    taps, gain, shift = params[:3]
    channels = source.shape[2]
    edges = borders(source, dates)
    mixed, local = stencil_forward(source, edges, taps, sea)
    event = between(mixed)
    totals = sum_all(jnp.concatenate([local, jnp.broadcast_to(ocean, (1, channels))]), event)
    first, square, ocean = totals
    mean = first / ocean
    factor = lax.rsqrt(square / ocean - mean * mean + epsilon)
    scales = jnp.stack([mean, factor, gain, shift])
    mix = source, edges, taps, mixed.reshape(-1, channels), scales, ocean
    return (mix, event) if event else mix


def block_forward(mix, params, sea, pooling=()):
    source, edges, taps, mixed, scales, ocean = mix
    up, up_bias, down, down_bias = params[3:]
    channels = source.shape[2]
    output, active, slope, normed, *coarse = mlp_forward(
        mixed,
        source.reshape(-1, channels),
        sea.reshape(-1, lanes),
        scales,
        up,
        up_bias,
        down,
        down_bias,
        pooling,
    )
    return output, coarse, mix + (normed, slope, active)


def block_hidden(upstream, params, sea, stored):
    scales, mixed, slope = stored[4], stored[3], stored[7]
    return mlp_backward(upstream, mixed, slope, sea.reshape(-1, lanes), scales, params[3], params[5])


def block_norm(grad_normed, local, sea, stored, dates):
    source, edges, taps, mixed, scales, ocean = stored[:6]
    channels = source.shape[2]
    grad_shift, grad_gain = sum_all(local)
    mean, factor, gain = scales[0], scales[1], scales[2]
    unit = (mixed - mean) * factor
    weight = spread(sea.reshape(-1, lanes), channels) / ocean
    grad_mixed = factor * (gain * grad_normed - weight * (gain * grad_shift + unit * (gain * grad_gain)))
    grad_mixed = grad_mixed.astype(bf16).reshape(source.shape)
    return grad_mixed, borders(grad_mixed, dates), grad_gain, grad_shift


def block_source(grad_mixed, grad_edges, upstream, sea, stored):
    source, taps = stored[0], stored[2]
    grad_source, sums = stencil_backward(grad_mixed, grad_edges, taps, sea, upstream.reshape(source.shape))
    return grad_source.reshape(-1, source.shape[2]), sums


def shards(
    fine_map,
    ocean_mask,
    out_grad,
    encode_depth,
    encode_gain,
    encode_shift,
    encode_up,
    encode_up_bias,
    encode_down,
    encode_down_bias,
    widen_weight,
    widen_bias,
    bottle_depth,
    bottle_gain,
    bottle_shift,
    bottle_up,
    bottle_up_bias,
    bottle_down,
    bottle_down_bias,
    merge_weight,
    merge_bias,
    decode_depth,
    decode_gain,
    decode_shift,
    decode_up,
    decode_up_bias,
    decode_down,
    decode_down_bias,
):
    dates, tile_rows, breadth, channels = fine_map.shape
    wide = bottle_depth.shape[2]
    extra = jnp.swapaxes(ocean_mask, 1, 2).astype(bf16)[:, None]
    extra = jnp.pad(extra, ((0, 0), (0, 0), (0, 0), (0, channels - tile_rows)))
    pieces = send_dates(jnp.concatenate([fine_map, extra], axis=1))
    kernels = (encode_depth, bottle_depth, decode_depth)
    rows = (encode_up_bias, encode_down_bias, bottle_up_bias, bottle_down_bias, decode_up_bias, decode_down_bias)
    small = (
        [kernel.astype(f32).reshape(49, -1) for kernel in kernels],
        [row.astype(f32)[None] for row in rows + (widen_bias, merge_bias)],
        [row.astype(f32) for row in (encode_gain, encode_shift, bottle_gain, bottle_shift, decode_gain, decode_shift)],
    )
    pieces, (taps, rows, norms) = lax.optimization_barrier((pieces, small))
    encode_up_bias, encode_down_bias, bottle_up_bias, bottle_down_bias, decode_up_bias, decode_down_bias = rows[:6]
    widen_bias, merge_bias = rows[6:]
    encode_norm, bottle_norm, decode_norm = [(taps[i], norms[2 * i], norms[2 * i + 1]) for i in range(3)]
    packed = to_dates(pieces).reshape(dates, tile_rows + 1, breadth, channels)
    fine = packed[:, :tile_rows].reshape(-1, breadth, channels)
    ocean_band = jnp.swapaxes(packed[:, tile_rows, :, :tile_rows], 1, 2).reshape(-1, breadth).astype(f32)
    height = fine.shape[0]
    half_height, half_breadth = height // 2, breadth // 2


    coarse_band = jnp.max(ocean_band.reshape(half_height, 2, half_breadth, 2), axis=(1, 3))
    sea_fine = jnp.broadcast_to(ocean_band[..., None], (height, breadth, lanes))
    sea_coarse = jnp.broadcast_to(coarse_band[..., None], (half_height, half_breadth, lanes))
    ocean_fine = jnp.sum(ocean_band)
    ocean_coarse = jnp.sum(coarse_band)
    parts = height * breadth // math.gcd(height * breadth, 384)
    pixel = np.arange(height * breadth // parts)
    block = pixel // breadth // 2 * half_breadth + pixel % breadth // 2
    members = jnp.asarray(block[:, None] == np.arange(pixel.size // 4), dtype=bf16)
    blocks = jnp.asarray(np.arange(pixel.size // 4)[:, None] == block, dtype=bf16)

    mix = block_mix(fine, encode_norm, sea_fine, ocean_fine, dates)
    encode_up, encode_down = gathered_pair(encode_up, encode_down, mix[3])
    encode = encode_norm + (encode_up, encode_up_bias, encode_down, encode_down_bias)
    widen_weight = gathered(after(widen_weight, mix[3]))
    skip_rows, (pooled, coarse_in), encode_stored = block_forward(
        mix, encode, sea_fine, (blocks, widen_weight, widen_bias)
    )
    decode_up = lax.all_gather(after(decode_up, skip_rows), "lat", axis=0, tiled=True)
    decode_down = lax.all_gather(after(decode_down, skip_rows), "lat", axis=0, tiled=True)
    decode = decode_norm + (decode_up, decode_up_bias, decode_down, decode_down_bias)
    coarse_in = coarse_in.reshape(half_height, half_breadth, wide)
    bottle_down, coarse_in = gathered_by_rows(after(bottle_down, encode_stored[3]), coarse_in)
    mix, (bottle_up, bottle_down) = block_mix(
        coarse_in,
        bottle_norm,
        sea_coarse,
        ocean_coarse,
        dates,
        lambda mixed: (gathered_by_columns(bottle_up, mixed), bottle_down),
    )
    bottle = bottle_norm + (bottle_up, bottle_up_bias, bottle_down, bottle_down_bias)
    coarse_low, _, coarse_stored = block_forward(mix, bottle, sea_coarse)
    merge_rows = merge_weight.shape[0]
    merge_weight = jnp.pad(after(merge_weight, skip_rows), ((0, -merge_rows % 16), (0, 0)))
    merge_weight = gathered(merge_weight, coarse_low).reshape(-1, merge_rows + -merge_rows % 16, channels)
    merge_weight = merge_weight[:, :merge_rows].reshape(-1, channels)
    upstream = send_dates(after(out_grad, mix[3]))
    merged = merge_forward(coarse_low, skip_rows, merge_weight, merge_bias, members, parts)
    mix = block_mix(merged.reshape(fine.shape), decode, sea_fine, ocean_fine, dates)
    upstream = to_dates(after(upstream, mix[3])).reshape(-1, channels)
    decode_rows, _, decode_stored = block_forward(mix, decode, sea_fine)
    result = from_dates(decode_rows.reshape(fine.shape), dates)

    grad_branch, grad_hidden, grad_normed, local, *decode_small = block_hidden(upstream, decode, sea_fine, decode_stored)
    early = [
        cross_rows(decode_stored[6], grad_hidden),
        cross_rows(grad_branch, decode_stored[8]),
    ]
    grad_mixed, grad_edges, *decode_total = block_norm(grad_normed, local, sea_fine, decode_stored, dates)
    decode_mixed = grad_mixed
    grad_merged, merge_sums = block_source(grad_mixed, grad_edges, upstream, sea_fine, decode_stored)

    block_sums, grad_coarse = merge_backward(grad_merged, merge_weight, blocks, wide, parts)
    early += [cross_rows(block_sums, coarse_low), cross_rows(grad_merged, skip_rows)]

    grad_branch, grad_hidden, grad_normed, local, *bottle_small = block_hidden(
        grad_coarse, bottle, sea_coarse, coarse_stored
    )
    decode_kernel = kernel_grad(*decode_stored[:2], after(decode_mixed, local))
    early += [cross_rows(coarse_stored[6], grad_hidden), cross_rows(grad_branch, coarse_stored[8])]
    early = lax.psum([part.astype(bf16) for part in early], both)
    early = [total.astype(f32) for total in early]
    decode_up_sum, decode_down_sum, bottle_up_sum, bottle_down_sum = early[0], early[1].T, early[4], early[5].T
    merge_sum = jnp.concatenate(early[2:4], axis=1).T
    grad_mixed, grad_edges, *bottle_total = block_norm(grad_normed, local, sea_coarse, coarse_stored, dates)
    bottle_kernel = kernel_grad(*coarse_stored[:2], grad_mixed)
    grad_wide, widen_sums = block_source(grad_mixed, grad_edges, grad_coarse, sea_coarse, coarse_stored)
    grad_skip = skip_backward(grad_merged, grad_wide, merge_weight, widen_weight, members, parts)

    grad_branch, grad_hidden, grad_normed, local, *encode_small = block_hidden(
        grad_skip, encode, sea_fine, encode_stored
    )
    encode_pair = weight_grads(grad_branch, encode_stored[6], encode_stored[8], grad_hidden).reshape(2, -1, lanes)
    grad_mixed, grad_edges, *encode_total = block_norm(grad_normed, local, sea_fine, encode_stored, dates)
    encode_kernel = kernel_grad(*encode_stored[:2], grad_mixed)
    grad_fine, _ = block_source(grad_mixed, grad_edges, grad_skip, sea_fine, encode_stored)
    core = (lax.axis_index("lon") % 2).astype(jnp.int32)[None]
    grad_widen = cross_rows(pooled, grad_wide).astype(bf16)
    widen_tiles = pl.cdiv(wide, 2 * lanes)
    grad_widen = jnp.pad(grad_widen, ((0, 0), (0, 2 * widen_tiles * lanes - wide)))
    grad_widen = grad_widen.reshape(channels, 2, widen_tiles, lanes).transpose(1, 2, 0, 3).reshape(2, -1, lanes)
    fine_grad = from_dates(grad_fine.reshape(fine.shape), dates)
    state = jnp.concatenate([encode_pair, grad_widen], axis=1)
    for stage in group_stages():
        state = stage(state)
    own, other = state
    encode_up_sum, encode_down_sum = unpack(core, own, other, channels, encode_up.shape[1])
    encode_down_sum = encode_down_sum.T
    start = encode_pair.shape[1]
    lower = jnp.where(core == 0, own[start : start + grad_widen.shape[1]], other[start : start + grad_widen.shape[1]])
    upper = jnp.where(core == 0, other[start : start + grad_widen.shape[1]], own[start : start + grad_widen.shape[1]])
    widen_sum = jnp.stack([lower, upper]).reshape(2 * widen_tiles, channels, lanes).astype(f32)
    widen_sum = widen_sum.transpose(1, 0, 2).reshape(channels, -1)[:, :wide]

    kernels = [encode_kernel, bottle_kernel, decode_kernel]
    rows = [encode_small, (widen_sums,), bottle_small, (merge_sums,), decode_small]
    rows = [row for group in rows for row in group]
    padded = [jnp.pad(row, ((0, 0), (0, -row.shape[1] % lanes))) for row in rows]
    line = jnp.concatenate(padded, axis=1)
    small = sum_small(jnp.concatenate([array.reshape(-1, lanes) for array in kernels] + [line.reshape(-1, lanes)]))
    kernel_sums, at = [], 0
    for array, shape in zip(kernels, (encode_depth.shape, bottle_depth.shape, decode_depth.shape)):
        count = array.shape[0] * 56
        total = small[at : at + count].reshape(array.shape)[:, :49].transpose(1, 0, 2).reshape(49, -1)
        kernel_sums.append(total[:, : shape[2]].reshape(shape))
        at += count
    line = small[at:].reshape(-1)
    row_sums, at = [], 0
    for row, wider in zip(rows, padded):
        row_sums.append(line[at : at + row.shape[1]])
        at += wider.shape[1]
    (encode_upb, encode_downb, widen_b, bottle_upb, bottle_downb, bottle_merge_b, decode_upb, decode_downb) = (
        row_sums[1],
        row_sums[0],
        row_sums[2],
        row_sums[4],
        row_sums[3],
        row_sums[5],
        row_sums[7],
        row_sums[6],
    )
    return (
        result,
        fine_grad,
        kernel_sums[0],
        encode_total[0],
        encode_total[1],
        encode_up_sum,
        encode_upb,
        encode_down_sum,
        encode_downb,
        widen_sum,
        widen_b,
        kernel_sums[1],
        bottle_total[0],
        bottle_total[1],
        bottle_up_sum,
        bottle_upb,
        bottle_down_sum,
        bottle_downb,
        merge_sum,
        bottle_merge_b,
        kernel_sums[2],
        decode_total[0],
        decode_total[1],
        decode_up_sum,
        decode_upb,
        decode_down_sum,
        decode_downb,
    )


def solution(mesh):
    whole = P()
    rows = P("lat", None)
    tile = P(None, "lat", "lon", None)
    block = (whole, whole, whole, rows, whole, rows, whole)
    placed = (tile, P(None, "lat", "lon"), tile) + block + (rows, whole) + block + (rows, whole) + block
    return jax.shard_map(
        shards,
        mesh=mesh,
        in_specs=placed,
        out_specs=(tile, tile) + (whole,) * 25,
        check_vma=False,
    )
```
